256 devices in a mesh: img: 64 (over x, z, core), grp: 4 (over y).
Axes of the slice: x: 4, y: 4, z: 8, core: 2. Of those that a mesh axis runs over, the one named last changes fastest.
Arguments:
- desc: bfloat16 [256, 1024, 256], P(('img', 'grp')), may hold values from -20 to 20
- w_proj: bfloat16 [256, 512], replicated, may hold values from -0.375 to 0.375
- w_out: bfloat16 [256, 256], replicated, may hold values from -0.375 to 0.375
- pair_list: int32 [1280, 2], P(('img', 'grp')), may hold values from 0 to 255, as said below
- pair_count: int32 [256], P(('img', 'grp')), may hold values from 1 to 5, as said below
Outputs:
- updated: bfloat16 [256, 1024, 256], P(('img', 'grp'))
The draws below stay inside these ranges and needn't reach their ends.
Inputs may be any that keep to these rules, and one draw needn't show every extreme that they name: `pair_list`: for a slot of the device at img index i, the first image lies in column i (ids i * 4 to i * 4 + 3) and the second in column i or column (i + 1) % 64, and the two ids differ; every slot holds such a pair, live or not. `pair_count`: some device has all 5 slots live.
All inputs are finite; a program needn't handle non-finite values.
Results may differ from the reference program's by a relative error of at most 0.0072.
Values may be sent and summed in bfloat16 or wider, within the bound.
No kernel may reach another device: no remote copies, remote signals or barrier semaphores. Data moves between devices by JAX's collectives and lax.ppermute only.
A program may use at most 64 MiB of HBM per device.

```python
import jax
import jax.numpy as jnp
from jax import lax

D = 256
HEADS = 4
HEAD_DIM = 64
KEYS = 1024
PAIR_CAP = 5
COLUMNS = 64
GROUP = 4
NIMAGES = 256
SLOTS = 1280


def draw_desc(key, part):
    keys_main = jax.random.split(jax.random.fold_in(key, 5), 1)
    base = jax.random.normal(keys_main[0], (NIMAGES, KEYS, D), jnp.float32)
    return jnp.clip(base, -4.0, 4.0).astype(jnp.bfloat16)


def draw_pair_list(key, part):
    keys_main = jax.random.split(jax.random.fold_in(key, 11), 3)
    position = jnp.arange(SLOTS, dtype=jnp.int32)
    column = position // PAIR_CAP // GROUP
    first_member = jax.random.randint(keys_main[0], (SLOTS,), 0, GROUP)
    step_ahead = (jax.random.randint(keys_main[1], (SLOTS,), 0, 4) > 0).astype(jnp.int32)
    second_member = jax.random.randint(keys_main[2], (SLOTS,), 0, GROUP)
    clash = (step_ahead == 0) & (second_member == first_member)
    second_member = jnp.where(clash, (second_member + 1) % GROUP, second_member)
    first_id = column * GROUP + first_member
    second_id = (column + step_ahead) % COLUMNS * GROUP + second_member
    return jnp.stack([first_id, second_id], 1).astype(jnp.int32)


def draw_pair_count(key, part):
    keys_main = jax.random.split(jax.random.fold_in(key, 23), 3)
    base = jax.random.randint(keys_main[0], (NIMAGES,), 1, PAIR_CAP // 2 + 2)
    base = jnp.minimum(base, PAIR_CAP)
    busy = jax.random.randint(keys_main[1], (NIMAGES,), 0, 8) == 0
    chosen = jax.random.randint(keys_main[2], (), 0, NIMAGES)
    marked = busy | (jnp.arange(NIMAGES, dtype=jnp.int32) == chosen)
    return jnp.where(marked, PAIR_CAP, base).astype(jnp.int32)


def noise(own_key, dims, spread, bound, kind=jnp.bfloat16):
    result = spread * jax.random.normal(own_key, dims, jnp.float32)
    return jnp.clip(result, min=-bound, max=bound).astype(kind)


def setup_inputs(seed: int = 0) -> dict:
    keys = jax.random.split(jax.random.key(seed), 6)
    desc = draw_desc(jax.random.fold_in(keys[5], 71), 0)
    w_proj = noise(keys[1], (D, 2 * D), D ** -0.5, 0.375)
    w_out = noise(keys[2], (D, D), D ** -0.5, 0.375)
    pair_list = draw_pair_list(jax.random.fold_in(keys[5], 71), 0)
    pair_count = draw_pair_count(jax.random.fold_in(keys[5], 71), 0)
    return {"desc": desc, "w_proj": w_proj, "w_out": w_out, "pair_list": pair_list, "pair_count": pair_count}


def pair_messages(first_rows, second_rows):
    to_first = []
    to_second = []
    for head_index in range(HEADS):
        lower = head_index * HEAD_DIM
        query_first = first_rows[:, lower:lower + HEAD_DIM]
        query_second = second_rows[:, lower:lower + HEAD_DIM]
        value_first = first_rows[:, D + lower:D + lower + HEAD_DIM]
        value_second = second_rows[:, D + lower:D + lower + HEAD_DIM]
        scores = jnp.dot(query_first, query_second.T, preferred_element_type=jnp.float32) * (HEAD_DIM ** -0.5)
        across = jnp.exp(scores - jnp.max(scores, axis=1, keepdims=True))
        across = (across / jnp.sum(across, axis=1, keepdims=True)).astype(jnp.bfloat16)
        downward = jnp.exp(scores - jnp.max(scores, axis=0, keepdims=True))
        downward = (downward / jnp.sum(downward, axis=0, keepdims=True)).astype(jnp.bfloat16)
        to_first.append(jnp.dot(across, value_second, preferred_element_type=jnp.float32))
        to_second.append(lax.dot_general(downward, value_first, (((0,), (0,)), ((), ())), preferred_element_type=jnp.float32))
    return jnp.concatenate(to_first, 1).astype(jnp.bfloat16), jnp.concatenate(to_second, 1).astype(jnp.bfloat16)


def reference(desc, w_proj, w_out, pair_list, pair_count):
    proj = jnp.dot(desc.reshape(NIMAGES * KEYS, D), w_proj, preferred_element_type=jnp.float32)
    proj = proj.astype(jnp.bfloat16).reshape(NIMAGES, KEYS, 2 * D)
    position = jnp.arange(SLOTS, dtype=jnp.int32)
    live = (position % PAIR_CAP) < pair_count[position // PAIR_CAP]

    def visit(totals, item):
        first_id, second_id, flag = item

        def work(current):
            first_rows = lax.dynamic_index_in_dim(proj, first_id, 0, keepdims=False)
            second_rows = lax.dynamic_index_in_dim(proj, second_id, 0, keepdims=False)
            to_first, to_second = pair_messages(first_rows, second_rows)
            current = current.at[first_id].add(to_first.astype(jnp.float32))
            return current.at[second_id].add(to_second.astype(jnp.float32))

        return lax.cond(flag, work, lambda current: current, totals), None

    totals = jnp.zeros((NIMAGES, KEYS, D), jnp.float32)
    totals, _ = lax.scan(visit, totals, (pair_list[:, 0].astype(jnp.int32), pair_list[:, 1].astype(jnp.int32), live))
    message = totals.astype(jnp.bfloat16)
    update = jnp.dot(message.reshape(NIMAGES * KEYS, D), w_out, preferred_element_type=jnp.float32)
    updated = desc.astype(jnp.float32) + update.reshape(NIMAGES, KEYS, D)
    return updated.astype(jnp.bfloat16)
```

```python
import functools
import math

import jax
import jax.numpy as jnp
from jax import lax
from jax.experimental import pallas as pl
from jax.experimental.pallas import tpu as pltpu
from jax.sharding import PartitionSpec as P

D = 256
HEADS = 4
HEAD_DIM = 64
ONES = 16
INFO = 16
SCALE = HEAD_DIM ** -0.5
LOG2E = math.log2(math.e)
SAFE_SCORE = 64.0
NORM_CAP = 250.0
BF16 = jnp.bfloat16
F32 = jnp.float32
NT = (((1,), (1,)), ((), ()))
TN = (((0,), (0,)), ((), ()))
VMEM_LIMIT = 56 * 1024 * 1024


def project_kernel(list_ref, count_ref, desc_ref, w_ref, out_ref):
    keypoints = desc_ref.shape[1]
    cap = list_ref.shape[0]
    desc = desc_ref[0]
    lane = lax.broadcasted_iota(jnp.int32, (INFO, 2 * HEAD_DIM), 1)
    common = jnp.where(lane == 0, count_ref[0], 0)
    for slot in range(cap):
        common = jnp.where(lane == 2 + 2 * slot, list_ref[slot, 0], common)
        common = jnp.where(lane == 3 + 2 * slot, list_ref[slot, 1], common)
    ones = jnp.ones((HEAD_DIM, 2 * HEAD_DIM), BF16)
    for head in range(HEADS):
        lower = head * HEAD_DIM
        weights = jnp.concatenate(
            [w_ref[:, lower : lower + HEAD_DIM], w_ref[:, D + lower : D + lower + HEAD_DIM]], 1
        )
        rows = jnp.dot(desc, weights, preferred_element_type=F32).astype(BF16)
        out_ref[head, :keypoints, :] = rows
        query = rows[:, :HEAD_DIM].astype(F32)
        squares = jnp.dot((query * query).astype(BF16), ones, preferred_element_type=F32)
        norm = jnp.sqrt(jnp.max(squares, axis=0, keepdims=True)) * 1.01
        norm = jnp.ceil(jnp.minimum(norm, NORM_CAP))
        info = jnp.where(lane == 1, jnp.broadcast_to(norm, lane.shape), common.astype(F32))
        out_ref[head, keypoints:, :] = info.astype(BF16)


def project(pair_list, pair_count, desc, w_proj):
    keypoints = desc.shape[1]
    smem = pl.BlockSpec(memory_space=pltpu.SMEM)
    vmem = pl.BlockSpec(memory_space=pltpu.VMEM)
    return pl.pallas_call(
        project_kernel,
        out_shape=jax.ShapeDtypeStruct((HEADS, keypoints + INFO, 2 * HEAD_DIM), BF16),
        in_specs=[smem, smem, vmem, vmem],
        out_specs=vmem,
        compiler_params=pltpu.CompilerParams(vmem_limit_bytes=VMEM_LIMIT),
        name="project",
    )(pair_list, pair_count, desc, w_proj)


def attend(rows, values, totals, target, source, safe, block):
    keypoints = values.shape[2]

    @pl.when(safe)
    def _():
        for i in range(0, keypoints, block):
            query = rows[target, i : i + block, :HEAD_DIM]
            total = None
            for j in range(0, keypoints, block):
                keys = rows[source, j : j + block, :HEAD_DIM]
                scores = lax.dot_general(keys, query, NT, preferred_element_type=F32)
                weights = jnp.exp2(scores * (SCALE * LOG2E)).astype(BF16)
                part = jnp.dot(
                    values[source, :, j : j + block], weights, preferred_element_type=F32
                )
                total = part if total is None else total + part
            totals[target, :, i : i + block] += total[ONES:] / total[:1]

    @pl.when(jnp.logical_not(safe))
    def _():
        narrow = 256
        for i in range(0, keypoints, narrow):
            query = rows[target, i : i + narrow, :HEAD_DIM]
            keys = rows[source, :keypoints, :HEAD_DIM]
            scores = lax.dot_general(keys, query, NT, preferred_element_type=F32) * SCALE
            weights = jnp.exp(scores - jnp.max(scores, axis=0, keepdims=True)).astype(BF16)
            total = jnp.dot(values[source], weights, preferred_element_type=F32)
            totals[target, :, i : i + narrow] += total[ONES:] / total[:1]


def attention_kernel(columns, members, cap, *refs):
    count = 3 * members
    pieces = refs[:count]
    out_ref = refs[count]
    rows, values, totals, info_v, info, units, sems, info_sem = refs[count + 1 :]
    keypoints = values.shape[2]
    column = lax.axis_index("img")
    member = lax.axis_index("grp")

    copies = [
        pltpu.make_async_copy(pieces[k], rows.at[k], sems.at[k]) for k in range(count)
    ]
    for copy in copies:
        copy.start()
    totals[...] = jnp.zeros_like(totals)
    for k in range(count):
        copies[k].wait()
        values[k, :ONES, :] = jnp.ones((ONES, keypoints), BF16)
        values[k, ONES:, :] = rows[k, :keypoints, :].T[HEAD_DIM:]
        info_v[k] = rows[k, keypoints:, :].astype(F32).astype(jnp.int32)[:8]
    copy = pltpu.make_async_copy(info_v, info, info_sem)
    copy.start()
    copy.wait()

    even = lax.rem(column, 2) == 0
    next_base = jnp.where(even, members, 2 * members)
    prev_base = jnp.where(even, 2 * members, members)

    def place(image):
        return lax.rem(lax.rem(image, members) - member + members, members)

    def push(found, wanted, target, source):
        @pl.when(wanted)
        def _():
            units[0, found] = target
            units[1, found] = source

        return found + wanted.astype(jnp.int32)

    def own(step, found):
        slot = step // cap
        position = step % cap
        first = info[slot, 0, 2 + 2 * position]
        second = info[slot, 0, 3 + 2 * position]
        live = position < info[slot, 0, 0]
        inside = second // members == column
        target = place(first)
        other = place(second)
        found = push(found, live, target, jnp.where(inside, other, next_base + other))
        return push(found, jnp.logical_and(live, inside), other, target)

    def behind(step, found):
        slot = prev_base + step // cap
        position = step % cap
        first = info[slot, 0, 2 + 2 * position]
        second = info[slot, 0, 3 + 2 * position]
        live = position < info[slot, 0, 0]
        inside = second // members == column
        return push(
            found, jnp.logical_and(live, inside), place(second), prev_base + place(first)
        )

    found = lax.fori_loop(0, members * cap, own, jnp.int32(0))
    found = lax.fori_loop(0, members * cap, behind, found)

    def visit(index, carry):
        target = units[0, index]
        source = units[1, index]
        left = info[target, 0, 1]
        right = info[source, 0, 1]
        largest = jnp.maximum(left, right)
        safe = jnp.logical_and(
            largest < int(NORM_CAP), left * right <= int(SAFE_SCORE / SCALE)
        )
        attend(rows, values, totals, target, source, safe, 512)
        return carry

    lax.fori_loop(0, found, visit, 0)
    out_ref[...] = totals[...].astype(BF16)


def attention(columns, members, cap, pieces):
    full, width = pieces[0].shape
    keypoints = full - INFO
    count = len(pieces)
    return pl.pallas_call(
        functools.partial(attention_kernel, columns, members, cap),
        out_shape=jax.ShapeDtypeStruct((members, HEAD_DIM, keypoints), BF16),
        in_specs=[pl.BlockSpec(memory_space=pl.ANY)] * count,
        out_specs=pl.BlockSpec(memory_space=pltpu.VMEM),
        scratch_shapes=[
            pltpu.VMEM((count, full, width), BF16),
            pltpu.VMEM((count, ONES + HEAD_DIM, keypoints), BF16),
            pltpu.VMEM((members, HEAD_DIM, keypoints), F32),
            pltpu.VMEM((count, 8, width), jnp.int32),
            pltpu.SMEM((count, 8, width), jnp.int32),
            pltpu.SMEM((2, 3 * members * cap), jnp.int32),
            pltpu.SemaphoreType.DMA((count,)),
            pltpu.SemaphoreType.DMA,
        ],
        compiler_params=pltpu.CompilerParams(vmem_limit_bytes=VMEM_LIMIT),
        name="attention",
    )(*pieces)


def update_kernel(members, desc_ref, w_ref, *refs):
    pieces = refs[:members]
    out_ref = refs[members]
    member = lax.axis_index("grp")
    weights = []
    for distance in range(members):
        head = lax.rem(member - distance + members, members)
        weights.append(w_ref[pl.ds(pl.multiple_of(head * HEAD_DIM, HEAD_DIM), HEAD_DIM), :])
    message = jnp.concatenate([piece[...] for piece in pieces], 0)
    update = lax.dot_general(
        message, jnp.concatenate(weights, 0), TN, preferred_element_type=F32
    )
    out_ref[0] = (desc_ref[0].astype(F32) + update).astype(BF16)


def update(members, desc, w_out, pieces):
    vmem = pl.BlockSpec(memory_space=pltpu.VMEM)
    return pl.pallas_call(
        functools.partial(update_kernel, members),
        out_shape=jax.ShapeDtypeStruct(desc.shape, BF16),
        in_specs=[vmem] * (2 + members),
        out_specs=vmem,
        compiler_params=pltpu.CompilerParams(vmem_limit_bytes=VMEM_LIMIT),
        name="update",
    )(desc, w_out, *pieces)


def on_device(desc, w_proj, w_out, pair_list, pair_count):
    columns = lax.axis_size("img")
    members = lax.axis_size("grp")
    cap = pair_list.shape[0]
    member = lax.axis_index("grp")

    def ahead(block, distance):
        route = [((i + distance) % members, i) for i in range(members)]
        return lax.ppermute(block, "grp", route)

    def swap(block, offset):
        pairs = []
        for i in range(offset, columns + offset, 2):
            low, high = i % columns, (i + 1) % columns
            pairs += [(low, high), (high, low)]
        return lax.ppermute(block, "img", pairs)

    sent = project(pair_list, pair_count, desc, w_proj)
    own = []
    for distance in range(members):
        head = (member - distance) % members
        block = lax.dynamic_index_in_dim(sent, head, 0, keepdims=False)
        own.append(ahead(block, distance) if distance else block)
    near = [swap(block, 0) for block in own]
    far = [swap(block, 1) for block in own]
    messages = attention(columns, members, cap, own + near + far)
    back = [messages[0]]
    for distance in range(1, members):
        back.append(ahead(messages[distance], members - distance))
    return update(members, desc, w_out, back)


def solution(mesh):
    return jax.shard_map(
        on_device,
        mesh=mesh,
        in_specs=(
            P(("img", "grp"), None, None),
            P(),
            P(),
            P(("img", "grp"), None),
            P(("img", "grp")),
        ),
        out_specs=P(("img", "grp"), None, None),
        check_vma=False,
    )
```

```python
import functools
import math

import jax
import jax.numpy as jnp
from jax import lax
from jax.experimental import pallas as pl
from jax.experimental.pallas import tpu as pltpu
from jax.sharding import PartitionSpec as P

D = 256
HEADS = 4
HEAD_DIM = 64
LANES = 128
ONES = 16
INFO = 16
SCALE = HEAD_DIM ** -0.5
LOG2E = math.log2(math.e)
SAFE_SCORE = 64.0
NORM_CAP = 250.0
BF16 = jnp.bfloat16
F32 = jnp.float32
NT = (((1,), (1,)), ((), ()))
TN = (((0,), (0,)), ((), ()))
VMEM_LIMIT = 48 * 1024 * 1024


def project_kernel(members, count_ref, list_ref, desc_ref, w_ref, *refs):
    outs = refs[:members]
    turned = refs[members]
    keypoints = desc_ref.shape[1]
    cap = list_ref.shape[0]
    member = lax.axis_index("grp")
    turned[...] = w_ref[...].T
    lane = lax.broadcasted_iota(jnp.int32, (INFO, LANES), 1)
    common = jnp.where(lane == 0, count_ref[0], 0)
    for slot in range(cap):
        first = jnp.broadcast_to(list_ref[slot : slot + 1, 0:1], lane.shape)
        second = jnp.broadcast_to(list_ref[slot : slot + 1, 1:2], lane.shape)
        common = jnp.where(lane == 2 + 2 * slot, first, common)
        common = jnp.where(lane == 3 + 2 * slot, second, common)
    common = common.astype(F32)
    desc = desc_ref[0]
    for distance in range(members):
        head = lax.rem(member - distance + members, members)
        lower = pl.multiple_of(head * HEAD_DIM, HEAD_DIM)
        weights = jnp.concatenate(
            [turned[pl.ds(lower, HEAD_DIM), :], turned[pl.ds(D + lower, HEAD_DIM), :]], 0
        )
        both = lax.dot_general(weights, desc, NT, preferred_element_type=F32).astype(BF16)
        for block in range(keypoints // LANES):
            outs[distance][block * LANES : (block + 1) * LANES, :] = both[
                :, block * LANES : (block + 1) * LANES
            ]
        query = both[:HEAD_DIM].astype(F32)
        squares = jnp.sum(query * query, axis=0, keepdims=True)
        norm = jnp.sqrt(jnp.max(squares, axis=1, keepdims=True)) * 1.001
        norm = jnp.ceil(jnp.minimum(norm, NORM_CAP))
        info = jnp.where(lane == 1, jnp.broadcast_to(norm, lane.shape), common)
        outs[distance][keypoints:, :] = info.astype(BF16)


def project(members, pair_list, pair_count, desc, w_proj):
    keypoints = desc.shape[1]
    vmem = pl.BlockSpec(memory_space=pltpu.VMEM)
    out = jax.ShapeDtypeStruct((keypoints + INFO, LANES), BF16)
    return pl.pallas_call(
        functools.partial(project_kernel, members),
        out_shape=[out] * members,
        in_specs=[pl.BlockSpec(memory_space=pltpu.SMEM), vmem, vmem, vmem],
        out_specs=[vmem] * members,
        scratch_shapes=[pltpu.VMEM((2 * D, D), BF16)],
        compiler_params=pltpu.CompilerParams(vmem_limit_bytes=VMEM_LIMIT),
        name="project",
    )(pair_count, pair_list, desc, w_proj)


def query_of(rows, image, lower, size):
    parts = [
        rows[image, block : block + HEAD_DIM, :] for block in range(lower, lower + size, LANES)
    ]
    return jnp.concatenate(parts, 1)


def value_of(rows, image, lower, size):
    parts = [
        rows[image, block + HEAD_DIM : block + LANES, :]
        for block in range(lower, lower + size, LANES)
    ]
    return jnp.concatenate([jnp.ones((ONES, size), BF16), jnp.concatenate(parts, 1)], 0)


def one_sided(rows, totals, target, source, keypoints, block):
    query = query_of(rows, target, 0, keypoints)
    total = None
    for lower in range(0, keypoints, block):
        keys = query_of(rows, source, lower, block)
        scores = lax.dot_general(keys, query, TN, preferred_element_type=F32)
        weights = jnp.exp2(scores * (SCALE * LOG2E)).astype(BF16)
        part = jnp.dot(value_of(rows, source, lower, block), weights, preferred_element_type=F32)
        total = part if total is None else total + part
    totals[target] += total[ONES:] / total[:1]


def two_sided(rows, totals, target, source, keypoints, block):
    keys = query_of(rows, source, 0, keypoints)
    values = value_of(rows, source, 0, keypoints)
    back = None
    for lower in range(0, keypoints, block):
        query = query_of(rows, target, lower, block)
        scores = lax.dot_general(query, keys, TN, preferred_element_type=F32)
        weights = jnp.exp2(scores * (SCALE * LOG2E)).astype(BF16)
        total = lax.dot_general(values, weights, NT, preferred_element_type=F32)
        totals[target, :, lower : lower + block] += total[ONES:] / total[:1]
        part = jnp.dot(value_of(rows, target, lower, block), weights, preferred_element_type=F32)
        back = part if back is None else back + part
    totals[source] += back[ONES:] / back[:1]


def shifted(rows, totals, target, source, keypoints):
    narrow = 2 * LANES
    keys = query_of(rows, source, 0, keypoints)
    values = value_of(rows, source, 0, keypoints)

    def step(index, carry):
        lower = pl.multiple_of(index * narrow, narrow)
        parts = [
            rows[target, pl.ds(pl.multiple_of(lower + offset, LANES), HEAD_DIM), :]
            for offset in range(0, narrow, LANES)
        ]
        query = jnp.concatenate(parts, 1)
        scores = lax.dot_general(keys, query, TN, preferred_element_type=F32) * SCALE
        weights = jnp.exp(scores - jnp.max(scores, axis=0, keepdims=True)).astype(BF16)
        total = jnp.dot(values, weights, preferred_element_type=F32)
        totals[target, :, pl.ds(lower, narrow)] += total[ONES:] / total[:1]
        return carry

    lax.fori_loop(0, keypoints // narrow, step, 0)


def attention_kernel(members, groups, inner, targets, first_call, last_call, *refs):
    count = (1 + len(groups)) * members
    pieces, refs = refs[:count], refs[count:]
    if not first_call:
        start_ref, refs = refs[0], refs[1:]
    outs = refs[: last_call or 1]
    rows, totals, info_v, info, sems, info_sem = refs[len(outs) :]
    keypoints = totals.shape[2]
    column = lax.axis_index("img")
    member = lax.axis_index("grp")

    copies = [pltpu.make_async_copy(pieces[k], rows.at[k], sems.at[k]) for k in range(count)]
    for copy in copies:
        copy.start()
    if first_call:
        totals[...] = jnp.zeros_like(totals)
    else:
        totals[...] = start_ref[...]
    for k in range(count):
        copies[k].wait()
        info_v[k] = rows[k, keypoints:, :].astype(F32).astype(jnp.int32)[:8]
    copy = pltpu.make_async_copy(info_v, info, info_sem)
    copy.start()
    copy.wait()
    even = lax.rem(column, 2) == 0

    def place(image):
        return lax.rem(lax.rem(image, members) - member + members, members)

    def is_safe(target, source):
        left = info[target, 0, 1]
        right = info[source, 0, 1]
        return jnp.logical_and(
            jnp.maximum(left, right) < int(NORM_CAP), left * right <= int(SAFE_SCORE / SCALE)
        )

    def visit(listed, act):
        def slot(index, carry):
            owner = listed + index

            def position(step, inside):
                first = info[owner, 0, 2 + 2 * step]
                second = info[owner, 0, 3 + 2 * step]
                act(first, second, second // members == column)
                return inside

            return lax.fori_loop(0, info[owner, 0, 0], position, carry)

        lax.fori_loop(0, members, slot, 0)

    if inner:

        def act(first, second, inside):
            @pl.when(inside)
            def _():
                target, source = place(first), place(second)
                safe = is_safe(target, source)

                @pl.when(safe)
                def _():
                    two_sided(rows, totals, target, source, keypoints, keypoints // 2)

                @pl.when(jnp.logical_not(safe))
                def _():
                    shifted(rows, totals, target, source, keypoints)
                    shifted(rows, totals, source, target, keypoints)

        visit(0, act)

    def cross(index, carry):
        base = (1 + index) * members
        if len(groups) == 1:
            ahead = even if groups[0] == "near" else jnp.logical_not(even)
        else:
            ahead = (index == 0) == even
        listed = jnp.where(ahead, 0, base)

        def act(first, second, inside):
            target = jnp.where(ahead, place(first), place(second))
            source = base + jnp.where(ahead, place(second), place(first))
            wanted = inside != ahead
            if targets == "own":
                wanted = jnp.logical_and(wanted, target == 0)
            elif targets == "others":
                wanted = jnp.logical_and(wanted, target != 0)

            @pl.when(wanted)
            def _():
                safe = is_safe(target, source)

                @pl.when(safe)
                def _():
                    one_sided(rows, totals, target, source, keypoints, keypoints // 2)

                @pl.when(jnp.logical_not(safe))
                def _():
                    shifted(rows, totals, target, source, keypoints)

        visit(listed, act)
        return carry

    if groups:
        lax.fori_loop(0, len(groups), cross, 0)
    if not last_call:
        outs[0][...] = totals[...]
    elif targets == "own":
        outs[0][...] = totals[0].astype(BF16)
    else:
        for slot in range(1, members):
            outs[slot - 1][...] = totals[slot].astype(BF16)
        outs[members - 1][...] = totals[...]


def attention(members, groups, inner, targets, pieces, start, last_call):
    full = pieces[0].shape[0]
    keypoints = full - INFO
    count = len(pieces)
    hbm = pl.BlockSpec(memory_space=pltpu.HBM)
    vmem = pl.BlockSpec(memory_space=pltpu.VMEM)
    whole = jax.ShapeDtypeStruct((members, HEAD_DIM, keypoints), F32)
    message = jax.ShapeDtypeStruct((HEAD_DIM, keypoints), BF16)
    if not last_call:
        outs = [whole]
    elif targets == "own":
        outs = [message]
    else:
        outs = [message] * (members - 1) + [whole]
    inputs = list(pieces) + ([] if start is None else [start])
    return pl.pallas_call(
        functools.partial(
            attention_kernel, members, groups, inner, targets, start is None,
            len(outs) if last_call else 0,
        ),
        out_shape=outs,
        in_specs=[hbm] * count + [vmem] * (start is not None),
        out_specs=[vmem] * len(outs),
        scratch_shapes=[
            pltpu.VMEM((count, full, LANES), BF16),
            pltpu.VMEM((members, HEAD_DIM, keypoints), F32),
            pltpu.VMEM((count, 8, LANES), jnp.int32),
            pltpu.SMEM((count, 8, LANES), jnp.int32),
            pltpu.SemaphoreType.DMA((count,)),
            pltpu.SemaphoreType.DMA,
        ],
        compiler_params=pltpu.CompilerParams(vmem_limit_bytes=VMEM_LIMIT),
        cost_estimate=pl.CostEstimate(
            flops=10**10, bytes_accessed=count * full * LANES * 2, transcendentals=10**7
        ),
        name="attention_" + "_".join(("own",) * inner + groups) + "_" + targets,
    )(*inputs)


def update_kernel(members, desc_ref, w_ref, *refs):
    pieces = refs[:members]
    out_ref = refs[members]
    member = lax.axis_index("grp")
    weights = []
    for distance in range(members):
        head = lax.rem(member - distance + members, members)
        weights.append(w_ref[pl.ds(pl.multiple_of(head * HEAD_DIM, HEAD_DIM), HEAD_DIM), :])
    message = jnp.concatenate([piece[...] for piece in pieces], 0)
    update = lax.dot_general(
        message, jnp.concatenate(weights, 0), TN, preferred_element_type=F32
    )
    out_ref[0] = (desc_ref[0].astype(F32) + update).astype(BF16)


def update(members, desc, w_out, pieces):
    vmem = pl.BlockSpec(memory_space=pltpu.VMEM)
    return pl.pallas_call(
        functools.partial(update_kernel, members),
        out_shape=jax.ShapeDtypeStruct(desc.shape, BF16),
        in_specs=[vmem] * (2 + members),
        out_specs=vmem,
        compiler_params=pltpu.CompilerParams(vmem_limit_bytes=VMEM_LIMIT),
        name="update",
    )(desc, w_out, *pieces)


def on_device(desc, w_proj, w_out, pair_list, pair_count):
    columns = lax.axis_size("img")
    members = lax.axis_size("grp")

    def from_ahead(block, distance):
        route = [((i + distance) % members, i) for i in range(members)]
        return lax.ppermute(block, "grp", route)

    def swap(block, offset):
        pairs = []
        for i in range(offset, columns + offset, 2):
            low, high = i % columns, (i + 1) % columns
            pairs += [(low, high), (high, low)]
        return lax.ppermute(block, "img", pairs)

    sent = project(members, pair_list, pair_count, desc, w_proj)
    own = [sent[0]] + [from_ahead(sent[k], k) for k in range(1, members)]
    near = [swap(block, 0) for block in own]
    far = [swap(block, 1) for block in own]
    totals = attention(members, (), True, "all", own, None, False)[0]
    totals = attention(members, ("near",), False, "others", own + near, totals, False)[0]
    *messages, totals = attention(members, ("far",), False, "others", own + far, totals, True)
    mine = attention(members, ("near", "far"), False, "own", own + near + far, totals, True)[0]
    back = [mine]
    for distance in range(1, members):
        back.append(from_ahead(messages[distance - 1], members - distance))
    return update(members, desc, w_out, back)


def solution(mesh):
    return jax.shard_map(
        on_device,
        mesh=mesh,
        in_specs=(
            P(("img", "grp"), None, None),
            P(),
            P(),
            P(("img", "grp"), None),
            P(("img", "grp")),
        ),
        out_specs=P(("img", "grp"), None, None),
        check_vma=False,
    )
```

```python
import functools
import math

import jax
import jax.numpy as jnp
from jax import lax
from jax.experimental import pallas as pl
from jax.experimental.pallas import tpu as pltpu
from jax.sharding import PartitionSpec as P

D = 256
HEADS = 4
HEAD_DIM = 64
LANES = 128
ONES = 16
INFO = 16
SCALE = HEAD_DIM ** -0.5
LOG2E = math.log2(math.e)
SAFE_SCORE = 64.0
NORM_CAP = 250.0
BF16 = jnp.bfloat16
F32 = jnp.float32
NT = (((1,), (1,)), ((), ()))
TN = (((0,), (0,)), ((), ()))
VMEM_LIMIT = 28 * 1024 * 1024
PAIR_COST = 11
SIDE_COST = 8
TYPICAL = 7
SHORT = pl.CostEstimate(flops=10**4, bytes_accessed=10**4, transcendentals=0)
LONG = pl.CostEstimate(flops=10**10, bytes_accessed=10**7, transcendentals=0)


def project_kernel(members, count_ref, list_hbm, desc_hbm, w_hbm, *refs):
    outs = refs[:members]
    turned, list_ref, desc_ref, w_ref, sems = refs[members:]
    copies = [
        pltpu.make_async_copy(source, target, sems.at[k])
        for k, (source, target) in enumerate(
            ((w_hbm, w_ref), (desc_hbm, desc_ref), (list_hbm, list_ref))
        )
    ]
    for copy in copies:
        copy.start()
    keypoints = desc_ref.shape[1]
    cap = list_ref.shape[1]
    member = lax.axis_index("grp")
    copies[0].wait()
    turned[...] = w_ref[...].T
    copies[2].wait()
    lane = lax.broadcasted_iota(jnp.int32, (INFO, LANES), 1)
    common = jnp.where(lane == 0, count_ref[0], 0)
    for slot in range(cap):
        first = jnp.broadcast_to(list_ref[0:1, slot : slot + 1], lane.shape)
        second = jnp.broadcast_to(list_ref[1:2, slot : slot + 1], lane.shape)
        common = jnp.where(lane == 2 + 2 * slot, first, common)
        common = jnp.where(lane == 3 + 2 * slot, second, common)
    common = common.astype(F32)
    copies[1].wait()
    desc = desc_ref[0]
    for distance in range(members):
        head = lax.rem(member - distance + members, members)
        lower = pl.multiple_of(head * HEAD_DIM, HEAD_DIM)
        weights = jnp.concatenate(
            [turned[pl.ds(lower, HEAD_DIM), :], turned[pl.ds(D + lower, HEAD_DIM), :]], 0
        )
        both = lax.dot_general(weights, desc, NT, preferred_element_type=F32).astype(BF16)
        for block in range(keypoints // LANES):
            outs[distance][block * LANES : (block + 1) * LANES, :] = both[
                :, block * LANES : (block + 1) * LANES
            ]
        query = both[:HEAD_DIM].astype(F32)
        squares = jnp.sum(query * query, axis=0, keepdims=True)
        norm = jnp.sqrt(jnp.max(squares, axis=1, keepdims=True)) * 1.001
        norm = jnp.ceil(jnp.minimum(norm, NORM_CAP))
        info = jnp.where(lane == 1, jnp.broadcast_to(norm, lane.shape), common)
        outs[distance][keypoints:, :] = info.astype(BF16)


def project(members, pair_list, pair_count, desc, w_proj):
    keypoints = desc.shape[1]
    vmem = pl.BlockSpec(memory_space=pltpu.VMEM)
    hbm = pl.BlockSpec(memory_space=pltpu.HBM)
    out = jax.ShapeDtypeStruct((keypoints + INFO, LANES), BF16)
    listed = pair_list.T
    return pl.pallas_call(
        functools.partial(project_kernel, members),
        out_shape=[out] * members,
        in_specs=[pl.BlockSpec(memory_space=pltpu.SMEM), hbm, hbm, hbm],
        out_specs=[vmem] * members,
        scratch_shapes=[
            pltpu.VMEM((2 * D, D), BF16),
            pltpu.VMEM(listed.shape, jnp.int32),
            pltpu.VMEM(desc.shape, BF16),
            pltpu.VMEM(w_proj.shape, BF16),
            pltpu.SemaphoreType.DMA((3,)),
        ],
        name="project",
    )(pair_count, listed, desc, w_proj)


def query_of(rows, image, lower, size):
    parts = [
        rows[image, block : block + HEAD_DIM, :] for block in range(lower, lower + size, LANES)
    ]
    return jnp.concatenate(parts, 1)


def value_of(rows, image, lower, size):
    parts = [
        rows[image, block + HEAD_DIM : block + LANES, :]
        for block in range(lower, lower + size, LANES)
    ]
    return jnp.concatenate([jnp.ones((ONES, size), BF16), jnp.concatenate(parts, 1)], 0)


def one_sided(rows, totals, target, source, keypoints, block):
    query = query_of(rows, target, 0, keypoints)
    total = None
    for lower in range(0, keypoints, block):
        keys = query_of(rows, source, lower, block)
        scores = lax.dot_general(keys, query, TN, preferred_element_type=F32)
        weights = jnp.exp2(scores * (SCALE * LOG2E)).astype(BF16)
        part = jnp.dot(value_of(rows, source, lower, block), weights, preferred_element_type=F32)
        total = part if total is None else total + part
    totals[target] += total[ONES:] / total[:1]


def two_sided(rows, totals, target, source, keypoints, block):
    keys = query_of(rows, source, 0, keypoints)
    values = value_of(rows, source, 0, keypoints)
    back = None
    for lower in range(0, keypoints, block):
        query = query_of(rows, target, lower, block)
        scores = lax.dot_general(query, keys, TN, preferred_element_type=F32)
        weights = jnp.exp2(scores * (SCALE * LOG2E)).astype(BF16)
        total = lax.dot_general(values, weights, NT, preferred_element_type=F32)
        totals[target, :, lower : lower + block] += total[ONES:] / total[:1]
        part = jnp.dot(value_of(rows, target, lower, block), weights, preferred_element_type=F32)
        back = part if back is None else back + part
    totals[source] += back[ONES:] / back[:1]


def shifted(rows, totals, target, source, keypoints):
    narrow = 2 * LANES
    keys = query_of(rows, source, 0, keypoints)
    values = value_of(rows, source, 0, keypoints)

    def step(index, carry):
        lower = pl.multiple_of(index * narrow, narrow)
        parts = [
            rows[target, pl.ds(pl.multiple_of(lower + offset, LANES), HEAD_DIM), :]
            for offset in range(0, narrow, LANES)
        ]
        query = jnp.concatenate(parts, 1)
        scores = lax.dot_general(keys, query, TN, preferred_element_type=F32) * SCALE
        weights = jnp.exp(scores - jnp.max(scores, axis=0, keepdims=True)).astype(BF16)
        total = jnp.dot(values, weights, preferred_element_type=F32)
        totals[target, :, pl.ds(lower, narrow)] += total[ONES:] / total[:1]
        return carry

    lax.fori_loop(0, keypoints // narrow, step, 0)


def load_pieces(positions, pieces, rows, info_v, info, sems, info_sem, fill):
    keypoints = rows.shape[1] - INFO
    copies = [
        pltpu.make_async_copy(piece, rows.at[position], sems.at[k])
        for k, (position, piece) in enumerate(zip(positions, pieces))
    ]
    for copy in copies:
        copy.start()
    fill()
    for position, copy in zip(positions, copies):
        copy.wait()
        info_v[position] = rows[position, keypoints:, :].astype(F32).astype(jnp.int32)[:8]
    copy = pltpu.make_async_copy(info_v, info, info_sem)
    copy.start()
    copy.wait()


def place_of(image, members, member):
    return lax.rem(lax.rem(image, members) - member + members, members)


def is_safe(info, target, source):
    left = info[target, 0, 1]
    right = info[source, 0, 1]
    return jnp.logical_and(
        jnp.maximum(left, right) < int(NORM_CAP), left * right <= int(SAFE_SCORE / SCALE)
    )


def shared_kernel(members, positions, second_part, *refs):
    pieces, refs = refs[: len(positions)], refs[len(positions) :]
    if second_part:
        start_ref, own_ref, other_ref = refs[:3]
        refs = refs[3:]
    else:
        out_ref, refs = refs[0], refs[1:]
    rows, totals, info_v, info, units, sems, info_sem = refs
    keypoints = totals.shape[2]
    column = lax.axis_index("img")
    member = lax.axis_index("grp")
    late = members // 2

    def fill():
        if second_part:
            totals[...] = start_ref[...]
        else:
            totals[...] = jnp.zeros_like(totals)
            for position in range(2 * members):
                if position not in positions:
                    info_v[position] = jnp.zeros(info_v.shape[1:], jnp.int32)

    load_pieces(positions, pieces, rows, info_v, info, sems, info_sem, fill)
    side = lax.rem(column, 2)

    def slot(index, carry):
        late_list = lax.rem(index, members) == late
        right = index >= members
        base = jnp.where(right == (side == 1), 0, members)
        other = members - base
        owner = base + lax.rem(index, members)
        listed = column - side + right.astype(jnp.int32)

        def position(step, carry):
            early, found, leaving = carry
            first = info[owner, 0, 2 + 2 * step]
            second = info[owner, 0, 3 + 2 * step]
            inside = second // members == listed
            shared = jnp.logical_or(jnp.logical_not(right), inside)
            left, down = place_of(first, members, member), place_of(second, members, member)
            touches = jnp.logical_or(late_list, jnp.logical_or(left == late, down == late))
            wanted = jnp.logical_and(shared, touches == second_part)

            @pl.when(wanted)
            def _():
                units[0, found] = base + left
                units[1, found] = jnp.where(inside, base, other) + down

            early += jnp.logical_and(shared, jnp.logical_not(touches)).astype(jnp.int32)
            found += wanted.astype(jnp.int32)
            leaving += jnp.logical_not(shared).astype(jnp.int32)
            return early, found, leaving

        return lax.fori_loop(0, info[owner, 0, 0], position, carry)

    zero = jnp.int32(0)
    early, found, leaving = lax.fori_loop(0, 2 * members, slot, (zero, zero, zero))
    half = early // 2
    if second_part:
        load = (early + found) * PAIR_COST + (leaving - TYPICAL) * SIDE_COST
        half = jnp.clip((load + PAIR_COST) // (2 * PAIR_COST) - half, 0, found)
    begin = jnp.where(side == 0, 0, half)
    end = jnp.where(side == 0, half, found)

    def visit(index, carry):
        target, source = units[0, index], units[1, index]
        safe = is_safe(info, target, source)

        @pl.when(safe)
        def _():
            two_sided(rows, totals, target, source, keypoints, keypoints // 2)

        @pl.when(jnp.logical_not(safe))
        def _():
            shifted(rows, totals, target, source, keypoints)
            shifted(rows, totals, source, target, keypoints)

        return carry

    lax.fori_loop(begin, end, visit, 0)
    if second_part:
        own_ref[...] = totals[:members]
        other_ref[...] = totals[members:]
    else:
        out_ref[...] = totals[...]


def shared(members, positions, second_part, pieces, start):
    full = pieces[0].shape[0]
    keypoints = full - INFO
    hbm = pl.BlockSpec(memory_space=pltpu.HBM)
    vmem = pl.BlockSpec(memory_space=pltpu.VMEM)
    one = jax.ShapeDtypeStruct((members, HEAD_DIM, keypoints), F32)
    two = jax.ShapeDtypeStruct((2 * members, HEAD_DIM, keypoints), F32)
    outs = [one, one] if second_part else [two]
    return pl.pallas_call(
        functools.partial(shared_kernel, members, positions, second_part),
        out_shape=outs,
        in_specs=[hbm] * len(pieces) + [vmem] * second_part,
        out_specs=[vmem] * len(outs),
        scratch_shapes=[
            pltpu.VMEM((2 * members, full, LANES), BF16),
            pltpu.VMEM(two.shape, F32),
            pltpu.VMEM((2 * members, 8, LANES), jnp.int32),
            pltpu.SMEM((2 * members, 8, LANES), jnp.int32),
            pltpu.SMEM((2, 8 * LANES), jnp.int32),
            pltpu.SemaphoreType.DMA((len(pieces),)),
            pltpu.SemaphoreType.DMA,
        ],
        compiler_params=pltpu.CompilerParams(vmem_limit_bytes=VMEM_LIMIT),
        cost_estimate=SHORT if second_part else LONG,
        name="shared_second" if second_part else "shared_first",
    )(*pieces, *([start] if second_part else []))


def far_kernel(members, mine, *refs):
    count = 2 * members
    pieces, refs = refs[:count], refs[count:]
    if mine:
        partial_ref, start_ref, out_ref = refs[:3]
        refs = refs[3:]
    else:
        start_ref, out_ref = refs[:2]
        refs = refs[2:]
    rows, totals, info_v, info, sems, info_sem = refs
    keypoints = totals.shape[2]
    column = lax.axis_index("img")
    member = lax.axis_index("grp")

    def fill():
        totals[...] = start_ref[...]

    load_pieces(range(count), pieces, rows, info_v, info, sems, info_sem, fill)
    ahead = lax.rem(column, 2) == 1
    listed = jnp.where(ahead, 0, members)

    def slot(index, carry):
        owner = listed + index

        def position(step, inner):
            first = place_of(info[owner, 0, 2 + 2 * step], members, member)
            second = info[owner, 0, 3 + 2 * step]
            inside = second // members == column
            second = place_of(second, members, member)
            target = jnp.where(ahead, first, second)
            source = members + jnp.where(ahead, second, first)
            wanted = jnp.logical_and(inside != ahead, (target == 0) == mine)

            @pl.when(wanted)
            def _():
                safe = is_safe(info, target, source)

                @pl.when(safe)
                def _():
                    one_sided(rows, totals, target, source, keypoints, keypoints // 2)

                @pl.when(jnp.logical_not(safe))
                def _():
                    shifted(rows, totals, target, source, keypoints)

            return inner

        return lax.fori_loop(0, info[owner, 0, 0], position, carry)

    lax.fori_loop(0, members, slot, 0)
    if mine:
        out_ref[...] = (totals[0] + partial_ref[0]).astype(BF16)
    else:
        out_ref[...] = totals[...]


def far_pairs(members, mine, pieces, *totals):
    full = pieces[0].shape[0]
    keypoints = full - INFO
    count = len(pieces)
    hbm = pl.BlockSpec(memory_space=pltpu.HBM)
    vmem = pl.BlockSpec(memory_space=pltpu.VMEM)
    whole = jax.ShapeDtypeStruct((members, HEAD_DIM, keypoints), F32)
    message = jax.ShapeDtypeStruct((HEAD_DIM, keypoints), BF16)
    return pl.pallas_call(
        functools.partial(far_kernel, members, mine),
        out_shape=message if mine else whole,
        in_specs=[hbm] * count + [vmem] * len(totals),
        out_specs=vmem,
        scratch_shapes=[
            pltpu.VMEM((count, full, LANES), BF16),
            pltpu.VMEM(whole.shape, F32),
            pltpu.VMEM((count, 8, LANES), jnp.int32),
            pltpu.SMEM((count, 8, LANES), jnp.int32),
            pltpu.SemaphoreType.DMA((count,)),
            pltpu.SemaphoreType.DMA,
        ],
        compiler_params=pltpu.CompilerParams(vmem_limit_bytes=VMEM_LIMIT),
        cost_estimate=LONG,
        name="far_mine" if mine else "far_others",
    )(*pieces, *totals)


def merge_kernel(members, totals_ref, partial_ref, *outs):
    for slot in range(1, members):
        outs[slot - 1][...] = (totals_ref[slot] + partial_ref[slot]).astype(BF16)


def merge(members, totals, partial):
    vmem = pl.BlockSpec(memory_space=pltpu.VMEM)
    message = jax.ShapeDtypeStruct(totals.shape[1:], BF16)
    return pl.pallas_call(
        functools.partial(merge_kernel, members),
        out_shape=[message] * (members - 1),
        in_specs=[vmem, vmem],
        out_specs=[vmem] * (members - 1),
        compiler_params=pltpu.CompilerParams(vmem_limit_bytes=VMEM_LIMIT),
        name="merge",
    )(totals, partial)


def update_kernel(members, desc_ref, w_ref, *refs):
    pieces = refs[:members]
    out_ref = refs[members]
    member = lax.axis_index("grp")
    weights = []
    for distance in range(members):
        head = lax.rem(member - distance + members, members)
        weights.append(w_ref[pl.ds(pl.multiple_of(head * HEAD_DIM, HEAD_DIM), HEAD_DIM), :])
    message = jnp.concatenate([piece[...] for piece in pieces], 0)
    update = lax.dot_general(
        message, jnp.concatenate(weights, 0), TN, preferred_element_type=F32
    )
    out_ref[0] = (desc_ref[0].astype(F32) + update).astype(BF16)


def update(members, desc, w_out, pieces):
    vmem = pl.BlockSpec(memory_space=pltpu.VMEM)
    return pl.pallas_call(
        functools.partial(update_kernel, members),
        out_shape=jax.ShapeDtypeStruct(desc.shape, BF16),
        in_specs=[vmem] * (2 + members),
        out_specs=vmem,
        compiler_params=pltpu.CompilerParams(vmem_limit_bytes=VMEM_LIMIT),
        name="update",
    )(desc, w_out, *pieces)


def on_device(desc, w_proj, w_out, pair_list, pair_count):
    columns = lax.axis_size("img")
    members = lax.axis_size("grp")

    def from_ahead(block, distance):
        route = [((i + distance) % members, i) for i in range(members)]
        return lax.ppermute(block, "grp", route)

    def swap(block, offset):
        pairs = []
        for i in range(offset, columns + offset, 2):
            low, high = i % columns, (i + 1) % columns
            pairs += [(low, high), (high, low)]
        return lax.ppermute(block, "img", pairs)

    sent = project(members, pair_list, pair_count, desc, w_proj)
    late = members // 2
    own = [None] * members
    own[0] = sent[0]
    for k in range(1, members):
        if k != late:
            own[k] = from_ahead(sent[k], k)
    early = [k for k in range(members) if k != late]
    held = lax.optimization_barrier([sent[late]] + [own[k] for k in early[1:]])
    own[late] = from_ahead(held[0], late)
    for k, piece in zip(early[1:], held[1:]):
        own[k] = piece
    near, far = [None] * members, [None] * members
    for k in early:
        near[k], far[k] = swap(own[k], 0), swap(own[k], 1)
    first = tuple(early) + tuple(members + k for k in early)
    both = own + near
    totals = shared(members, first, False, [both[k] for k in first], None)[0]
    totals, own[late], *held = lax.optimization_barrier(
        [totals, own[late]] + [far[k] for k in early]
    )
    for k, piece in zip(early, held):
        far[k] = piece
    near[late], far[late] = swap(own[late], 0), swap(own[late], 1)
    both = own + near
    totals, other = shared(members, tuple(range(2 * members)), True, both, totals)
    partial = swap(other, 0)
    totals = far_pairs(members, False, own + far, totals)
    messages = merge(members, totals, partial)
    mine = far_pairs(members, True, own + far, partial, totals)
    back = [mine]
    for distance in range(1, members):
        back.append(from_ahead(messages[distance - 1], members - distance))
    return update(members, desc, w_out, back)


def solution(mesh):
    return jax.shard_map(
        on_device,
        mesh=mesh,
        in_specs=(
            P(("img", "grp"), None, None),
            P(),
            P(),
            P(("img", "grp"), None),
            P(("img", "grp")),
        ),
        out_specs=P(("img", "grp"), None, None),
        check_vma=False,
    )
```

```python
import functools
import math

import jax
import jax.numpy as jnp
from jax import lax
from jax.experimental import pallas as pl
from jax.experimental.pallas import tpu as pltpu
from jax.sharding import PartitionSpec as P

D = 256
HEADS = 4
HEAD_DIM = 64
LANES = 128
ONES = 16
INFO = 16
SCALE = HEAD_DIM ** -0.5
LOG2E = math.log2(math.e)
SAFE_SCORE = 64.0
NORM_CAP = 250.0
BF16 = jnp.bfloat16
F32 = jnp.float32
NT = (((1,), (1,)), ((), ()))
TN = (((0,), (0,)), ((), ()))
VMEM_LIMIT = 28 * 1024 * 1024
SHORT = pl.CostEstimate(flops=10**4, bytes_accessed=10**4, transcendentals=0)
LONG = pl.CostEstimate(flops=10**10, bytes_accessed=10**7, transcendentals=0)


def project_kernel(members, count_ref, list_hbm, desc_hbm, w_hbm, *refs):
    outs = refs[:members]
    turned, list_ref, desc_ref, w_ref, sems = refs[members:]
    copies = [
        pltpu.make_async_copy(source, target, sems.at[k])
        for k, (source, target) in enumerate(
            ((w_hbm, w_ref), (desc_hbm, desc_ref), (list_hbm, list_ref))
        )
    ]
    for copy in copies:
        copy.start()
    keypoints = desc_ref.shape[1]
    cap = list_ref.shape[1]
    member = lax.axis_index("grp")
    copies[0].wait()
    turned[...] = w_ref[...].T
    copies[2].wait()
    lane = lax.broadcasted_iota(jnp.int32, (INFO, LANES), 1)
    common = jnp.where(lane == 0, count_ref[0], 0)
    for slot in range(cap):
        first = jnp.broadcast_to(list_ref[0:1, slot : slot + 1], lane.shape)
        second = jnp.broadcast_to(list_ref[1:2, slot : slot + 1], lane.shape)
        common = jnp.where(lane == 2 + 2 * slot, first, common)
        common = jnp.where(lane == 3 + 2 * slot, second, common)
    common = common.astype(F32)
    copies[1].wait()
    desc = desc_ref[0]
    for distance in range(members):
        head = lax.rem(member - distance + members, members)
        lower = pl.multiple_of(head * HEAD_DIM, HEAD_DIM)
        weights = jnp.concatenate(
            [turned[pl.ds(lower, HEAD_DIM), :], turned[pl.ds(D + lower, HEAD_DIM), :]], 0
        )
        both = lax.dot_general(weights, desc, NT, preferred_element_type=F32).astype(BF16)
        for block in range(keypoints // LANES):
            outs[distance][block * LANES : (block + 1) * LANES, :] = both[
                :, block * LANES : (block + 1) * LANES
            ]
        query = both[:HEAD_DIM].astype(F32)
        squares = jnp.sum(query * query, axis=0, keepdims=True)
        norm = jnp.sqrt(jnp.max(squares, axis=1, keepdims=True)) * 1.001
        norm = jnp.ceil(jnp.minimum(norm, NORM_CAP))
        info = jnp.where(lane == 1, jnp.broadcast_to(norm, lane.shape), common)
        outs[distance][keypoints:, :] = info.astype(BF16)


def project(members, pair_list, pair_count, desc, w_proj):
    keypoints = desc.shape[1]
    vmem = pl.BlockSpec(memory_space=pltpu.VMEM)
    hbm = pl.BlockSpec(memory_space=pltpu.HBM)
    out = jax.ShapeDtypeStruct((keypoints + INFO, LANES), BF16)
    listed = pair_list.T
    return pl.pallas_call(
        functools.partial(project_kernel, members),
        out_shape=[out] * members,
        in_specs=[pl.BlockSpec(memory_space=pltpu.SMEM), hbm, hbm, hbm],
        out_specs=[vmem] * members,
        scratch_shapes=[
            pltpu.VMEM((2 * D, D), BF16),
            pltpu.VMEM(listed.shape, jnp.int32),
            pltpu.VMEM(desc.shape, BF16),
            pltpu.VMEM(w_proj.shape, BF16),
            pltpu.SemaphoreType.DMA((3,)),
        ],
        name="project",
    )(pair_count, listed, desc, w_proj)


def query_of(rows, image, lower, size):
    parts = [
        rows[image, block : block + HEAD_DIM, :] for block in range(lower, lower + size, LANES)
    ]
    return jnp.concatenate(parts, 1)


def value_of(rows, image, lower, size):
    parts = [
        rows[image, block + HEAD_DIM : block + LANES, :]
        for block in range(lower, lower + size, LANES)
    ]
    return jnp.concatenate([jnp.ones((ONES, size), BF16), jnp.concatenate(parts, 1)], 0)


def one_sided(rows, totals, target, source, keypoints, block):
    query = query_of(rows, target, 0, keypoints)
    total = None
    for lower in range(0, keypoints, block):
        keys = query_of(rows, source, lower, block)
        scores = lax.dot_general(keys, query, TN, preferred_element_type=F32)
        weights = jnp.exp2(scores * (SCALE * LOG2E)).astype(BF16)
        part = jnp.dot(value_of(rows, source, lower, block), weights, preferred_element_type=F32)
        total = part if total is None else total + part
    totals[target] += total[ONES:] / total[:1]


def two_sided(rows, totals, target, source, keypoints, block):
    keys = query_of(rows, source, 0, keypoints)
    values = value_of(rows, source, 0, keypoints)
    back = None
    for lower in range(0, keypoints, block):
        query = query_of(rows, target, lower, block)
        scores = lax.dot_general(query, keys, TN, preferred_element_type=F32)
        weights = jnp.exp2(scores * (SCALE * LOG2E)).astype(BF16)
        total = lax.dot_general(values, weights, NT, preferred_element_type=F32)
        totals[target, :, lower : lower + block] += total[ONES:] / total[:1]
        part = jnp.dot(value_of(rows, target, lower, block), weights, preferred_element_type=F32)
        back = part if back is None else back + part
    totals[source] += back[ONES:] / back[:1]


def shifted(rows, totals, target, source, keypoints):
    narrow = 2 * LANES
    keys = query_of(rows, source, 0, keypoints)
    values = value_of(rows, source, 0, keypoints)

    def step(index, carry):
        lower = pl.multiple_of(index * narrow, narrow)
        parts = [
            rows[target, pl.ds(pl.multiple_of(lower + offset, LANES), HEAD_DIM), :]
            for offset in range(0, narrow, LANES)
        ]
        query = jnp.concatenate(parts, 1)
        scores = lax.dot_general(keys, query, TN, preferred_element_type=F32) * SCALE
        weights = jnp.exp(scores - jnp.max(scores, axis=0, keepdims=True)).astype(BF16)
        total = jnp.dot(values, weights, preferred_element_type=F32)
        totals[target, :, pl.ds(lower, narrow)] += total[ONES:] / total[:1]
        return carry

    lax.fori_loop(0, keypoints // narrow, step, 0)


def load_pieces(positions, pieces, rows, info_v, info, sems, info_sem, fill):
    keypoints = rows.shape[1] - INFO
    copies = [
        pltpu.make_async_copy(piece, rows.at[position], sems.at[k])
        for k, (position, piece) in enumerate(zip(positions, pieces))
    ]
    for copy in copies:
        copy.start()
    fill()
    for position, copy in zip(positions, copies):
        copy.wait()
        info_v[position] = rows[position, keypoints:, :].astype(F32).astype(jnp.int32)[:8]
    copy = pltpu.make_async_copy(info_v, info, info_sem)
    copy.start()
    copy.wait()


def place_of(image, members, member):
    return lax.rem(lax.rem(image, members) - member + members, members)


def is_safe(info, target, source):
    left = info[target, 0, 1]
    right = info[source, 0, 1]
    return jnp.logical_and(
        jnp.maximum(left, right) < int(NORM_CAP), left * right <= int(SAFE_SCORE / SCALE)
    )


def shared_kernel(members, *refs):
    count = 2 * members
    pieces, (own_ref, other_ref, *refs) = refs[:count], refs[count:]
    rows, totals, info_v, info, units, sems, info_sem = refs
    keypoints = totals.shape[2]
    column = lax.axis_index("img")
    member = lax.axis_index("grp")

    def fill():
        totals[...] = jnp.zeros_like(totals)

    load_pieces(range(count), pieces, rows, info_v, info, sems, info_sem, fill)
    side = lax.rem(column, 2)

    def slot(index, found):
        right = index >= members
        base = jnp.where(right == (side == 1), 0, members)
        owner = base + lax.rem(index, members)
        listed = column - side + right.astype(jnp.int32)

        def position(step, found):
            first = info[owner, 0, 2 + 2 * step]
            second = info[owner, 0, 3 + 2 * step]
            inside = second // members == listed
            shared = jnp.logical_or(jnp.logical_not(right), inside)

            @pl.when(shared)
            def _():
                units[0, found] = base + place_of(first, members, member)
                units[1, found] = jnp.where(inside, base, members - base) + place_of(
                    second, members, member
                )

            return found + shared.astype(jnp.int32)

        return lax.fori_loop(0, info[owner, 0, 0], position, found)

    found = lax.fori_loop(0, count, slot, jnp.int32(0))
    half = found // 2
    begin = jnp.where(side == 0, 0, half)
    end = jnp.where(side == 0, half, found)

    def visit(index, carry):
        target, source = units[0, index], units[1, index]
        safe = is_safe(info, target, source)

        @pl.when(safe)
        def _():
            two_sided(rows, totals, target, source, keypoints, keypoints // 2)

        @pl.when(jnp.logical_not(safe))
        def _():
            shifted(rows, totals, target, source, keypoints)
            shifted(rows, totals, source, target, keypoints)

        return carry

    lax.fori_loop(begin, end, visit, 0)
    own_ref[...] = totals[:members]
    other_ref[...] = totals[members:]


def shared(members, pieces):
    full = pieces[0].shape[0]
    keypoints = full - INFO
    count = len(pieces)
    hbm = pl.BlockSpec(memory_space=pltpu.HBM)
    vmem = pl.BlockSpec(memory_space=pltpu.VMEM)
    whole = jax.ShapeDtypeStruct((members, HEAD_DIM, keypoints), F32)
    return pl.pallas_call(
        functools.partial(shared_kernel, members),
        out_shape=[whole, whole],
        in_specs=[hbm] * count,
        out_specs=[vmem, vmem],
        scratch_shapes=[
            pltpu.VMEM((count, full, LANES), BF16),
            pltpu.VMEM((count, HEAD_DIM, keypoints), F32),
            pltpu.VMEM((count, 8, LANES), jnp.int32),
            pltpu.SMEM((count, 8, LANES), jnp.int32),
            pltpu.SMEM((2, 8 * LANES), jnp.int32),
            pltpu.SemaphoreType.DMA((count,)),
            pltpu.SemaphoreType.DMA,
        ],
        compiler_params=pltpu.CompilerParams(vmem_limit_bytes=VMEM_LIMIT),
        cost_estimate=SHORT,
        name="shared",
    )(*pieces)


def far_kernel(members, *refs):
    count = 2 * members
    pieces, (start_ref, out_ref, *refs) = refs[:count], refs[count:]
    rows, info_v, info, sems, info_sem = refs
    keypoints = out_ref.shape[2]
    column = lax.axis_index("img")
    member = lax.axis_index("grp")

    def fill():
        out_ref[...] = start_ref[...]

    load_pieces(range(count), pieces, rows, info_v, info, sems, info_sem, fill)
    ahead = lax.rem(column, 2) == 1
    listed = jnp.where(ahead, 0, members)

    def slot(index, carry):
        owner = listed + index

        def position(step, inner):
            first = info[owner, 0, 2 + 2 * step]
            second = info[owner, 0, 3 + 2 * step]
            inside = second // members == column

            @pl.when(inside != ahead)
            def _():
                left = place_of(first, members, member)
                right = place_of(second, members, member)
                target = jnp.where(ahead, left, right)
                source = members + jnp.where(ahead, right, left)
                safe = is_safe(info, target, source)

                @pl.when(safe)
                def _():
                    one_sided(rows, out_ref, target, source, keypoints, keypoints // 2)

                @pl.when(jnp.logical_not(safe))
                def _():
                    shifted(rows, out_ref, target, source, keypoints)

            return inner

        return lax.fori_loop(0, info[owner, 0, 0], position, carry)

    lax.fori_loop(0, members, slot, 0)


def far_pairs(members, pieces, totals):
    full = pieces[0].shape[0]
    count = len(pieces)
    hbm = pl.BlockSpec(memory_space=pltpu.HBM)
    vmem = pl.BlockSpec(memory_space=pltpu.VMEM)
    return pl.pallas_call(
        functools.partial(far_kernel, members),
        out_shape=jax.ShapeDtypeStruct(totals.shape, F32),
        in_specs=[hbm] * count + [vmem],
        out_specs=vmem,
        scratch_shapes=[
            pltpu.VMEM((count, full, LANES), BF16),
            pltpu.VMEM((count, 8, LANES), jnp.int32),
            pltpu.SMEM((count, 8, LANES), jnp.int32),
            pltpu.SemaphoreType.DMA((count,)),
            pltpu.SemaphoreType.DMA,
        ],
        compiler_params=pltpu.CompilerParams(vmem_limit_bytes=VMEM_LIMIT),
        cost_estimate=LONG,
        name="far_pairs",
    )(*pieces, totals)


def merge_kernel(totals_ref, partial_ref, *outs):
    for slot, out_ref in enumerate(outs):
        out_ref[...] = (totals_ref[slot] + partial_ref[slot]).astype(BF16)


def merge(members, totals, partial):
    vmem = pl.BlockSpec(memory_space=pltpu.VMEM)
    message = jax.ShapeDtypeStruct(totals.shape[1:], BF16)
    return pl.pallas_call(
        merge_kernel,
        out_shape=[message] * members,
        in_specs=[vmem, vmem],
        out_specs=[vmem] * members,
        compiler_params=pltpu.CompilerParams(vmem_limit_bytes=VMEM_LIMIT),
        name="merge",
    )(totals, partial)


def update_kernel(members, desc_ref, w_ref, *refs):
    pieces = refs[:members]
    out_ref = refs[members]
    member = lax.axis_index("grp")
    weights = []
    for distance in range(members):
        head = lax.rem(member - distance + members, members)
        weights.append(w_ref[pl.ds(pl.multiple_of(head * HEAD_DIM, HEAD_DIM), HEAD_DIM), :])
    message = jnp.concatenate([piece[...] for piece in pieces], 0)
    update = lax.dot_general(
        message, jnp.concatenate(weights, 0), TN, preferred_element_type=F32
    )
    out_ref[0] = (desc_ref[0].astype(F32) + update).astype(BF16)


def update(members, desc, w_out, pieces):
    vmem = pl.BlockSpec(memory_space=pltpu.VMEM)
    return pl.pallas_call(
        functools.partial(update_kernel, members),
        out_shape=jax.ShapeDtypeStruct(desc.shape, BF16),
        in_specs=[vmem] * (2 + members),
        out_specs=vmem,
        compiler_params=pltpu.CompilerParams(vmem_limit_bytes=VMEM_LIMIT),
        name="update",
    )(desc, w_out, *pieces)


def on_device(desc, w_proj, w_out, pair_list, pair_count):
    columns = lax.axis_size("img")
    members = lax.axis_size("grp")

    def from_ahead(block, distance):
        route = [((i + distance) % members, i) for i in range(members)]
        return lax.ppermute(block, "grp", route)

    def swap(block, offset):
        pairs = []
        for i in range(offset, columns + offset, 2):
            low, high = i % columns, (i + 1) % columns
            pairs += [(low, high), (high, low)]
        return lax.ppermute(block, "img", pairs)

    sent = project(members, pair_list, pair_count, desc, w_proj)
    own = [sent[0]] + [from_ahead(sent[k], k) for k in range(1, members)]
    near, far = [swap(own[0], 0)], [swap(own[0], 1)]
    last = members // 2
    far[0], own[last] = lax.optimization_barrier((far[0], own[last]))
    near += [swap(block, 0) for block in own[1:]]
    far += [swap(block, 1) for block in own[1:]]
    totals, other = shared(members, own + near)
    partial = swap(other, 0)
    totals = far_pairs(members, own + far, totals)
    messages = merge(members, totals, partial)
    back = [messages[0]]
    for distance in range(1, members):
        back.append(from_ahead(messages[distance], members - distance))
    return update(members, desc, w_out, back)


def solution(mesh):
    return jax.shard_map(
        on_device,
        mesh=mesh,
        in_specs=(
            P(("img", "grp"), None, None),
            P(),
            P(),
            P(("img", "grp"), None),
            P(("img", "grp")),
        ),
        out_specs=P(("img", "grp"), None, None),
        check_vma=False,
    )
```

```python
import functools
import math

import jax
import jax.numpy as jnp
from jax import lax
from jax.experimental import pallas as pl
from jax.experimental.pallas import tpu as pltpu
from jax.sharding import PartitionSpec as P

D = 256
HEADS = 4
HEAD_DIM = 64
LANES = 128
ONES = 16
INFO = 16
SCALE = HEAD_DIM ** -0.5
LOG2E = math.log2(math.e)
SAFE_SCORE = 64.0
NORM_CAP = 250.0
BF16 = jnp.bfloat16
F32 = jnp.float32
NT = (((1,), (1,)), ((), ()))
TN = (((0,), (0,)), ((), ()))
VMEM_LIMIT = 28 * 1024 * 1024
SHORT = pl.CostEstimate(flops=10**4, bytes_accessed=10**4, transcendentals=0)
LONG = pl.CostEstimate(flops=10**10, bytes_accessed=10**7, transcendentals=0)


def project_kernel(members, count_ref, list_hbm, desc_hbm, w_hbm, *refs):
    outs = refs[:members]
    turned, list_ref, desc_ref, w_ref, sems = refs[members:]
    copies = [
        pltpu.make_async_copy(source, target, sems.at[k])
        for k, (source, target) in enumerate(
            ((w_hbm, w_ref), (desc_hbm, desc_ref), (list_hbm, list_ref))
        )
    ]
    for copy in copies:
        copy.start()
    keypoints = desc_ref.shape[1]
    cap = list_ref.shape[1]
    member = lax.axis_index("grp")
    copies[0].wait()
    turned[...] = w_ref[...].T
    copies[2].wait()
    lane = lax.broadcasted_iota(jnp.int32, (INFO, LANES), 1)
    common = jnp.where(lane == 0, count_ref[0], 0)
    for slot in range(cap):
        first = jnp.broadcast_to(list_ref[0:1, slot : slot + 1], lane.shape)
        second = jnp.broadcast_to(list_ref[1:2, slot : slot + 1], lane.shape)
        common = jnp.where(lane == 2 + 2 * slot, first, common)
        common = jnp.where(lane == 3 + 2 * slot, second, common)
    common = common.astype(F32)
    copies[1].wait()
    desc = desc_ref[0]
    for distance in range(members):
        head = lax.rem(member - distance + members, members)
        lower = pl.multiple_of(head * HEAD_DIM, HEAD_DIM)
        weights = jnp.concatenate(
            [turned[pl.ds(lower, HEAD_DIM), :], turned[pl.ds(D + lower, HEAD_DIM), :]], 0
        )
        both = lax.dot_general(weights, desc, NT, preferred_element_type=F32).astype(BF16)
        for block in range(keypoints // LANES):
            outs[distance][block * LANES : (block + 1) * LANES, :] = both[
                :, block * LANES : (block + 1) * LANES
            ]
        query = both[:HEAD_DIM].astype(F32)
        squares = jnp.sum(query * query, axis=0, keepdims=True)
        norm = jnp.sqrt(jnp.max(squares, axis=1, keepdims=True)) * 1.001
        norm = jnp.ceil(jnp.minimum(norm, NORM_CAP))
        info = jnp.where(lane == 1, jnp.broadcast_to(norm, lane.shape), common)
        outs[distance][keypoints:, :] = info.astype(BF16)


def project(members, pair_list, pair_count, desc, w_proj):
    keypoints = desc.shape[1]
    vmem = pl.BlockSpec(memory_space=pltpu.VMEM)
    hbm = pl.BlockSpec(memory_space=pltpu.HBM)
    out = jax.ShapeDtypeStruct((keypoints + INFO, LANES), BF16)
    listed = pair_list.T
    return pl.pallas_call(
        functools.partial(project_kernel, members),
        out_shape=[out] * members,
        in_specs=[pl.BlockSpec(memory_space=pltpu.SMEM), hbm, hbm, hbm],
        out_specs=[vmem] * members,
        scratch_shapes=[
            pltpu.VMEM((2 * D, D), BF16),
            pltpu.VMEM(listed.shape, jnp.int32),
            pltpu.VMEM(desc.shape, BF16),
            pltpu.VMEM(w_proj.shape, BF16),
            pltpu.SemaphoreType.DMA((3,)),
        ],
        name="project",
    )(pair_count, listed, desc, w_proj)


def query_of(rows, image, lower, size):
    parts = [
        rows[image, block : block + HEAD_DIM, :] for block in range(lower, lower + size, LANES)
    ]
    return jnp.concatenate(parts, 1)


def value_of(rows, image, lower, size):
    parts = [
        rows[image, block + HEAD_DIM : block + LANES, :]
        for block in range(lower, lower + size, LANES)
    ]
    return jnp.concatenate([jnp.ones((ONES, size), BF16), jnp.concatenate(parts, 1)], 0)


def score_one(rows, target, source, weights, block):
    keypoints = weights.shape[0]
    query = query_of(rows, target, 0, keypoints)
    for lower in range(0, keypoints, block):
        keys = query_of(rows, source, lower, block)
        scores = lax.dot_general(keys, query, TN, preferred_element_type=F32)
        weights[lower : lower + block, :] = jnp.exp2(scores * (SCALE * LOG2E)).astype(BF16)


def apply_one(rows, totals, target, source, weights):
    values = value_of(rows, source, 0, weights.shape[0])
    total = jnp.dot(values, weights[...], preferred_element_type=F32)
    totals[target] += total[ONES:] / total[:1]


def score_two(rows, target, source, weights, block):
    score_one(rows, source, target, weights, block)


def apply_two(rows, totals, target, source, weights):
    values = value_of(rows, source, 0, weights.shape[0])
    total = lax.dot_general(values, weights[...], NT, preferred_element_type=F32)
    totals[target] += total[ONES:] / total[:1]
    apply_one(rows, totals, source, target, weights)


def run_units(rows, totals, units, begin, count, even_weights, odd_weights, score, apply):
    block = even_weights.shape[0] // 2

    def scored(index, weights):
        score(rows, units[0, index], units[1, index], weights, block)

    def applied(index, weights):
        apply(rows, totals, units[0, index], units[1, index], weights)

    @pl.when(count > 0)
    def _():
        scored(begin, even_weights)

        def step(index, carry):
            now = begin + 2 * index
            scored(now + 1, odd_weights)
            applied(now, even_weights)
            scored(now + 2, even_weights)
            applied(now + 1, odd_weights)
            return carry

        lax.fori_loop(0, (count - 1) // 2, step, 0)
        last = begin + count - 1

        @pl.when(lax.rem(count, 2) == 0)
        def _():
            scored(last, odd_weights)
            applied(last - 1, even_weights)
            applied(last, odd_weights)

        @pl.when(lax.rem(count, 2) == 1)
        def _():
            applied(last, even_weights)


def shifted(rows, totals, target, source, keypoints):
    narrow = 2 * LANES
    keys = query_of(rows, source, 0, keypoints)
    values = value_of(rows, source, 0, keypoints)

    def step(index, carry):
        lower = pl.multiple_of(index * narrow, narrow)
        parts = [
            rows[target, pl.ds(pl.multiple_of(lower + offset, LANES), HEAD_DIM), :]
            for offset in range(0, narrow, LANES)
        ]
        query = jnp.concatenate(parts, 1)
        scores = lax.dot_general(keys, query, TN, preferred_element_type=F32) * SCALE
        weights = jnp.exp(scores - jnp.max(scores, axis=0, keepdims=True)).astype(BF16)
        total = jnp.dot(values, weights, preferred_element_type=F32)
        totals[target, :, pl.ds(lower, narrow)] += total[ONES:] / total[:1]
        return carry

    lax.fori_loop(0, keypoints // narrow, step, 0)


def load_pieces(pieces, rows, info_v, info, sems, info_sem, fill):
    keypoints = rows.shape[1] - INFO
    copies = []
    position = 0
    for piece in pieces:
        size = piece.shape[0] if len(piece.shape) == 3 else 1
        place = rows.at[position : position + size] if len(piece.shape) == 3 else rows.at[position]
        copies.append(pltpu.make_async_copy(piece, place, sems.at[len(copies)]))
        position += size
    for copy in copies:
        copy.start()
    fill()
    for copy in copies:
        copy.wait()
    for position in range(rows.shape[0]):
        info_v[position] = rows[position, keypoints:, :].astype(F32).astype(jnp.int32)[:8]
    copy = pltpu.make_async_copy(info_v, info, info_sem)
    copy.start()
    copy.wait()


def place_of(image, members, member):
    return lax.rem(lax.rem(image, members) - member + members, members)


def shared_kernel(members, pieces_count, *refs):
    count = 2 * members
    pieces, (own_ref, other_ref, *refs) = refs[:pieces_count], refs[pieces_count:]
    rows, totals, even_weights, odd_weights, info_v, info, units, sems, info_sem = refs
    keypoints = totals.shape[2]
    column = lax.axis_index("img")
    member = lax.axis_index("grp")

    def fill():
        totals[...] = jnp.zeros_like(totals)

    load_pieces(pieces, rows, info_v, info, sems, info_sem, fill)
    side = lax.rem(column, 2)

    def slot(index, found):
        right = index >= members
        base = jnp.where(right == (side == 1), 0, members)
        owner = base + lax.rem(index, members)
        listed = column - side + right.astype(jnp.int32)

        def position(step, found):
            first = info[owner, 0, 2 + 2 * step]
            second = info[owner, 0, 3 + 2 * step]
            inside = second // members == listed
            shared = jnp.logical_or(jnp.logical_not(right), inside)

            @pl.when(shared)
            def _():
                units[0, found] = base + place_of(first, members, member)
                units[1, found] = jnp.where(inside, base, members - base) + place_of(
                    second, members, member
                )

            return found + shared.astype(jnp.int32)

        return lax.fori_loop(0, info[owner, 0, 0], position, found)

    found = lax.fori_loop(0, count, slot, jnp.int32(0))
    half = found // 2
    begin = jnp.where(side == 0, 0, half)
    end = jnp.where(side == 0, half, found)
    largest = info[0, 0, 1]
    for position in range(1, count):
        largest = jnp.maximum(largest, info[position, 0, 1])
    safe = largest * largest <= int(SAFE_SCORE / SCALE)

    @pl.when(safe)
    def _():
        run_units(
            rows, totals, units, begin, end - begin, even_weights, odd_weights,
            score_two, apply_two,
        )

    @pl.when(jnp.logical_not(safe))
    def _():
        def visit(index, carry):
            target, source = units[0, index], units[1, index]
            shifted(rows, totals, target, source, keypoints)
            shifted(rows, totals, source, target, keypoints)
            return carry

        lax.fori_loop(begin, end, visit, 0)

    own_ref[...] = totals[:members]
    other_ref[...] = totals[members:]


def pair_scratch(count, full, pieces_count):
    keypoints = full - INFO
    return [
        pltpu.VMEM((keypoints, keypoints), BF16),
        pltpu.VMEM((keypoints, keypoints), BF16),
        pltpu.VMEM((count, 8, LANES), jnp.int32),
        pltpu.SMEM((count, 8, LANES), jnp.int32),
        pltpu.SMEM((2, 8 * LANES), jnp.int32),
        pltpu.SemaphoreType.DMA((pieces_count,)),
        pltpu.SemaphoreType.DMA,
    ]


def shared(members, pieces):
    full = pieces[0].shape[1]
    keypoints = full - INFO
    count = 2 * members
    hbm = pl.BlockSpec(memory_space=pltpu.HBM)
    vmem = pl.BlockSpec(memory_space=pltpu.VMEM)
    whole = jax.ShapeDtypeStruct((members, HEAD_DIM, keypoints), F32)
    return pl.pallas_call(
        functools.partial(shared_kernel, members, len(pieces)),
        out_shape=[whole, whole],
        in_specs=[hbm] * len(pieces),
        out_specs=[vmem, vmem],
        scratch_shapes=[
            pltpu.VMEM((count, full, LANES), BF16),
            pltpu.VMEM((count, HEAD_DIM, keypoints), F32),
            *pair_scratch(count, full, len(pieces)),
        ],
        compiler_params=pltpu.CompilerParams(vmem_limit_bytes=VMEM_LIMIT),
        cost_estimate=SHORT,
        name="shared",
    )(*pieces)


def far_kernel(members, pieces_count, *refs):
    count = 2 * members
    pieces, (start_ref, out_ref, *refs) = refs[:pieces_count], refs[pieces_count:]
    rows, even_weights, odd_weights, info_v, info, units, sems, info_sem = refs
    keypoints = out_ref.shape[2]
    column = lax.axis_index("img")
    member = lax.axis_index("grp")

    def fill():
        out_ref[...] = start_ref[...]

    load_pieces(pieces, rows, info_v, info, sems, info_sem, fill)
    ahead = lax.rem(column, 2) == 1
    listed = jnp.where(ahead, 0, members)

    def slot(index, found):
        owner = listed + index

        def position(step, found):
            first = info[owner, 0, 2 + 2 * step]
            second = info[owner, 0, 3 + 2 * step]
            wanted = (second // members == column) != ahead

            @pl.when(wanted)
            def _():
                left = place_of(first, members, member)
                right = place_of(second, members, member)
                units[0, found] = jnp.where(ahead, left, right)
                units[1, found] = members + jnp.where(ahead, right, left)

            return found + wanted.astype(jnp.int32)

        return lax.fori_loop(0, info[owner, 0, 0], position, found)

    found = lax.fori_loop(0, members, slot, jnp.int32(0))
    left, right = info[0, 0, 1], info[members, 0, 1]
    for position in range(1, members):
        left = jnp.maximum(left, info[position, 0, 1])
        right = jnp.maximum(right, info[members + position, 0, 1])
    safe = jnp.logical_and(
        jnp.maximum(left, right) < int(NORM_CAP), left * right <= int(SAFE_SCORE / SCALE)
    )

    @pl.when(safe)
    def _():
        run_units(
            rows, out_ref, units, jnp.int32(0), found, even_weights, odd_weights,
            score_one, apply_one,
        )

    @pl.when(jnp.logical_not(safe))
    def _():
        def visit(index, carry):
            shifted(rows, out_ref, units[0, index], units[1, index], keypoints)
            return carry

        lax.fori_loop(0, found, visit, 0)


def far_pairs(members, pieces, totals):
    full = pieces[0].shape[1]
    count = 2 * members
    hbm = pl.BlockSpec(memory_space=pltpu.HBM)
    vmem = pl.BlockSpec(memory_space=pltpu.VMEM)
    return pl.pallas_call(
        functools.partial(far_kernel, members, len(pieces)),
        out_shape=jax.ShapeDtypeStruct(totals.shape, F32),
        in_specs=[hbm] * len(pieces) + [vmem],
        out_specs=vmem,
        scratch_shapes=[
            pltpu.VMEM((count, full, LANES), BF16),
            *pair_scratch(count, full, len(pieces)),
        ],
        compiler_params=pltpu.CompilerParams(vmem_limit_bytes=VMEM_LIMIT),
        cost_estimate=LONG,
        name="far_pairs",
    )(*pieces, totals)


def merge_kernel(totals_ref, partial_ref, *outs):
    for slot, out_ref in enumerate(outs):
        out_ref[...] = (totals_ref[slot] + partial_ref[slot]).astype(BF16)


def merge(members, totals, partial):
    vmem = pl.BlockSpec(memory_space=pltpu.VMEM)
    message = jax.ShapeDtypeStruct(totals.shape[1:], BF16)
    return pl.pallas_call(
        merge_kernel,
        out_shape=[message] * members,
        in_specs=[vmem, vmem],
        out_specs=[vmem] * members,
        compiler_params=pltpu.CompilerParams(vmem_limit_bytes=VMEM_LIMIT),
        name="merge",
    )(totals, partial)


def update_kernel(members, desc_ref, w_ref, *refs):
    pieces = refs[:members]
    out_ref = refs[members]
    member = lax.axis_index("grp")
    weights = []
    for distance in range(members):
        head = lax.rem(member - distance + members, members)
        weights.append(w_ref[pl.ds(pl.multiple_of(head * HEAD_DIM, HEAD_DIM), HEAD_DIM), :])
    message = jnp.concatenate([piece[...] for piece in pieces], 0)
    update = lax.dot_general(
        message, jnp.concatenate(weights, 0), TN, preferred_element_type=F32
    )
    out_ref[0] = (desc_ref[0].astype(F32) + update).astype(BF16)


def update(members, desc, w_out, pieces):
    vmem = pl.BlockSpec(memory_space=pltpu.VMEM)
    return pl.pallas_call(
        functools.partial(update_kernel, members),
        out_shape=jax.ShapeDtypeStruct(desc.shape, BF16),
        in_specs=[vmem] * (2 + members),
        out_specs=vmem,
        compiler_params=pltpu.CompilerParams(vmem_limit_bytes=VMEM_LIMIT),
        name="update",
    )(desc, w_out, *pieces)


def on_device(desc, w_proj, w_out, pair_list, pair_count):
    columns = lax.axis_size("img")
    members = lax.axis_size("grp")

    def from_ahead(block, distance):
        route = [((i + distance) % members, i) for i in range(members)]
        return lax.ppermute(block, "grp", route)

    def swap(block, offset):
        pairs = []
        for i in range(offset, columns + offset, 2):
            low, high = i % columns, (i + 1) % columns
            pairs += [(low, high), (high, low)]
        return lax.ppermute(block, "img", pairs)

    sent = project(members, pair_list, pair_count, desc, w_proj)
    own = [sent[0]] + [from_ahead(sent[k], k) for k in range(1, members)]
    near = [swap(block, 0) for block in own]
    gathered, *near = lax.optimization_barrier([jnp.stack(own)] + near)
    far = swap(gathered, 1)
    totals, other = shared(members, [gathered] + near)
    partial = swap(other, 0)
    totals = far_pairs(members, [gathered, far], totals)
    messages = merge(members, totals, partial)
    back = [messages[0]]
    for distance in range(1, members):
        back.append(from_ahead(messages[distance], members - distance))
    return update(members, desc, w_out, back)


def solution(mesh):
    return jax.shard_map(
        on_device,
        mesh=mesh,
        in_specs=(
            P(("img", "grp"), None, None),
            P(),
            P(),
            P(("img", "grp"), None),
            P(("img", "grp")),
        ),
        out_specs=P(("img", "grp"), None, None),
        check_vma=False,
    )
```

```python
import functools
import math

import jax
import jax.numpy as jnp
from jax import lax
from jax.experimental import pallas as pl
from jax.experimental.pallas import tpu as pltpu
from jax.sharding import PartitionSpec as P

D = 256
HEADS = 4
HEAD_DIM = 64
LANES = 128
ONES = 16
INFO = 16
SCALE = HEAD_DIM ** -0.5
LOG2E = math.log2(math.e)
SAFE_SCORE = 64.0
NORM_CAP = 250.0
BF16 = jnp.bfloat16
F32 = jnp.float32
NT = (((1,), (1,)), ((), ()))
TN = (((0,), (0,)), ((), ()))
VMEM_LIMIT = 28 * 1024 * 1024
ROW = 16
SHORT = pl.CostEstimate(flops=10**4, bytes_accessed=10**4, transcendentals=0)
LONG = pl.CostEstimate(flops=10**10, bytes_accessed=10**7, transcendentals=0)


def project_kernel(members, count_ref, list_hbm, desc_hbm, w_hbm, *refs):
    outs = refs[:members]
    turned, list_ref, desc_ref, w_ref, held, sems, out_sems = refs[members:]
    copies = [
        pltpu.make_async_copy(source, target, sems.at[k])
        for k, (source, target) in enumerate(
            ((w_hbm, w_ref), (desc_hbm, desc_ref), (list_hbm, list_ref))
        )
    ]
    for copy in copies:
        copy.start()
    keypoints = desc_ref.shape[1]
    cap = list_ref.shape[1]
    member = lax.axis_index("grp")
    copies[0].wait()
    turned[...] = w_ref[...].T
    copies[2].wait()
    lane = lax.broadcasted_iota(jnp.int32, (INFO, LANES), 1)
    common = jnp.where(lane == 0, count_ref[0], 0)
    for slot in range(cap):
        first = jnp.broadcast_to(list_ref[0:1, slot : slot + 1], lane.shape)
        second = jnp.broadcast_to(list_ref[1:2, slot : slot + 1], lane.shape)
        common = jnp.where(lane == 2 + 2 * slot, first, common)
        common = jnp.where(lane == 3 + 2 * slot, second, common)
    common = common.astype(F32)
    copies[1].wait()
    desc = desc_ref[0]
    written = []
    for distance in range(members):
        head = lax.rem(member - distance + members, members)
        lower = pl.multiple_of(head * HEAD_DIM, HEAD_DIM)
        weights = jnp.concatenate(
            [turned[pl.ds(lower, HEAD_DIM), :], turned[pl.ds(D + lower, HEAD_DIM), :]], 0
        )
        both = lax.dot_general(weights, desc, NT, preferred_element_type=F32).astype(BF16)
        for block in range(keypoints // LANES):
            held[distance, block * LANES : (block + 1) * LANES, :] = both[
                :, block * LANES : (block + 1) * LANES
            ]
        query = both[:HEAD_DIM].astype(F32)
        squares = jnp.sum(query * query, axis=0, keepdims=True)
        norm = jnp.sqrt(jnp.max(squares, axis=1, keepdims=True)) * 1.001
        norm = jnp.ceil(jnp.minimum(norm, NORM_CAP))
        info = jnp.where(lane == 1, jnp.broadcast_to(norm, lane.shape), common)
        held[distance, keypoints:, :] = info.astype(BF16)
        copy = pltpu.make_async_copy(held.at[distance], outs[distance], out_sems.at[distance])
        copy.start()
        written.append(copy)
    for copy in written:
        copy.wait()


def project(members, pair_list, pair_count, desc, w_proj):
    keypoints = desc.shape[1]
    hbm = pl.BlockSpec(memory_space=pltpu.HBM)
    out = jax.ShapeDtypeStruct((keypoints + INFO, LANES), BF16)
    listed = pair_list.T
    return pl.pallas_call(
        functools.partial(project_kernel, members),
        out_shape=[out] * members,
        in_specs=[pl.BlockSpec(memory_space=pltpu.SMEM), hbm, hbm, hbm],
        out_specs=[hbm] * members,
        scratch_shapes=[
            pltpu.VMEM((2 * D, D), BF16),
            pltpu.VMEM(listed.shape, jnp.int32),
            pltpu.VMEM(desc.shape, BF16),
            pltpu.VMEM(w_proj.shape, BF16),
            pltpu.VMEM((members, *out.shape), BF16),
            pltpu.SemaphoreType.DMA((3,)),
            pltpu.SemaphoreType.DMA((members,)),
        ],
        name="project",
    )(pair_count, listed, desc, w_proj)


def query_of(rows, image, lower, size):
    parts = [
        rows[image, block : block + HEAD_DIM, :] for block in range(lower, lower + size, LANES)
    ]
    return jnp.concatenate(parts, 1)


def value_of(rows, image, lower, size):
    parts = [
        rows[image, block + HEAD_DIM : block + LANES, :]
        for block in range(lower, lower + size, LANES)
    ]
    return jnp.concatenate([jnp.ones((ONES, size), BF16), jnp.concatenate(parts, 1)], 0)


def score_one(rows, others, target, source, weights, block):
    keypoints = weights.shape[0]
    query = query_of(rows, target, 0, keypoints)
    for lower in range(0, keypoints, block):
        keys = query_of(others, source, lower, block)
        scores = lax.dot_general(keys, query, TN, preferred_element_type=F32)
        weights[lower : lower + block, :] = jnp.exp2(scores * (SCALE * LOG2E)).astype(BF16)


def apply_one(rows, others, totals, target, source, weights):
    values = value_of(others, source, 0, weights.shape[0])
    total = jnp.dot(values, weights[...], preferred_element_type=F32)
    totals[target] += total[ONES:] / total[:1]


def score_two(rows, others, target, source, weights, block):
    score_one(others, rows, source, target, weights, block)


def apply_two(rows, others, totals, target, source, weights):
    values = value_of(others, source, 0, weights.shape[0])
    total = lax.dot_general(values, weights[...], NT, preferred_element_type=F32)
    totals[target] += total[ONES:] / total[:1]
    apply_one(others, rows, totals, source, target, weights)


def run_units(rows, others, totals, units, begin, count, even_weights, odd_weights, score, apply):
    block = even_weights.shape[0] // 2

    def scored(index, weights):
        score(rows, others, units[0, index], units[1, index], weights, block)

    def applied(index, weights):
        apply(rows, others, totals, units[0, index], units[1, index], weights)

    @pl.when(count > 0)
    def _():
        scored(begin, even_weights)

        def step(index, carry):
            now = begin + 2 * index
            scored(now + 1, odd_weights)
            applied(now, even_weights)
            scored(now + 2, even_weights)
            applied(now + 1, odd_weights)
            return carry

        lax.fori_loop(0, (count - 1) // 2, step, 0)
        last = begin + count - 1

        @pl.when(lax.rem(count, 2) == 0)
        def _():
            scored(last, odd_weights)
            applied(last - 1, even_weights)
            applied(last, odd_weights)

        @pl.when(lax.rem(count, 2) == 1)
        def _():
            applied(last, even_weights)


def shifted(rows, others, totals, target, source, keypoints):
    narrow = 2 * LANES
    keys = query_of(others, source, 0, keypoints)
    values = value_of(others, source, 0, keypoints)

    def step(index, carry):
        lower = pl.multiple_of(index * narrow, narrow)
        parts = [
            rows[target, pl.ds(pl.multiple_of(lower + offset, LANES), HEAD_DIM), :]
            for offset in range(0, narrow, LANES)
        ]
        query = jnp.concatenate(parts, 1)
        scores = lax.dot_general(keys, query, TN, preferred_element_type=F32) * SCALE
        weights = jnp.exp(scores - jnp.max(scores, axis=0, keepdims=True)).astype(BF16)
        total = jnp.dot(values, weights, preferred_element_type=F32)
        totals[target, :, pl.ds(lower, narrow)] += total[ONES:] / total[:1]
        return carry

    lax.fori_loop(0, keypoints // narrow, step, 0)


def start_copies(pieces, rows, info_b, sems):
    keypoints = rows.shape[1] - INFO
    lists, bodies = [], []
    position = 0
    for piece in pieces:
        if len(piece.shape) == 3:
            place = slice(position, position + piece.shape[0])
            listed = piece.at[:, keypoints:, :]
            position += piece.shape[0]
        else:
            place = position
            listed = piece.at[keypoints:, :]
            position += 1
        k = len(lists)
        lists.append(pltpu.make_async_copy(listed, info_b.at[place], sems.at[0, k]))
        bodies.append(pltpu.make_async_copy(piece, rows.at[place], sems.at[1, k]))
    for copy in lists + bodies:
        copy.start()
    return lists, bodies


def to_scalars(info_v, info, info_sem):
    copy = pltpu.make_async_copy(info_v, info, info_sem)
    copy.start()
    copy.wait()


def place_of(image, members, member):
    return lax.rem(lax.rem(image, members) - member + members, members)


def shared_kernel(members, pieces_count, *refs):
    count = 2 * members
    pieces, (own_ref, other_ref, *refs) = refs[:pieces_count], refs[pieces_count:]
    rows, info_b, totals, even_weights, odd_weights, *refs = refs
    info_v, info, units, info_sem, sems = refs
    keypoints = totals.shape[2]
    column = lax.axis_index("img")
    member = lax.axis_index("grp")

    lists, bodies = start_copies(pieces, rows, info_b, sems)
    totals[...] = jnp.zeros_like(totals)
    for copy in lists:
        copy.wait()
    info_v[...] = info_b[:, :8].astype(F32).astype(jnp.int32)
    to_scalars(info_v, info, info_sem)
    side = lax.rem(column, 2)

    def slot(index, found):
        right = index >= members
        base = jnp.where(right == (side == 1), 0, members)
        owner = base + lax.rem(index, members)
        listed = column - side + right.astype(jnp.int32)

        def position(step, found):
            first = info[owner, 0, 2 + 2 * step]
            second = info[owner, 0, 3 + 2 * step]
            inside = second // members == listed
            shared = jnp.logical_or(jnp.logical_not(right), inside)

            @pl.when(shared)
            def _():
                units[0, found] = base + place_of(first, members, member)
                units[1, found] = jnp.where(inside, base, members - base) + place_of(
                    second, members, member
                )

            return found + shared.astype(jnp.int32)

        return lax.fori_loop(0, info[owner, 0, 0], position, found)

    found = lax.fori_loop(0, count, slot, jnp.int32(0))
    row = lax.rem(column - side, ROW)
    half = found // 2 + (row == ROW - 2).astype(jnp.int32) - (row == 0).astype(jnp.int32)
    half = jnp.clip(half, 0, found)
    begin = jnp.where(side == 0, 0, half)
    end = jnp.where(side == 0, half, found)
    largest = info[0, 0, 1]
    for position in range(1, count):
        largest = jnp.maximum(largest, info[position, 0, 1])
    safe = largest * largest <= int(SAFE_SCORE / SCALE)
    for copy in bodies:
        copy.wait()

    @pl.when(safe)
    def _():
        run_units(
            rows, rows, totals, units, begin, end - begin, even_weights, odd_weights,
            score_two, apply_two,
        )

    @pl.when(jnp.logical_not(safe))
    def _():
        def visit(index, carry):
            target, source = units[0, index], units[1, index]
            shifted(rows, rows, totals, target, source, keypoints)
            shifted(rows, rows, totals, source, target, keypoints)
            return carry

        lax.fori_loop(begin, end, visit, 0)

    own_ref[...] = totals[:members]
    other_ref[...] = totals[members:]


def pair_scratch(count, full):
    keypoints = full - INFO
    return [
        pltpu.VMEM((keypoints, keypoints), BF16),
        pltpu.VMEM((keypoints, keypoints), BF16),
        pltpu.VMEM((count, 8, LANES), jnp.int32),
        pltpu.SMEM((count, 8, LANES), jnp.int32),
        pltpu.SMEM((2, 8 * LANES), jnp.int32),
        pltpu.SemaphoreType.DMA,
    ]


def shared(members, pieces):
    full = pieces[0].shape[1]
    keypoints = full - INFO
    count = 2 * members
    hbm = pl.BlockSpec(memory_space=pltpu.HBM)
    vmem = pl.BlockSpec(memory_space=pltpu.VMEM)
    whole = jax.ShapeDtypeStruct((members, HEAD_DIM, keypoints), F32)
    return pl.pallas_call(
        functools.partial(shared_kernel, members, len(pieces)),
        out_shape=[whole, whole],
        in_specs=[hbm] * len(pieces),
        out_specs=[vmem, vmem],
        scratch_shapes=[
            pltpu.VMEM((count, full, LANES), BF16),
            pltpu.VMEM((count, INFO, LANES), BF16),
            pltpu.VMEM((count, HEAD_DIM, keypoints), F32),
            *pair_scratch(count, full),
            pltpu.SemaphoreType.DMA((2, len(pieces))),
        ],
        compiler_params=pltpu.CompilerParams(vmem_limit_bytes=VMEM_LIMIT),
        cost_estimate=SHORT,
        name="shared",
    )(*pieces)


def far_kernel(members, own_ref, far_ref, start_ref, out_ref, *refs):
    even_weights, odd_weights, info_v, info, units, info_sem = refs
    keypoints = out_ref.shape[2]
    column = lax.axis_index("img")
    member = lax.axis_index("grp")
    info_v[:members] = own_ref[:, keypoints : keypoints + 8].astype(F32).astype(jnp.int32)
    info_v[members:] = far_ref[:, keypoints : keypoints + 8].astype(F32).astype(jnp.int32)
    to_scalars(info_v, info, info_sem)
    out_ref[...] = start_ref[...]
    ahead = lax.rem(column, 2) == 1
    listed = jnp.where(ahead, 0, members)

    def slot(index, found):
        owner = listed + index

        def position(step, found):
            first = info[owner, 0, 2 + 2 * step]
            second = info[owner, 0, 3 + 2 * step]
            wanted = (second // members == column) != ahead

            @pl.when(wanted)
            def _():
                left = place_of(first, members, member)
                right = place_of(second, members, member)
                units[0, found] = jnp.where(ahead, left, right)
                units[1, found] = jnp.where(ahead, right, left)

            return found + wanted.astype(jnp.int32)

        return lax.fori_loop(0, info[owner, 0, 0], position, found)

    found = lax.fori_loop(0, members, slot, jnp.int32(0))
    left, right = info[0, 0, 1], info[members, 0, 1]
    for position in range(1, members):
        left = jnp.maximum(left, info[position, 0, 1])
        right = jnp.maximum(right, info[members + position, 0, 1])
    safe = jnp.logical_and(
        jnp.maximum(left, right) < int(NORM_CAP), left * right <= int(SAFE_SCORE / SCALE)
    )

    @pl.when(safe)
    def _():
        run_units(
            own_ref, far_ref, out_ref, units, jnp.int32(0), found, even_weights, odd_weights,
            score_one, apply_one,
        )

    @pl.when(jnp.logical_not(safe))
    def _():
        def visit(index, carry):
            shifted(own_ref, far_ref, out_ref, units[0, index], units[1, index], keypoints)
            return carry

        lax.fori_loop(0, found, visit, 0)


def far_pairs(members, own, far, totals):
    full = own.shape[1]
    vmem = pl.BlockSpec(memory_space=pltpu.VMEM)
    return pl.pallas_call(
        functools.partial(far_kernel, members),
        out_shape=jax.ShapeDtypeStruct(totals.shape, F32),
        in_specs=[vmem] * 3,
        out_specs=vmem,
        scratch_shapes=pair_scratch(2 * members, full),
        compiler_params=pltpu.CompilerParams(vmem_limit_bytes=VMEM_LIMIT),
        cost_estimate=LONG,
        name="far_pairs",
    )(own, far, totals)


def merge_kernel(totals_ref, partial_ref, *outs):
    for slot, out_ref in enumerate(outs):
        out_ref[...] = (totals_ref[slot] + partial_ref[slot]).astype(BF16)


def merge(members, totals, partial):
    vmem = pl.BlockSpec(memory_space=pltpu.VMEM)
    message = jax.ShapeDtypeStruct(totals.shape[1:], BF16)
    return pl.pallas_call(
        merge_kernel,
        out_shape=[message] * members,
        in_specs=[vmem, vmem],
        out_specs=[vmem] * members,
        compiler_params=pltpu.CompilerParams(vmem_limit_bytes=VMEM_LIMIT),
        name="merge",
    )(totals, partial)


def update_kernel(members, desc_ref, w_ref, *refs):
    pieces = refs[:members]
    out_ref = refs[members]
    member = lax.axis_index("grp")
    weights = []
    for distance in range(members):
        head = lax.rem(member - distance + members, members)
        weights.append(w_ref[pl.ds(pl.multiple_of(head * HEAD_DIM, HEAD_DIM), HEAD_DIM), :])
    message = jnp.concatenate([piece[...] for piece in pieces], 0)
    update = lax.dot_general(
        message, jnp.concatenate(weights, 0), TN, preferred_element_type=F32
    )
    out_ref[0] = (desc_ref[0].astype(F32) + update).astype(BF16)


def update(members, desc, w_out, pieces):
    vmem = pl.BlockSpec(memory_space=pltpu.VMEM)
    return pl.pallas_call(
        functools.partial(update_kernel, members),
        out_shape=jax.ShapeDtypeStruct(desc.shape, BF16),
        in_specs=[vmem] * (2 + members),
        out_specs=vmem,
        compiler_params=pltpu.CompilerParams(vmem_limit_bytes=VMEM_LIMIT),
        name="update",
    )(desc, w_out, *pieces)


def on_device(desc, w_proj, w_out, pair_list, pair_count):
    columns = lax.axis_size("img")
    members = lax.axis_size("grp")

    def from_ahead(block, distance):
        route = [((i + distance) % members, i) for i in range(members)]
        return lax.ppermute(block, "grp", route)

    def swap(block, offset):
        pairs = []
        for i in range(offset, columns + offset, 2):
            low, high = i % columns, (i + 1) % columns
            pairs += [(low, high), (high, low)]
        return lax.ppermute(block, "img", pairs)

    sent = project(members, pair_list, pair_count, desc, w_proj)
    own = [sent[0]] + [from_ahead(sent[k], k) for k in range(1, members)]
    near = [swap(block, 0) for block in own]
    gathered, *near = lax.optimization_barrier([jnp.stack(own)] + near)
    far = swap(gathered, 1)
    totals, other = shared(members, [gathered] + near)
    partial = swap(other, 0)
    totals = far_pairs(members, gathered, far, totals)
    messages = merge(members, totals, partial)
    back = [messages[0]]
    for distance in range(1, members):
        back.append(from_ahead(messages[distance], members - distance))
    return update(members, desc, w_out, back)


def solution(mesh):
    return jax.shard_map(
        on_device,
        mesh=mesh,
        in_specs=(
            P(("img", "grp"), None, None),
            P(),
            P(),
            P(("img", "grp"), None),
            P(("img", "grp")),
        ),
        out_specs=P(("img", "grp"), None, None),
        check_vma=False,
    )
```

```python
import functools
import math

import jax
import jax.numpy as jnp
from jax import lax
from jax.experimental import pallas as pl
from jax.experimental.pallas import tpu as pltpu
from jax.sharding import PartitionSpec as P

D = 256
HEADS = 4
HEAD_DIM = 64
LANES = 128
ONES = 16
INFO = 16
CHUNKS = 4
SCALE = HEAD_DIM ** -0.5
LOG2E = math.log2(math.e)
SAFE_SCORE = 64.0
NORM_CAP = 250.0
BF16 = jnp.bfloat16
F32 = jnp.float32
NT = (((1,), (1,)), ((), ()))
TN = (((0,), (0,)), ((), ()))
VMEM_LIMIT = 28 * 1024 * 1024
ROW = 16
SHORT = pl.CostEstimate(flops=10**4, bytes_accessed=10**4, transcendentals=0)
LONG = pl.CostEstimate(flops=10**10, bytes_accessed=10**7, transcendentals=0)


def project_kernel(members, count_ref, list_hbm, desc_hbm, w_hbm, *refs):
    outs = refs[:members]
    list_ref, desc_ref, w_ref, held, sems, out_sems = refs[members:]
    keypoints = desc_ref.shape[0]
    cap = list_ref.shape[1]
    chunk = keypoints // CHUNKS
    fetches = [
        pltpu.make_async_copy(w_hbm, w_ref, sems.at[0]),
        pltpu.make_async_copy(list_hbm, list_ref, sems.at[1]),
    ]
    for c in range(CHUNKS):
        fetches.append(
            pltpu.make_async_copy(
                desc_hbm.at[0, c * chunk : (c + 1) * chunk],
                desc_ref.at[c * chunk : (c + 1) * chunk],
                sems.at[2 + c],
            )
        )
    for copy in fetches:
        copy.start()
    member = lax.axis_index("grp")
    fetches[1].wait()
    lane = lax.broadcasted_iota(jnp.int32, (INFO, LANES), 1)
    common = jnp.where(lane == 0, count_ref[0], 0)
    for slot in range(cap):
        first = jnp.broadcast_to(list_ref[0:1, slot : slot + 1], lane.shape)
        second = jnp.broadcast_to(list_ref[1:2, slot : slot + 1], lane.shape)
        common = jnp.where(lane == 2 + 2 * slot, first, common)
        common = jnp.where(lane == 3 + 2 * slot, second, common)
    common = common.astype(F32)
    fetches[0].wait()
    turned = w_ref[...].T
    written = []

    def send(lower, size, k):
        for distance in range(members):
            head = lax.rem(member - distance + members, members)
            copy = pltpu.make_async_copy(
                held.at[head, lower : lower + size],
                outs[distance].at[lower : lower + size],
                out_sems.at[k, distance],
            )
            copy.start()
            written.append(copy)

    norms = [None] * members
    for c in range(CHUNKS):
        fetches[2 + c].wait()
        lower = c * chunk
        both = lax.dot_general(
            turned, desc_ref[lower : lower + chunk, :], NT, preferred_element_type=F32
        ).astype(BF16)
        for head in range(members):
            query = both[head * HEAD_DIM : (head + 1) * HEAD_DIM]
            value = both[D + head * HEAD_DIM : D + (head + 1) * HEAD_DIM]
            for block in range(0, chunk, LANES):
                row = lower + block
                held[head, row : row + HEAD_DIM, :] = query[:, block : block + LANES]
                held[head, row + HEAD_DIM : row + LANES, :] = value[:, block : block + LANES]
            query = query.astype(F32)
            squares = jnp.sum(query * query, axis=0, keepdims=True)
            norms[head] = squares if c == 0 else jnp.maximum(norms[head], squares)
        send(lower, chunk, c)
    for head in range(members):
        norm = jnp.sqrt(jnp.max(norms[head], axis=1, keepdims=True)) * 1.001
        norm = jnp.ceil(jnp.minimum(norm, NORM_CAP))
        info = jnp.where(lane == 1, jnp.broadcast_to(norm, lane.shape), common)
        held[head, keypoints:, :] = info.astype(BF16)
    send(keypoints, INFO, CHUNKS)
    for copy in written:
        copy.wait()


def project(members, pair_list, pair_count, desc, w_proj):
    keypoints = desc.shape[1]
    hbm = pl.BlockSpec(memory_space=pltpu.HBM)
    out = jax.ShapeDtypeStruct((keypoints + INFO, LANES), BF16)
    listed = pair_list.T
    return pl.pallas_call(
        functools.partial(project_kernel, members),
        out_shape=[out] * members,
        in_specs=[pl.BlockSpec(memory_space=pltpu.SMEM), hbm, hbm, hbm],
        out_specs=[pl.BlockSpec(memory_space=pltpu.VMEM)] * members,
        scratch_shapes=[
            pltpu.VMEM(listed.shape, jnp.int32),
            pltpu.VMEM(desc.shape[1:], BF16),
            pltpu.VMEM(w_proj.shape, BF16),
            pltpu.VMEM((members, *out.shape), BF16),
            pltpu.SemaphoreType.DMA((2 + CHUNKS,)),
            pltpu.SemaphoreType.DMA((CHUNKS + 1, members)),
        ],
        compiler_params=pltpu.CompilerParams(vmem_limit_bytes=VMEM_LIMIT),
        name="project",
    )(pair_count, *[pltpu.with_memory_space_constraint(x, pltpu.HBM) for x in (listed, desc, w_proj)])


def query_of(rows, image, lower, size):
    parts = [
        rows[image, block : block + HEAD_DIM, :] for block in range(lower, lower + size, LANES)
    ]
    return jnp.concatenate(parts, 1)


def value_of(rows, image, lower, size):
    parts = [
        rows[image, block + HEAD_DIM : block + LANES, :]
        for block in range(lower, lower + size, LANES)
    ]
    return jnp.concatenate([jnp.ones((ONES, size), BF16), jnp.concatenate(parts, 1)], 0)


def score_one(rows, others, target, source, weights, block):
    keypoints = weights.shape[0]
    query = query_of(rows, target, 0, keypoints)
    for lower in range(0, keypoints, block):
        keys = query_of(others, source, lower, block)
        scores = lax.dot_general(keys, query, TN, preferred_element_type=F32)
        weights[lower : lower + block, :] = jnp.exp2(scores * (SCALE * LOG2E)).astype(BF16)


def apply_one(rows, others, totals, target, source, weights):
    values = value_of(others, source, 0, weights.shape[0])
    total = jnp.dot(values, weights[...], preferred_element_type=F32)
    totals[target] += total[ONES:] / total[:1]


def score_two(rows, others, target, source, weights, block):
    score_one(others, rows, source, target, weights, block)


def apply_two(rows, others, totals, target, source, weights):
    values = value_of(others, source, 0, weights.shape[0])
    total = lax.dot_general(values, weights[...], NT, preferred_element_type=F32)
    totals[target] += total[ONES:] / total[:1]
    apply_one(others, rows, totals, source, target, weights)


def run_units(rows, others, totals, units, begin, count, even_weights, odd_weights, score, apply):
    block = even_weights.shape[0] // 2

    def scored(index, weights):
        score(rows, others, units[0, index], units[1, index], weights, block)

    def applied(index, weights):
        apply(rows, others, totals, units[0, index], units[1, index], weights)

    @pl.when(count > 0)
    def _():
        scored(begin, even_weights)

        def step(index, carry):
            now = begin + 2 * index
            scored(now + 1, odd_weights)
            applied(now, even_weights)
            scored(now + 2, even_weights)
            applied(now + 1, odd_weights)
            return carry

        lax.fori_loop(0, (count - 1) // 2, step, 0)
        last = begin + count - 1

        @pl.when(lax.rem(count, 2) == 0)
        def _():
            scored(last, odd_weights)
            applied(last - 1, even_weights)
            applied(last, odd_weights)

        @pl.when(lax.rem(count, 2) == 1)
        def _():
            applied(last, even_weights)


def shifted(rows, others, totals, target, source, keypoints):
    narrow = 2 * LANES
    keys = query_of(others, source, 0, keypoints)
    values = value_of(others, source, 0, keypoints)

    def step(index, carry):
        lower = pl.multiple_of(index * narrow, narrow)
        parts = [
            rows[target, pl.ds(pl.multiple_of(lower + offset, LANES), HEAD_DIM), :]
            for offset in range(0, narrow, LANES)
        ]
        query = jnp.concatenate(parts, 1)
        scores = lax.dot_general(keys, query, TN, preferred_element_type=F32) * SCALE
        weights = jnp.exp(scores - jnp.max(scores, axis=0, keepdims=True)).astype(BF16)
        total = jnp.dot(values, weights, preferred_element_type=F32)
        totals[target, :, pl.ds(lower, narrow)] += total[ONES:] / total[:1]
        return carry

    lax.fori_loop(0, keypoints // narrow, step, 0)


def start_copies(pieces, rows, info_b, sems):
    keypoints = rows.shape[1] - INFO
    lists, bodies = [], []
    position = 0
    for piece in pieces:
        if len(piece.shape) == 3:
            place = slice(position, position + piece.shape[0])
            listed = piece.at[:, keypoints:, :]
            position += piece.shape[0]
        else:
            place = position
            listed = piece.at[keypoints:, :]
            position += 1
        k = len(lists)
        lists.append(pltpu.make_async_copy(listed, info_b.at[place], sems.at[0, k]))
        bodies.append(pltpu.make_async_copy(piece, rows.at[place], sems.at[1, k]))
    for copy in lists + bodies:
        copy.start()
    return lists, bodies


def to_scalars(info_v, info, info_sem):
    copy = pltpu.make_async_copy(info_v, info, info_sem)
    copy.start()
    copy.wait()


def place_of(image, members, member):
    return lax.rem(lax.rem(image, members) - member + members, members)


def shared_kernel(members, pieces_count, *refs):
    count = 2 * members
    pieces, (own_ref, other_ref, *refs) = refs[:pieces_count], refs[pieces_count:]
    rows, info_b, totals, even_weights, odd_weights, *refs = refs
    info_v, info, units, info_sem, sems = refs
    keypoints = totals.shape[2]
    column = lax.axis_index("img")
    member = lax.axis_index("grp")

    lists, bodies = start_copies(pieces, rows, info_b, sems)
    totals[...] = jnp.zeros_like(totals)
    for copy in lists:
        copy.wait()
    info_v[...] = info_b[:, :8].astype(F32).astype(jnp.int32)
    to_scalars(info_v, info, info_sem)
    side = lax.rem(column, 2)

    def slot(index, found):
        right = index >= members
        base = jnp.where(right == (side == 1), 0, members)
        owner = base + lax.rem(index, members)
        listed = column - side + right.astype(jnp.int32)

        def position(step, found):
            first = info[owner, 0, 2 + 2 * step]
            second = info[owner, 0, 3 + 2 * step]
            inside = second // members == listed
            shared = jnp.logical_or(jnp.logical_not(right), inside)

            @pl.when(shared)
            def _():
                units[0, found] = base + place_of(first, members, member)
                units[1, found] = jnp.where(inside, base, members - base) + place_of(
                    second, members, member
                )

            return found + shared.astype(jnp.int32)

        return lax.fori_loop(0, info[owner, 0, 0], position, found)

    found = lax.fori_loop(0, count, slot, jnp.int32(0))
    row = lax.rem(column - side, ROW)
    half = found // 2 + (row == ROW - 2).astype(jnp.int32) - (row == 0).astype(jnp.int32)
    half = jnp.clip(half, 0, found)
    begin = jnp.where(side == 0, 0, half)
    end = jnp.where(side == 0, half, found)
    largest = info[0, 0, 1]
    for position in range(1, count):
        largest = jnp.maximum(largest, info[position, 0, 1])
    safe = largest * largest <= int(SAFE_SCORE / SCALE)
    for copy in bodies:
        copy.wait()

    @pl.when(safe)
    def _():
        run_units(
            rows, rows, totals, units, begin, end - begin, even_weights, odd_weights,
            score_two, apply_two,
        )

    @pl.when(jnp.logical_not(safe))
    def _():
        def visit(index, carry):
            target, source = units[0, index], units[1, index]
            shifted(rows, rows, totals, target, source, keypoints)
            shifted(rows, rows, totals, source, target, keypoints)
            return carry

        lax.fori_loop(begin, end, visit, 0)

    own_ref[...] = totals[:members]
    other_ref[...] = totals[members:]


def pair_scratch(count, full):
    keypoints = full - INFO
    return [
        pltpu.VMEM((keypoints, keypoints), BF16),
        pltpu.VMEM((keypoints, keypoints), BF16),
        pltpu.VMEM((count, 8, LANES), jnp.int32),
        pltpu.SMEM((count, 8, LANES), jnp.int32),
        pltpu.SMEM((2, 8 * LANES), jnp.int32),
        pltpu.SemaphoreType.DMA,
    ]


def shared(members, pieces):
    full = pieces[0].shape[1]
    keypoints = full - INFO
    count = 2 * members
    hbm = pl.BlockSpec(memory_space=pltpu.HBM)
    vmem = pl.BlockSpec(memory_space=pltpu.VMEM)
    whole = jax.ShapeDtypeStruct((members, HEAD_DIM, keypoints), F32)
    return pl.pallas_call(
        functools.partial(shared_kernel, members, len(pieces)),
        out_shape=[whole, whole],
        in_specs=[hbm] * len(pieces),
        out_specs=[vmem, vmem],
        scratch_shapes=[
            pltpu.VMEM((count, full, LANES), BF16),
            pltpu.VMEM((count, INFO, LANES), BF16),
            pltpu.VMEM((count, HEAD_DIM, keypoints), F32),
            *pair_scratch(count, full),
            pltpu.SemaphoreType.DMA((2, len(pieces))),
        ],
        compiler_params=pltpu.CompilerParams(vmem_limit_bytes=VMEM_LIMIT),
        cost_estimate=SHORT,
        name="shared",
    )(*pieces)


def far_kernel(members, own_ref, far_ref, start_ref, out_ref, *refs):
    even_weights, odd_weights, info_v, info, units, info_sem = refs
    keypoints = out_ref.shape[2]
    column = lax.axis_index("img")
    member = lax.axis_index("grp")
    info_v[:members] = own_ref[:, keypoints : keypoints + 8].astype(F32).astype(jnp.int32)
    info_v[members:] = far_ref[:, keypoints : keypoints + 8].astype(F32).astype(jnp.int32)
    to_scalars(info_v, info, info_sem)
    out_ref[...] = start_ref[...]
    ahead = lax.rem(column, 2) == 1
    listed = jnp.where(ahead, 0, members)

    def slot(index, found):
        owner = listed + index

        def position(step, found):
            first = info[owner, 0, 2 + 2 * step]
            second = info[owner, 0, 3 + 2 * step]
            wanted = (second // members == column) != ahead

            @pl.when(wanted)
            def _():
                left = place_of(first, members, member)
                right = place_of(second, members, member)
                units[0, found] = jnp.where(ahead, left, right)
                units[1, found] = jnp.where(ahead, right, left)

            return found + wanted.astype(jnp.int32)

        return lax.fori_loop(0, info[owner, 0, 0], position, found)

    found = lax.fori_loop(0, members, slot, jnp.int32(0))
    left, right = info[0, 0, 1], info[members, 0, 1]
    for position in range(1, members):
        left = jnp.maximum(left, info[position, 0, 1])
        right = jnp.maximum(right, info[members + position, 0, 1])
    safe = jnp.logical_and(
        jnp.maximum(left, right) < int(NORM_CAP), left * right <= int(SAFE_SCORE / SCALE)
    )

    @pl.when(safe)
    def _():
        run_units(
            own_ref, far_ref, out_ref, units, jnp.int32(0), found, even_weights, odd_weights,
            score_one, apply_one,
        )

    @pl.when(jnp.logical_not(safe))
    def _():
        def visit(index, carry):
            shifted(own_ref, far_ref, out_ref, units[0, index], units[1, index], keypoints)
            return carry

        lax.fori_loop(0, found, visit, 0)


def far_pairs(members, own, far, totals):
    full = own.shape[1]
    vmem = pl.BlockSpec(memory_space=pltpu.VMEM)
    return pl.pallas_call(
        functools.partial(far_kernel, members),
        out_shape=jax.ShapeDtypeStruct(totals.shape, F32),
        in_specs=[vmem] * 3,
        out_specs=vmem,
        scratch_shapes=pair_scratch(2 * members, full),
        compiler_params=pltpu.CompilerParams(vmem_limit_bytes=VMEM_LIMIT),
        cost_estimate=LONG,
        name="far_pairs",
    )(own, far, totals)


def merge_kernel(totals_ref, partial_ref, *outs):
    for slot, out_ref in enumerate(outs):
        out_ref[...] = (totals_ref[slot] + partial_ref[slot]).astype(BF16)


def merge(members, totals, partial):
    vmem = pl.BlockSpec(memory_space=pltpu.VMEM)
    message = jax.ShapeDtypeStruct(totals.shape[1:], BF16)
    return pl.pallas_call(
        merge_kernel,
        out_shape=[message] * members,
        in_specs=[vmem, vmem],
        out_specs=[vmem] * members,
        compiler_params=pltpu.CompilerParams(vmem_limit_bytes=VMEM_LIMIT),
        name="merge",
    )(totals, partial)


def update_kernel(members, desc_ref, w_ref, *refs):
    pieces = refs[:members]
    out_ref = refs[members]
    member = lax.axis_index("grp")
    weights = []
    for distance in range(members):
        head = lax.rem(member - distance + members, members)
        weights.append(w_ref[pl.ds(pl.multiple_of(head * HEAD_DIM, HEAD_DIM), HEAD_DIM), :])
    message = jnp.concatenate([piece[...] for piece in pieces], 0)
    update = lax.dot_general(
        message, jnp.concatenate(weights, 0), TN, preferred_element_type=F32
    )
    out_ref[0] = (desc_ref[0].astype(F32) + update).astype(BF16)


def update(members, desc, w_out, pieces):
    vmem = pl.BlockSpec(memory_space=pltpu.VMEM)
    return pl.pallas_call(
        functools.partial(update_kernel, members),
        out_shape=jax.ShapeDtypeStruct(desc.shape, BF16),
        in_specs=[vmem] * (2 + members),
        out_specs=vmem,
        compiler_params=pltpu.CompilerParams(vmem_limit_bytes=VMEM_LIMIT),
        name="update",
    )(desc, w_out, *pieces)


def on_device(desc, w_proj, w_out, pair_list, pair_count):
    columns = lax.axis_size("img")
    members = lax.axis_size("grp")

    def from_ahead(block, distance):
        route = [((i + distance) % members, i) for i in range(members)]
        return lax.ppermute(block, "grp", route)

    def swap(block, offset):
        pairs = []
        for i in range(offset, columns + offset, 2):
            low, high = i % columns, (i + 1) % columns
            pairs += [(low, high), (high, low)]
        return lax.ppermute(block, "img", pairs)

    sent = project(members, pair_list, pair_count, desc, w_proj)
    own = [sent[0]] + [from_ahead(sent[k], k) for k in range(1, members)]
    near = [swap(block, 0) for block in own]
    gathered, *near = lax.optimization_barrier([jnp.stack(own)] + near)
    far = swap(gathered, 1)
    totals, other = shared(members, [gathered] + near)
    partial = swap(other, 0)
    totals = far_pairs(members, gathered, far, totals)
    messages = merge(members, totals, partial)
    back = [messages[0]]
    for distance in range(1, members):
        back.append(from_ahead(messages[distance], members - distance))
    return update(members, desc, w_out, back)


def solution(mesh):
    return jax.shard_map(
        on_device,
        mesh=mesh,
        in_specs=(
            P(("img", "grp"), None, None),
            P(),
            P(),
            P(("img", "grp"), None),
            P(("img", "grp")),
        ),
        out_specs=P(("img", "grp"), None, None),
        check_vma=False,
    )
```

```python
import functools
import math

import jax
import jax.numpy as jnp
from jax import lax
from jax.experimental import pallas as pl
from jax.experimental.pallas import tpu as pltpu
from jax.sharding import PartitionSpec as P

D = 256
HEADS = 4
HEAD_DIM = 64
LANES = 128
ONES = 16
INFO = 16
SCALE = HEAD_DIM ** -0.5
LOG2E = math.log2(math.e)
SAFE_SCORE = 64.0
NORM_CAP = 250.0
BF16 = jnp.bfloat16
F32 = jnp.float32
NT = (((1,), (1,)), ((), ()))
TN = (((0,), (0,)), ((), ()))
VMEM_LIMIT = 28 * 1024 * 1024
ROW = 16
SHORT = pl.CostEstimate(flops=10**4, bytes_accessed=10**4, transcendentals=0)
LONG = pl.CostEstimate(flops=10**10, bytes_accessed=10**7, transcendentals=0)


def project_kernel(members, count_ref, list_hbm, desc_hbm, w_hbm, *refs):
    outs = refs[:members]
    turned, list_ref, desc_ref, w_ref, sems = refs[members:]
    copies = [
        pltpu.make_async_copy(source, target, sems.at[k])
        for k, (source, target) in enumerate(
            ((w_hbm, w_ref), (desc_hbm, desc_ref), (list_hbm, list_ref))
        )
    ]
    for copy in copies:
        copy.start()
    keypoints = desc_ref.shape[1]
    cap = list_ref.shape[1]
    member = lax.axis_index("grp")
    copies[0].wait()
    turned[...] = w_ref[...].T
    copies[2].wait()
    lane = lax.broadcasted_iota(jnp.int32, (INFO, LANES), 1)
    common = jnp.where(lane == 0, count_ref[0], 0)
    for slot in range(cap):
        first = jnp.broadcast_to(list_ref[0:1, slot : slot + 1], lane.shape)
        second = jnp.broadcast_to(list_ref[1:2, slot : slot + 1], lane.shape)
        common = jnp.where(lane == 2 + 2 * slot, first, common)
        common = jnp.where(lane == 3 + 2 * slot, second, common)
    common = common.astype(F32)
    copies[1].wait()
    desc = desc_ref[0]
    for distance in range(members):
        head = lax.rem(member - distance + members, members)
        lower = pl.multiple_of(head * HEAD_DIM, HEAD_DIM)
        weights = jnp.concatenate(
            [turned[pl.ds(lower, HEAD_DIM), :], turned[pl.ds(D + lower, HEAD_DIM), :]], 0
        )
        both = lax.dot_general(weights, desc, NT, preferred_element_type=F32).astype(BF16)
        for block in range(keypoints // LANES):
            outs[distance][block * LANES : (block + 1) * LANES, :] = both[
                :, block * LANES : (block + 1) * LANES
            ]
        query = both[:HEAD_DIM].astype(F32)
        squares = jnp.sum(query * query, axis=0, keepdims=True)
        norm = jnp.sqrt(jnp.max(squares, axis=1, keepdims=True)) * 1.001
        norm = jnp.ceil(jnp.minimum(norm, NORM_CAP))
        info = jnp.where(lane == 1, jnp.broadcast_to(norm, lane.shape), common)
        outs[distance][keypoints:, :] = info.astype(BF16)


def project(members, pair_list, pair_count, desc, w_proj):
    keypoints = desc.shape[1]
    hbm = pl.BlockSpec(memory_space=pltpu.HBM)
    out = jax.ShapeDtypeStruct((keypoints + INFO, LANES), BF16)
    listed = pair_list.T
    return pl.pallas_call(
        functools.partial(project_kernel, members),
        out_shape=[out] * members,
        in_specs=[pl.BlockSpec(memory_space=pltpu.SMEM), hbm, hbm, hbm],
        out_specs=[pl.BlockSpec(memory_space=pltpu.VMEM)] * members,
        scratch_shapes=[
            pltpu.VMEM((2 * D, D), BF16),
            pltpu.VMEM(listed.shape, jnp.int32),
            pltpu.VMEM(desc.shape, BF16),
            pltpu.VMEM(w_proj.shape, BF16),
            pltpu.SemaphoreType.DMA((3,)),
        ],
        compiler_params=pltpu.CompilerParams(vmem_limit_bytes=VMEM_LIMIT),
        name="project",
    )(pair_count, *[pltpu.with_memory_space_constraint(x, pltpu.HBM) for x in (listed, desc, w_proj)])


def query_of(rows, image, lower, size):
    parts = [
        rows[image, block : block + HEAD_DIM, :] for block in range(lower, lower + size, LANES)
    ]
    return jnp.concatenate(parts, 1)


def value_of(rows, image, lower, size):
    parts = [
        rows[image, block + HEAD_DIM : block + LANES, :]
        for block in range(lower, lower + size, LANES)
    ]
    return jnp.concatenate([jnp.ones((ONES, size), BF16), jnp.concatenate(parts, 1)], 0)


def score_one(rows, others, target, source, weights, block):
    keypoints = weights.shape[0]
    query = query_of(rows, target, 0, keypoints)
    for lower in range(0, keypoints, block):
        keys = query_of(others, source, lower, block)
        scores = lax.dot_general(keys, query, TN, preferred_element_type=F32)
        weights[lower : lower + block, :] = jnp.exp2(scores * (SCALE * LOG2E)).astype(BF16)


def apply_one(rows, others, totals, target, source, weights):
    values = value_of(others, source, 0, weights.shape[0])
    total = jnp.dot(values, weights[...], preferred_element_type=F32)
    totals[target] += total[ONES:] / total[:1]


def score_two(rows, others, target, source, weights, block):
    score_one(others, rows, source, target, weights, block)


def apply_two(rows, others, totals, target, source, weights):
    values = value_of(others, source, 0, weights.shape[0])
    total = lax.dot_general(values, weights[...], NT, preferred_element_type=F32)
    totals[target] += total[ONES:] / total[:1]
    apply_one(others, rows, totals, source, target, weights)


def run_units(rows, others, totals, units, begin, count, even_weights, odd_weights, score, apply):
    block = even_weights.shape[0] // 2

    def scored(index, weights):
        score(rows, others, units[0, index], units[1, index], weights, block)

    def applied(index, weights):
        apply(rows, others, totals, units[0, index], units[1, index], weights)

    @pl.when(count > 0)
    def _():
        scored(begin, even_weights)

        def step(index, carry):
            now = begin + 2 * index
            scored(now + 1, odd_weights)
            applied(now, even_weights)
            scored(now + 2, even_weights)
            applied(now + 1, odd_weights)
            return carry

        lax.fori_loop(0, (count - 1) // 2, step, 0)
        last = begin + count - 1

        @pl.when(lax.rem(count, 2) == 0)
        def _():
            scored(last, odd_weights)
            applied(last - 1, even_weights)
            applied(last, odd_weights)

        @pl.when(lax.rem(count, 2) == 1)
        def _():
            applied(last, even_weights)


def shifted(rows, others, totals, target, source, keypoints):
    narrow = 2 * LANES
    keys = query_of(others, source, 0, keypoints)
    values = value_of(others, source, 0, keypoints)

    def step(index, carry):
        lower = pl.multiple_of(index * narrow, narrow)
        parts = [
            rows[target, pl.ds(pl.multiple_of(lower + offset, LANES), HEAD_DIM), :]
            for offset in range(0, narrow, LANES)
        ]
        query = jnp.concatenate(parts, 1)
        scores = lax.dot_general(keys, query, TN, preferred_element_type=F32) * SCALE
        weights = jnp.exp(scores - jnp.max(scores, axis=0, keepdims=True)).astype(BF16)
        total = jnp.dot(values, weights, preferred_element_type=F32)
        totals[target, :, pl.ds(lower, narrow)] += total[ONES:] / total[:1]
        return carry

    lax.fori_loop(0, keypoints // narrow, step, 0)


def start_copies(pieces, rows, info_b, sems):
    keypoints = rows.shape[1] - INFO
    lists, bodies = [], []
    position = 0
    for piece in pieces:
        if len(piece.shape) == 3:
            place = slice(position, position + piece.shape[0])
            listed = piece.at[:, keypoints:, :]
            position += piece.shape[0]
        else:
            place = position
            listed = piece.at[keypoints:, :]
            position += 1
        k = len(lists)
        lists.append(pltpu.make_async_copy(listed, info_b.at[place], sems.at[0, k]))
        bodies.append(pltpu.make_async_copy(piece, rows.at[place], sems.at[1, k]))
    for copy in lists + bodies:
        copy.start()
    return lists, bodies


def to_scalars(info_v, info, info_sem):
    copy = pltpu.make_async_copy(info_v, info, info_sem)
    copy.start()
    copy.wait()


def place_of(image, members, member):
    return lax.rem(lax.rem(image, members) - member + members, members)


def shared_kernel(members, pieces_count, *refs):
    count = 2 * members
    pieces, (own_ref, other_ref, *refs) = refs[:pieces_count], refs[pieces_count:]
    rows, info_b, totals, even_weights, odd_weights, *refs = refs
    info_v, info, units, info_sem, sems = refs
    keypoints = totals.shape[2]
    column = lax.axis_index("img")
    member = lax.axis_index("grp")

    lists, bodies = start_copies(pieces, rows, info_b, sems)
    totals[...] = jnp.zeros_like(totals)
    for copy in lists:
        copy.wait()
    info_v[...] = info_b[:, :8].astype(F32).astype(jnp.int32)
    to_scalars(info_v, info, info_sem)
    side = lax.rem(column, 2)

    def slot(index, found):
        right = index >= members
        base = jnp.where(right == (side == 1), 0, members)
        owner = base + lax.rem(index, members)
        listed = column - side + right.astype(jnp.int32)

        def position(step, found):
            first = info[owner, 0, 2 + 2 * step]
            second = info[owner, 0, 3 + 2 * step]
            inside = second // members == listed
            shared = jnp.logical_or(jnp.logical_not(right), inside)

            @pl.when(shared)
            def _():
                units[0, found] = base + place_of(first, members, member)
                units[1, found] = jnp.where(inside, base, members - base) + place_of(
                    second, members, member
                )

            return found + shared.astype(jnp.int32)

        return lax.fori_loop(0, info[owner, 0, 0], position, found)

    found = lax.fori_loop(0, count, slot, jnp.int32(0))
    row = lax.rem(column - side, ROW)
    half = found // 2 + (row == ROW - 2).astype(jnp.int32) - (row == 0).astype(jnp.int32)
    half = jnp.clip(half, 0, found)
    begin = jnp.where(side == 0, 0, half)
    end = jnp.where(side == 0, half, found)
    largest = info[0, 0, 1]
    for position in range(1, count):
        largest = jnp.maximum(largest, info[position, 0, 1])
    safe = largest * largest <= int(SAFE_SCORE / SCALE)
    for copy in bodies:
        copy.wait()

    @pl.when(safe)
    def _():
        run_units(
            rows, rows, totals, units, begin, end - begin, even_weights, odd_weights,
            score_two, apply_two,
        )

    @pl.when(jnp.logical_not(safe))
    def _():
        def visit(index, carry):
            target, source = units[0, index], units[1, index]
            shifted(rows, rows, totals, target, source, keypoints)
            shifted(rows, rows, totals, source, target, keypoints)
            return carry

        lax.fori_loop(begin, end, visit, 0)

    own_ref[...] = totals[:members]
    other_ref[...] = totals[members:]


def pair_scratch(count, full):
    keypoints = full - INFO
    return [
        pltpu.VMEM((keypoints, keypoints), BF16),
        pltpu.VMEM((keypoints, keypoints), BF16),
        pltpu.VMEM((count, 8, LANES), jnp.int32),
        pltpu.SMEM((count, 8, LANES), jnp.int32),
        pltpu.SMEM((2, 8 * LANES), jnp.int32),
        pltpu.SemaphoreType.DMA,
    ]


def shared(members, pieces):
    full = pieces[0].shape[1]
    keypoints = full - INFO
    count = 2 * members
    hbm = pl.BlockSpec(memory_space=pltpu.HBM)
    vmem = pl.BlockSpec(memory_space=pltpu.VMEM)
    whole = jax.ShapeDtypeStruct((members, HEAD_DIM, keypoints), F32)
    return pl.pallas_call(
        functools.partial(shared_kernel, members, len(pieces)),
        out_shape=[whole, whole],
        in_specs=[hbm] * len(pieces),
        out_specs=[vmem, vmem],
        scratch_shapes=[
            pltpu.VMEM((count, full, LANES), BF16),
            pltpu.VMEM((count, INFO, LANES), BF16),
            pltpu.VMEM((count, HEAD_DIM, keypoints), F32),
            *pair_scratch(count, full),
            pltpu.SemaphoreType.DMA((2, len(pieces))),
        ],
        compiler_params=pltpu.CompilerParams(vmem_limit_bytes=VMEM_LIMIT),
        cost_estimate=SHORT,
        name="shared",
    )(*pieces)


def far_kernel(members, own_ref, far_ref, start_ref, out_ref, *refs):
    even_weights, odd_weights, info_v, info, units, info_sem = refs
    keypoints = out_ref.shape[2]
    column = lax.axis_index("img")
    member = lax.axis_index("grp")
    info_v[:members] = own_ref[:, keypoints : keypoints + 8].astype(F32).astype(jnp.int32)
    info_v[members:] = far_ref[:, keypoints : keypoints + 8].astype(F32).astype(jnp.int32)
    to_scalars(info_v, info, info_sem)
    out_ref[...] = start_ref[...]
    ahead = lax.rem(column, 2) == 1
    listed = jnp.where(ahead, 0, members)

    def slot(index, found):
        owner = listed + index

        def position(step, found):
            first = info[owner, 0, 2 + 2 * step]
            second = info[owner, 0, 3 + 2 * step]
            wanted = (second // members == column) != ahead

            @pl.when(wanted)
            def _():
                left = place_of(first, members, member)
                right = place_of(second, members, member)
                units[0, found] = jnp.where(ahead, left, right)
                units[1, found] = jnp.where(ahead, right, left)

            return found + wanted.astype(jnp.int32)

        return lax.fori_loop(0, info[owner, 0, 0], position, found)

    found = lax.fori_loop(0, members, slot, jnp.int32(0))
    left, right = info[0, 0, 1], info[members, 0, 1]
    for position in range(1, members):
        left = jnp.maximum(left, info[position, 0, 1])
        right = jnp.maximum(right, info[members + position, 0, 1])
    safe = jnp.logical_and(
        jnp.maximum(left, right) < int(NORM_CAP), left * right <= int(SAFE_SCORE / SCALE)
    )

    @pl.when(safe)
    def _():
        run_units(
            own_ref, far_ref, out_ref, units, jnp.int32(0), found, even_weights, odd_weights,
            score_one, apply_one,
        )

    @pl.when(jnp.logical_not(safe))
    def _():
        def visit(index, carry):
            shifted(own_ref, far_ref, out_ref, units[0, index], units[1, index], keypoints)
            return carry

        lax.fori_loop(0, found, visit, 0)


def far_pairs(members, own, far, totals):
    full = own.shape[1]
    vmem = pl.BlockSpec(memory_space=pltpu.VMEM)
    return pl.pallas_call(
        functools.partial(far_kernel, members),
        out_shape=jax.ShapeDtypeStruct(totals.shape, F32),
        in_specs=[vmem] * 3,
        out_specs=vmem,
        scratch_shapes=pair_scratch(2 * members, full),
        compiler_params=pltpu.CompilerParams(vmem_limit_bytes=VMEM_LIMIT),
        cost_estimate=LONG,
        name="far_pairs",
    )(own, far, totals)


def merge_kernel(totals_ref, partial_ref, *outs):
    for slot, out_ref in enumerate(outs):
        out_ref[...] = (totals_ref[slot] + partial_ref[slot]).astype(BF16)


def merge(members, totals, partial):
    vmem = pl.BlockSpec(memory_space=pltpu.VMEM)
    message = jax.ShapeDtypeStruct(totals.shape[1:], BF16)
    return pl.pallas_call(
        merge_kernel,
        out_shape=[message] * members,
        in_specs=[vmem, vmem],
        out_specs=[vmem] * members,
        compiler_params=pltpu.CompilerParams(vmem_limit_bytes=VMEM_LIMIT),
        name="merge",
    )(totals, partial)


def update_kernel(members, desc_ref, w_ref, *refs):
    pieces = refs[:members]
    out_ref = refs[members]
    member = lax.axis_index("grp")
    weights = []
    for distance in range(members):
        head = lax.rem(member - distance + members, members)
        weights.append(w_ref[pl.ds(pl.multiple_of(head * HEAD_DIM, HEAD_DIM), HEAD_DIM), :])
    message = jnp.concatenate([piece[...] for piece in pieces], 0)
    update = lax.dot_general(
        message, jnp.concatenate(weights, 0), TN, preferred_element_type=F32
    )
    out_ref[0] = (desc_ref[0].astype(F32) + update).astype(BF16)


def update(members, desc, w_out, pieces):
    vmem = pl.BlockSpec(memory_space=pltpu.VMEM)
    return pl.pallas_call(
        functools.partial(update_kernel, members),
        out_shape=jax.ShapeDtypeStruct(desc.shape, BF16),
        in_specs=[vmem] * (2 + members),
        out_specs=vmem,
        compiler_params=pltpu.CompilerParams(vmem_limit_bytes=VMEM_LIMIT),
        name="update",
    )(desc, w_out, *pieces)


def on_device(desc, w_proj, w_out, pair_list, pair_count):
    columns = lax.axis_size("img")
    members = lax.axis_size("grp")

    def from_ahead(block, distance):
        route = [((i + distance) % members, i) for i in range(members)]
        return lax.ppermute(block, "grp", route)

    def swap(block, offset):
        pairs = []
        for i in range(offset, columns + offset, 2):
            low, high = i % columns, (i + 1) % columns
            pairs += [(low, high), (high, low)]
        return lax.ppermute(block, "img", pairs)

    sent = project(members, pair_list, pair_count, desc, w_proj)
    own = [sent[0]] + [from_ahead(sent[k], k) for k in range(1, members)]
    near = [swap(block, 0) for block in own]
    gathered, *near = lax.optimization_barrier([jnp.stack(own)] + near)
    far = swap(gathered, 1)
    totals, other = shared(members, [gathered] + near)
    partial = swap(other, 0)
    totals = far_pairs(members, gathered, far, totals)
    messages = merge(members, totals, partial)
    back = [messages[0]]
    for distance in range(1, members):
        back.append(from_ahead(messages[distance], members - distance))
    return update(members, desc, w_out, back)


def solution(mesh):
    return jax.shard_map(
        on_device,
        mesh=mesh,
        in_specs=(
            P(("img", "grp"), None, None),
            P(),
            P(),
            P(("img", "grp"), None),
            P(("img", "grp")),
        ),
        out_specs=P(("img", "grp"), None, None),
        check_vma=False,
    )
```

```python
import functools
import math

import jax
import jax.numpy as jnp
from jax import lax
from jax.experimental import pallas as pl
from jax.experimental.pallas import tpu as pltpu
from jax.sharding import PartitionSpec as P

D = 256
HEADS = 4
HEAD_DIM = 64
LANES = 128
ONES = 16
INFO = 16
PARTS = 4
SCALE = HEAD_DIM ** -0.5
LOG2E = math.log2(math.e)
SAFE_SCORE = 64.0
NORM_CAP = 250.0
BF16 = jnp.bfloat16
F32 = jnp.float32
NT = (((1,), (1,)), ((), ()))
TN = (((0,), (0,)), ((), ()))
VMEM_LIMIT = 28 * 1024 * 1024
ROW = 16
SHORT = pl.CostEstimate(flops=10**4, bytes_accessed=10**4, transcendentals=0)
LONG = pl.CostEstimate(flops=10**10, bytes_accessed=10**7, transcendentals=0)


def project_kernel(members, count_ref, list_hbm, desc_hbm, w_hbm, *refs):
    outs = refs[:members]
    turned, list_ref, desc_ref, w_ref, sems = refs[members:]
    copies = [
        pltpu.make_async_copy(source, target, sems.at[k])
        for k, (source, target) in enumerate(
            ((w_hbm, w_ref), (desc_hbm, desc_ref), (list_hbm, list_ref))
        )
    ]
    for copy in copies:
        copy.start()
    keypoints = desc_ref.shape[1]
    cap = list_ref.shape[1]
    member = lax.axis_index("grp")
    copies[0].wait()
    turned[...] = w_ref[...].T
    copies[2].wait()
    lane = lax.broadcasted_iota(jnp.int32, (INFO, LANES), 1)
    common = jnp.where(lane == 0, count_ref[0], 0)
    for slot in range(cap):
        first = jnp.broadcast_to(list_ref[0:1, slot : slot + 1], lane.shape)
        second = jnp.broadcast_to(list_ref[1:2, slot : slot + 1], lane.shape)
        common = jnp.where(lane == 2 + 2 * slot, first, common)
        common = jnp.where(lane == 3 + 2 * slot, second, common)
    common = common.astype(F32)
    copies[1].wait()
    desc = desc_ref[0]
    for distance in range(members):
        head = lax.rem(member - distance + members, members)
        lower = pl.multiple_of(head * HEAD_DIM, HEAD_DIM)
        weights = jnp.concatenate(
            [turned[pl.ds(lower, HEAD_DIM), :], turned[pl.ds(D + lower, HEAD_DIM), :]], 0
        )
        both = lax.dot_general(weights, desc, NT, preferred_element_type=F32).astype(BF16)
        for block in range(keypoints // LANES):
            outs[distance][block * LANES : (block + 1) * LANES, :] = both[
                :, block * LANES : (block + 1) * LANES
            ]
        query = both[:HEAD_DIM].astype(F32)
        squares = jnp.sum(query * query, axis=0, keepdims=True)
        norm = jnp.sqrt(jnp.max(squares, axis=1, keepdims=True)) * 1.001
        norm = jnp.ceil(jnp.minimum(norm, NORM_CAP))
        info = jnp.where(lane == 1, jnp.broadcast_to(norm, lane.shape), common)
        outs[distance][keypoints:, :] = info.astype(BF16)


def project(members, pair_list, pair_count, desc, w_proj):
    keypoints = desc.shape[1]
    hbm = pl.BlockSpec(memory_space=pltpu.HBM)
    out = jax.ShapeDtypeStruct((keypoints + INFO, LANES), BF16)
    listed = pair_list.T
    return pl.pallas_call(
        functools.partial(project_kernel, members),
        out_shape=[out] * members,
        in_specs=[pl.BlockSpec(memory_space=pltpu.SMEM), hbm, hbm, hbm],
        out_specs=[pl.BlockSpec(memory_space=pltpu.VMEM)] * members,
        scratch_shapes=[
            pltpu.VMEM((2 * D, D), BF16),
            pltpu.VMEM(listed.shape, jnp.int32),
            pltpu.VMEM(desc.shape, BF16),
            pltpu.VMEM(w_proj.shape, BF16),
            pltpu.SemaphoreType.DMA((3,)),
        ],
        compiler_params=pltpu.CompilerParams(vmem_limit_bytes=VMEM_LIMIT),
        name="project",
    )(pair_count, *[pltpu.with_memory_space_constraint(x, pltpu.HBM) for x in (listed, desc, w_proj)])


def query_of(rows, image, lower, size):
    parts = [
        rows[image, block : block + HEAD_DIM, :] for block in range(lower, lower + size, LANES)
    ]
    return jnp.concatenate(parts, 1)


def value_of(rows, image, lower, size):
    parts = [
        rows[image, block + HEAD_DIM : block + LANES, :]
        for block in range(lower, lower + size, LANES)
    ]
    return jnp.concatenate([jnp.ones((ONES, size), BF16), jnp.concatenate(parts, 1)], 0)


def score_one(rows, others, target, source, weights, block):
    keypoints = weights.shape[0]
    query = query_of(rows, target, 0, keypoints)
    for lower in range(0, keypoints, block):
        keys = query_of(others, source, lower, block)
        scores = lax.dot_general(keys, query, TN, preferred_element_type=F32)
        weights[lower : lower + block, :] = jnp.exp2(scores * (SCALE * LOG2E)).astype(BF16)


def apply_one(rows, others, totals, target, source, weights):
    values = value_of(others, source, 0, weights.shape[0])
    total = jnp.dot(values, weights[...], preferred_element_type=F32)
    totals[target] += total[ONES:] / total[:1]


def score_two(rows, others, target, source, weights, block):
    score_one(others, rows, source, target, weights, block)


def apply_two(rows, others, totals, target, source, weights):
    values = value_of(others, source, 0, weights.shape[0])
    total = lax.dot_general(values, weights[...], NT, preferred_element_type=F32)
    totals[target] += total[ONES:] / total[:1]
    apply_one(others, rows, totals, source, target, weights)


def run_units(rows, others, totals, units, begin, count, even_weights, odd_weights, score, apply):
    block = even_weights.shape[0] // 2

    def scored(index, weights):
        score(rows, others, units[0, index], units[1, index], weights, block)

    def applied(index, weights):
        apply(rows, others, totals, units[0, index], units[1, index], weights)

    @pl.when(count > 0)
    def _():
        scored(begin, even_weights)

        def step(index, carry):
            now = begin + 2 * index
            scored(now + 1, odd_weights)
            applied(now, even_weights)
            scored(now + 2, even_weights)
            applied(now + 1, odd_weights)
            return carry

        lax.fori_loop(0, (count - 1) // 2, step, 0)
        last = begin + count - 1

        @pl.when(lax.rem(count, 2) == 0)
        def _():
            scored(last, odd_weights)
            applied(last - 1, even_weights)
            applied(last, odd_weights)

        @pl.when(lax.rem(count, 2) == 1)
        def _():
            applied(last, even_weights)


def shifted(rows, others, totals, target, source, keypoints):
    narrow = 2 * LANES
    keys = query_of(others, source, 0, keypoints)
    values = value_of(others, source, 0, keypoints)

    def step(index, carry):
        lower = pl.multiple_of(index * narrow, narrow)
        parts = [
            rows[target, pl.ds(pl.multiple_of(lower + offset, LANES), HEAD_DIM), :]
            for offset in range(0, narrow, LANES)
        ]
        query = jnp.concatenate(parts, 1)
        scores = lax.dot_general(keys, query, TN, preferred_element_type=F32) * SCALE
        weights = jnp.exp(scores - jnp.max(scores, axis=0, keepdims=True)).astype(BF16)
        total = jnp.dot(values, weights, preferred_element_type=F32)
        totals[target, :, pl.ds(lower, narrow)] += total[ONES:] / total[:1]
        return carry

    lax.fori_loop(0, keypoints // narrow, step, 0)


def start_copies(pieces, rows, info_v, sems):
    keypoints = rows.shape[1] - INFO
    copies = []
    position = 0
    for piece in pieces:
        if len(piece.shape) == 3:
            place = slice(position, position + piece.shape[0])
            position += piece.shape[0]
            listed = piece[:, keypoints : keypoints + 8]
        else:
            place = position
            position += 1
            listed = piece[keypoints : keypoints + 8]
        copies.append(pltpu.make_async_copy(piece, rows.at[place], sems.at[len(copies)]))
        copies[-1].start()
        info_v[place] = listed.astype(F32).astype(jnp.int32)
    return copies


def to_scalars(info_v, info, info_sem):
    copy = pltpu.make_async_copy(info_v, info, info_sem)
    copy.start()
    copy.wait()


def place_of(image, members, member):
    return lax.rem(lax.rem(image, members) - member + members, members)


def shared_kernel(members, pieces_count, *refs):
    count = 2 * members
    pieces, (own_ref, other_ref, *refs) = refs[:pieces_count], refs[pieces_count:]
    rows, totals, even_weights, odd_weights, *refs = refs
    info_v, info, units, info_sem, sems = refs
    keypoints = totals.shape[2]
    column = lax.axis_index("img")
    member = lax.axis_index("grp")

    copies = start_copies(pieces, rows, info_v, sems)
    to_scalars(info_v, info, info_sem)
    totals[...] = jnp.zeros_like(totals)
    side = lax.rem(column, 2)

    def slot(index, found):
        right = index >= members
        base = jnp.where(right == (side == 1), 0, members)
        owner = base + lax.rem(index, members)
        listed = column - side + right.astype(jnp.int32)

        def position(step, found):
            first = info[owner, 0, 2 + 2 * step]
            second = info[owner, 0, 3 + 2 * step]
            inside = second // members == listed
            shared = jnp.logical_or(jnp.logical_not(right), inside)

            @pl.when(shared)
            def _():
                units[0, found] = base + place_of(first, members, member)
                units[1, found] = jnp.where(inside, base, members - base) + place_of(
                    second, members, member
                )

            return found + shared.astype(jnp.int32)

        return lax.fori_loop(0, info[owner, 0, 0], position, found)

    found = lax.fori_loop(0, count, slot, jnp.int32(0))
    row = lax.rem(column - side, ROW)
    half = found // 2 + (row == ROW - 2).astype(jnp.int32) - (row == 0).astype(jnp.int32)
    half = jnp.clip(half, 0, found)
    begin = jnp.where(side == 0, 0, half)
    end = jnp.where(side == 0, half, found)
    largest = info[0, 0, 1]
    for position in range(1, count):
        largest = jnp.maximum(largest, info[position, 0, 1])
    safe = largest * largest <= int(SAFE_SCORE / SCALE)
    for copy in copies:
        copy.wait()

    @pl.when(safe)
    def _():
        run_units(
            rows, rows, totals, units, begin, end - begin, even_weights, odd_weights,
            score_two, apply_two,
        )

    @pl.when(jnp.logical_not(safe))
    def _():
        def visit(index, carry):
            target, source = units[0, index], units[1, index]
            shifted(rows, rows, totals, target, source, keypoints)
            shifted(rows, rows, totals, source, target, keypoints)
            return carry

        lax.fori_loop(begin, end, visit, 0)

    own_ref[...] = totals[:members]
    other_ref[...] = totals[members:]


def pair_scratch(count, full):
    keypoints = full - INFO
    return [
        pltpu.VMEM((keypoints, keypoints), BF16),
        pltpu.VMEM((keypoints, keypoints), BF16),
        pltpu.VMEM((count, 8, LANES), jnp.int32),
        pltpu.SMEM((count, 8, LANES), jnp.int32),
        pltpu.SMEM((2, 8 * LANES), jnp.int32),
        pltpu.SemaphoreType.DMA,
    ]


def shared(members, pieces):
    full = pieces[0].shape[1]
    keypoints = full - INFO
    count = 2 * members
    vmem = pl.BlockSpec(memory_space=pltpu.VMEM)
    whole = jax.ShapeDtypeStruct((members, HEAD_DIM, keypoints), F32)
    return pl.pallas_call(
        functools.partial(shared_kernel, members, len(pieces)),
        out_shape=[whole, whole],
        in_specs=[vmem] * len(pieces),
        out_specs=[vmem, vmem],
        scratch_shapes=[
            pltpu.VMEM((count, full, LANES), BF16),
            pltpu.VMEM((count, HEAD_DIM, keypoints), F32),
            *pair_scratch(count, full),
            pltpu.SemaphoreType.DMA((len(pieces),)),
        ],
        compiler_params=pltpu.CompilerParams(vmem_limit_bytes=VMEM_LIMIT),
        cost_estimate=SHORT,
        name="shared",
    )(*pieces)


def far_kernel(members, own_ref, far_ref, start_ref, out_ref, *refs):
    even_weights, odd_weights, info_v, info, units, info_sem = refs
    keypoints = out_ref.shape[2]
    column = lax.axis_index("img")
    member = lax.axis_index("grp")
    info_v[:members] = own_ref[:, keypoints : keypoints + 8].astype(F32).astype(jnp.int32)
    info_v[members:] = far_ref[:, keypoints : keypoints + 8].astype(F32).astype(jnp.int32)
    to_scalars(info_v, info, info_sem)
    out_ref[...] = start_ref[...]
    ahead = lax.rem(column, 2) == 1
    listed = jnp.where(ahead, 0, members)

    def slot(index, found):
        owner = listed + index

        def position(step, found):
            first = info[owner, 0, 2 + 2 * step]
            second = info[owner, 0, 3 + 2 * step]
            wanted = (second // members == column) != ahead

            @pl.when(wanted)
            def _():
                left = place_of(first, members, member)
                right = place_of(second, members, member)
                units[0, found] = jnp.where(ahead, left, right)
                units[1, found] = jnp.where(ahead, right, left)

            return found + wanted.astype(jnp.int32)

        return lax.fori_loop(0, info[owner, 0, 0], position, found)

    found = lax.fori_loop(0, members, slot, jnp.int32(0))
    left, right = info[0, 0, 1], info[members, 0, 1]
    for position in range(1, members):
        left = jnp.maximum(left, info[position, 0, 1])
        right = jnp.maximum(right, info[members + position, 0, 1])
    safe = jnp.logical_and(
        jnp.maximum(left, right) < int(NORM_CAP), left * right <= int(SAFE_SCORE / SCALE)
    )

    @pl.when(safe)
    def _():
        run_units(
            own_ref, far_ref, out_ref, units, jnp.int32(0), found, even_weights, odd_weights,
            score_one, apply_one,
        )

    @pl.when(jnp.logical_not(safe))
    def _():
        def visit(index, carry):
            shifted(own_ref, far_ref, out_ref, units[0, index], units[1, index], keypoints)
            return carry

        lax.fori_loop(0, found, visit, 0)


def far_pairs(members, own, far, totals):
    full = own.shape[1]
    vmem = pl.BlockSpec(memory_space=pltpu.VMEM)
    return pl.pallas_call(
        functools.partial(far_kernel, members),
        out_shape=jax.ShapeDtypeStruct(totals.shape, F32),
        in_specs=[vmem] * 3,
        out_specs=vmem,
        scratch_shapes=pair_scratch(2 * members, full),
        compiler_params=pltpu.CompilerParams(vmem_limit_bytes=VMEM_LIMIT),
        cost_estimate=LONG,
        name="far_pairs",
    )(own, far, totals)


def merge_kernel(totals_ref, partial_ref, *outs):
    for slot, out_ref in enumerate(outs):
        out_ref[...] = (totals_ref[slot] + partial_ref[slot]).astype(BF16)


def merge(members, totals, partial):
    vmem = pl.BlockSpec(memory_space=pltpu.VMEM)
    message = jax.ShapeDtypeStruct(totals.shape[1:], BF16)
    return pl.pallas_call(
        merge_kernel,
        out_shape=[message] * members,
        in_specs=[vmem, vmem],
        out_specs=[vmem] * members,
        compiler_params=pltpu.CompilerParams(vmem_limit_bytes=VMEM_LIMIT),
        name="merge",
    )(totals, partial)


def update_kernel(members, desc_ref, w_ref, *refs):
    pieces = refs[:members]
    out_hbm, held, sems = refs[members:]
    member = lax.axis_index("grp")
    weights = []
    for distance in range(members):
        head = lax.rem(member - distance + members, members)
        weights.append(w_ref[pl.ds(pl.multiple_of(head * HEAD_DIM, HEAD_DIM), HEAD_DIM), :])
    weights = jnp.concatenate(weights, 0)
    block = held.shape[0] // PARTS
    copies = []
    for part in range(PARTS):
        place = slice(part * block, (part + 1) * block)
        message = jnp.concatenate([piece[:, place] for piece in pieces], 0)
        update = lax.dot_general(message, weights, TN, preferred_element_type=F32)
        held[place, :] = (desc_ref[0, place, :].astype(F32) + update).astype(BF16)
        copies.append(
            pltpu.make_async_copy(held.at[place], out_hbm.at[0, place], sems.at[part])
        )
        copies[-1].start()
    for copy in copies:
        copy.wait()


def update(members, desc, w_out, pieces):
    vmem = pl.BlockSpec(memory_space=pltpu.VMEM)
    return pl.pallas_call(
        functools.partial(update_kernel, members),
        out_shape=jax.ShapeDtypeStruct(desc.shape, BF16),
        in_specs=[vmem] * (2 + members),
        out_specs=pl.BlockSpec(memory_space=pltpu.HBM),
        scratch_shapes=[
            pltpu.VMEM(desc.shape[1:], BF16),
            pltpu.SemaphoreType.DMA((PARTS,)),
        ],
        compiler_params=pltpu.CompilerParams(vmem_limit_bytes=VMEM_LIMIT),
        name="update",
    )(desc, w_out, *pieces)


def on_device(desc, w_proj, w_out, pair_list, pair_count):
    columns = lax.axis_size("img")
    members = lax.axis_size("grp")

    def from_ahead(block, distance):
        route = [((i + distance) % members, i) for i in range(members)]
        return lax.ppermute(block, "grp", route)

    def swap(block, offset):
        pairs = []
        for i in range(offset, columns + offset, 2):
            low, high = i % columns, (i + 1) % columns
            pairs += [(low, high), (high, low)]
        return lax.ppermute(block, "img", pairs)

    sent = project(members, pair_list, pair_count, desc, w_proj)
    own = [sent[0]] + [from_ahead(sent[k], k) for k in range(1, members)]
    near = [swap(block, 0) for block in own]
    gathered, *near = lax.optimization_barrier([jnp.stack(own)] + near)
    far = swap(gathered, 1)
    totals, other = shared(members, [gathered] + near)
    partial = swap(other, 0)
    totals = far_pairs(members, gathered, far, totals)
    messages = merge(members, totals, partial)
    back = [messages[0]]
    for distance in range(1, members):
        back.append(from_ahead(messages[distance], members - distance))
    return update(members, desc, w_out, back)


def solution(mesh):
    return jax.shard_map(
        on_device,
        mesh=mesh,
        in_specs=(
            P(("img", "grp"), None, None),
            P(),
            P(),
            P(("img", "grp"), None),
            P(("img", "grp")),
        ),
        out_specs=P(("img", "grp"), None, None),
        check_vma=False,
    )
```

```python
import functools
import math

import jax
import jax.numpy as jnp
from jax import lax
from jax.experimental import pallas as pl
from jax.experimental.pallas import tpu as pltpu
from jax.sharding import PartitionSpec as P

D = 256
HEADS = 4
HEAD_DIM = 64
LANES = 128
ONES = 16
INFO = 16
PARTS = 4
SCALE = HEAD_DIM ** -0.5
LOG2E = math.log2(math.e)
SAFE_SCORE = 64.0
NORM_CAP = 250.0
BF16 = jnp.bfloat16
F32 = jnp.float32
NT = (((1,), (1,)), ((), ()))
TN = (((0,), (0,)), ((), ()))
VMEM_LIMIT = 28 * 1024 * 1024
ROW = 16
SHORT = pl.CostEstimate(flops=10**4, bytes_accessed=10**4, transcendentals=0)
LONG = pl.CostEstimate(flops=10**10, bytes_accessed=10**7, transcendentals=0)


def project_kernel(members, count_ref, list_hbm, desc_hbm, w_hbm, *refs):
    outs = refs[:members]
    turned, list_ref, desc_ref, w_ref, sems = refs[members:]
    copies = [
        pltpu.make_async_copy(source, target, sems.at[k])
        for k, (source, target) in enumerate(
            ((w_hbm, w_ref), (desc_hbm, desc_ref), (list_hbm, list_ref))
        )
    ]
    for copy in copies:
        copy.start()
    keypoints = desc_ref.shape[1]
    cap = list_ref.shape[1]
    member = lax.axis_index("grp")
    copies[0].wait()
    turned[...] = w_ref[...].T
    copies[2].wait()
    lane = lax.broadcasted_iota(jnp.int32, (INFO, LANES), 1)
    common = jnp.where(lane == 0, count_ref[0], 0)
    for slot in range(cap):
        first = jnp.broadcast_to(list_ref[0:1, slot : slot + 1], lane.shape)
        second = jnp.broadcast_to(list_ref[1:2, slot : slot + 1], lane.shape)
        common = jnp.where(lane == 2 + 2 * slot, first, common)
        common = jnp.where(lane == 3 + 2 * slot, second, common)
    common = common.astype(F32)
    copies[1].wait()
    desc = desc_ref[0]
    for distance in range(members):
        head = lax.rem(member - distance + members, members)
        lower = pl.multiple_of(head * HEAD_DIM, HEAD_DIM)
        weights = jnp.concatenate(
            [turned[pl.ds(lower, HEAD_DIM), :], turned[pl.ds(D + lower, HEAD_DIM), :]], 0
        )
        both = lax.dot_general(weights, desc, NT, preferred_element_type=F32).astype(BF16)
        for block in range(keypoints // LANES):
            outs[distance][block * LANES : (block + 1) * LANES, :] = both[
                :, block * LANES : (block + 1) * LANES
            ]
        query = both[:HEAD_DIM].astype(F32)
        squares = jnp.sum(query * query, axis=0, keepdims=True)
        norm = jnp.sqrt(jnp.max(squares, axis=1, keepdims=True)) * 1.001
        norm = jnp.ceil(jnp.minimum(norm, NORM_CAP))
        info = jnp.where(lane == 1, jnp.broadcast_to(norm, lane.shape), common)
        outs[distance][keypoints:, :] = info.astype(BF16)


def project(members, pair_list, pair_count, desc, w_proj):
    keypoints = desc.shape[1]
    hbm = pl.BlockSpec(memory_space=pltpu.HBM)
    out = jax.ShapeDtypeStruct((keypoints + INFO, LANES), BF16)
    listed = pair_list.T
    return pl.pallas_call(
        functools.partial(project_kernel, members),
        out_shape=[out] * members,
        in_specs=[pl.BlockSpec(memory_space=pltpu.SMEM), hbm, hbm, hbm],
        out_specs=[pl.BlockSpec(memory_space=pltpu.VMEM)] * members,
        scratch_shapes=[
            pltpu.VMEM((2 * D, D), BF16),
            pltpu.VMEM(listed.shape, jnp.int32),
            pltpu.VMEM(desc.shape, BF16),
            pltpu.VMEM(w_proj.shape, BF16),
            pltpu.SemaphoreType.DMA((3,)),
        ],
        compiler_params=pltpu.CompilerParams(vmem_limit_bytes=VMEM_LIMIT),
        name="project",
    )(pair_count, *[pltpu.with_memory_space_constraint(x, pltpu.HBM) for x in (listed, desc, w_proj)])


def query_of(rows, image, lower, size):
    parts = [
        rows[image, block : block + HEAD_DIM, :] for block in range(lower, lower + size, LANES)
    ]
    return jnp.concatenate(parts, 1)


def value_of(rows, image, lower, size):
    parts = [
        rows[image, block + HEAD_DIM : block + LANES, :]
        for block in range(lower, lower + size, LANES)
    ]
    return jnp.concatenate([jnp.ones((ONES, size), BF16), jnp.concatenate(parts, 1)], 0)


def score_one(rows, others, target, source, weights, block):
    keypoints = weights.shape[0]
    query = query_of(rows, target, 0, keypoints)
    for lower in range(0, keypoints, block):
        keys = query_of(others, source, lower, block)
        scores = lax.dot_general(keys, query, TN, preferred_element_type=F32)
        weights[lower : lower + block, :] = jnp.exp2(scores * (SCALE * LOG2E)).astype(BF16)


def apply_one(rows, others, totals, target, source, weights):
    values = value_of(others, source, 0, weights.shape[0])
    total = jnp.dot(values, weights[...], preferred_element_type=F32)
    totals[target] += total[ONES:] / total[:1]


def score_two(rows, others, target, source, weights, block):
    score_one(others, rows, source, target, weights, block)


def apply_two(rows, others, totals, target, source, weights):
    values = value_of(others, source, 0, weights.shape[0])
    total = lax.dot_general(values, weights[...], NT, preferred_element_type=F32)
    totals[target] += total[ONES:] / total[:1]
    apply_one(others, rows, totals, source, target, weights)


def run_units(rows, others, totals, units, begin, count, even_weights, odd_weights, score, apply):
    block = even_weights.shape[0] // 2

    def scored(index, weights):
        score(rows, others, units[0, index], units[1, index], weights, block)

    def applied(index, weights):
        apply(rows, others, totals, units[0, index], units[1, index], weights)

    @pl.when(count > 0)
    def _():
        scored(begin, even_weights)

        def step(index, carry):
            now = begin + 2 * index
            scored(now + 1, odd_weights)
            applied(now, even_weights)
            scored(now + 2, even_weights)
            applied(now + 1, odd_weights)
            return carry

        lax.fori_loop(0, (count - 1) // 2, step, 0)
        last = begin + count - 1

        @pl.when(lax.rem(count, 2) == 0)
        def _():
            scored(last, odd_weights)
            applied(last - 1, even_weights)
            applied(last, odd_weights)

        @pl.when(lax.rem(count, 2) == 1)
        def _():
            applied(last, even_weights)


def shifted(rows, others, totals, target, source, keypoints):
    narrow = 2 * LANES
    keys = query_of(others, source, 0, keypoints)
    values = value_of(others, source, 0, keypoints)

    def step(index, carry):
        lower = pl.multiple_of(index * narrow, narrow)
        parts = [
            rows[target, pl.ds(pl.multiple_of(lower + offset, LANES), HEAD_DIM), :]
            for offset in range(0, narrow, LANES)
        ]
        query = jnp.concatenate(parts, 1)
        scores = lax.dot_general(keys, query, TN, preferred_element_type=F32) * SCALE
        weights = jnp.exp(scores - jnp.max(scores, axis=0, keepdims=True)).astype(BF16)
        total = jnp.dot(values, weights, preferred_element_type=F32)
        totals[target, :, pl.ds(lower, narrow)] += total[ONES:] / total[:1]
        return carry

    lax.fori_loop(0, keypoints // narrow, step, 0)


def start_copies(pieces, rows, info_v, sems):
    keypoints = rows.shape[1] - INFO
    copies = []
    position = 0
    for piece in pieces:
        if len(piece.shape) == 3:
            place = slice(position, position + piece.shape[0])
            position += piece.shape[0]
            listed = piece[:, keypoints : keypoints + 8]
        else:
            place = position
            position += 1
            listed = piece[keypoints : keypoints + 8]
        copies.append(pltpu.make_async_copy(piece, rows.at[place], sems.at[len(copies)]))
        copies[-1].start()
        info_v[place] = listed.astype(F32).astype(jnp.int32)
    return copies


def to_scalars(info_v, info, info_sem):
    copy = pltpu.make_async_copy(info_v, info, info_sem)
    copy.start()
    copy.wait()


def place_of(image, members, member):
    return lax.rem(lax.rem(image, members) - member + members, members)


def shared_kernel(members, pieces_count, *refs):
    count = 2 * members
    pieces, (own_ref, other_ref, *refs) = refs[:pieces_count], refs[pieces_count:]
    rows, totals, even_weights, odd_weights, *refs = refs
    info_v, info, units, info_sem, sems = refs
    keypoints = totals.shape[2]
    column = lax.axis_index("img")
    member = lax.axis_index("grp")

    copies = start_copies(pieces, rows, info_v, sems)
    to_scalars(info_v, info, info_sem)
    totals[...] = jnp.zeros_like(totals)
    side = lax.rem(column, 2)

    def slot(index, found):
        right = index >= members
        base = jnp.where(right == (side == 1), 0, members)
        owner = base + lax.rem(index, members)
        listed = column - side + right.astype(jnp.int32)

        def position(step, found):
            first = info[owner, 0, 2 + 2 * step]
            second = info[owner, 0, 3 + 2 * step]
            inside = second // members == listed
            shared = jnp.logical_or(jnp.logical_not(right), inside)

            @pl.when(shared)
            def _():
                units[0, found] = base + place_of(first, members, member)
                units[1, found] = jnp.where(inside, base, members - base) + place_of(
                    second, members, member
                )

            return found + shared.astype(jnp.int32)

        return lax.fori_loop(0, info[owner, 0, 0], position, found)

    found = lax.fori_loop(0, count, slot, jnp.int32(0))
    row = lax.rem(column - side, ROW)
    shift = (row == ROW - 2).astype(jnp.int32) - (row == 0).astype(jnp.int32)
    half = jnp.clip(found // 2 + 2 * shift, 0, found)
    begin = jnp.where(side == 0, 0, half)
    end = jnp.where(side == 0, half, found)
    largest = info[0, 0, 1]
    for position in range(1, count):
        largest = jnp.maximum(largest, info[position, 0, 1])
    safe = largest * largest <= int(SAFE_SCORE / SCALE)
    for copy in copies:
        copy.wait()

    @pl.when(safe)
    def _():
        run_units(
            rows, rows, totals, units, begin, end - begin, even_weights, odd_weights,
            score_two, apply_two,
        )

    @pl.when(jnp.logical_not(safe))
    def _():
        def visit(index, carry):
            target, source = units[0, index], units[1, index]
            shifted(rows, rows, totals, target, source, keypoints)
            shifted(rows, rows, totals, source, target, keypoints)
            return carry

        lax.fori_loop(begin, end, visit, 0)

    own_ref[...] = totals[:members]
    other_ref[...] = totals[members:]


def pair_scratch(count, full):
    keypoints = full - INFO
    return [
        pltpu.VMEM((keypoints, keypoints), BF16),
        pltpu.VMEM((keypoints, keypoints), BF16),
        pltpu.VMEM((count, 8, LANES), jnp.int32),
        pltpu.SMEM((count, 8, LANES), jnp.int32),
        pltpu.SMEM((2, 8 * LANES), jnp.int32),
        pltpu.SemaphoreType.DMA,
    ]


def shared(members, pieces):
    full = pieces[0].shape[1]
    keypoints = full - INFO
    count = 2 * members
    vmem = pl.BlockSpec(memory_space=pltpu.VMEM)
    whole = jax.ShapeDtypeStruct((members, HEAD_DIM, keypoints), F32)
    return pl.pallas_call(
        functools.partial(shared_kernel, members, len(pieces)),
        out_shape=[whole, whole],
        in_specs=[vmem] * len(pieces),
        out_specs=[vmem, vmem],
        scratch_shapes=[
            pltpu.VMEM((count, full, LANES), BF16),
            pltpu.VMEM((count, HEAD_DIM, keypoints), F32),
            *pair_scratch(count, full),
            pltpu.SemaphoreType.DMA((len(pieces),)),
        ],
        compiler_params=pltpu.CompilerParams(vmem_limit_bytes=VMEM_LIMIT),
        cost_estimate=SHORT,
        name="shared",
    )(*pieces)


def far_kernel(members, own_ref, far_ref, start_ref, out_ref, *refs):
    even_weights, odd_weights, info_v, info, units, info_sem = refs
    keypoints = out_ref.shape[2]
    column = lax.axis_index("img")
    member = lax.axis_index("grp")
    info_v[:members] = own_ref[:, keypoints : keypoints + 8].astype(F32).astype(jnp.int32)
    info_v[members:] = far_ref[:, keypoints : keypoints + 8].astype(F32).astype(jnp.int32)
    to_scalars(info_v, info, info_sem)
    out_ref[...] = start_ref[...]
    ahead = lax.rem(column, 2) == 1
    listed = jnp.where(ahead, 0, members)

    def slot(index, found):
        owner = listed + index

        def position(step, found):
            first = info[owner, 0, 2 + 2 * step]
            second = info[owner, 0, 3 + 2 * step]
            wanted = (second // members == column) != ahead

            @pl.when(wanted)
            def _():
                left = place_of(first, members, member)
                right = place_of(second, members, member)
                units[0, found] = jnp.where(ahead, left, right)
                units[1, found] = jnp.where(ahead, right, left)

            return found + wanted.astype(jnp.int32)

        return lax.fori_loop(0, info[owner, 0, 0], position, found)

    found = lax.fori_loop(0, members, slot, jnp.int32(0))
    left, right = info[0, 0, 1], info[members, 0, 1]
    for position in range(1, members):
        left = jnp.maximum(left, info[position, 0, 1])
        right = jnp.maximum(right, info[members + position, 0, 1])
    safe = jnp.logical_and(
        jnp.maximum(left, right) < int(NORM_CAP), left * right <= int(SAFE_SCORE / SCALE)
    )

    @pl.when(safe)
    def _():
        run_units(
            own_ref, far_ref, out_ref, units, jnp.int32(0), found, even_weights, odd_weights,
            score_one, apply_one,
        )

    @pl.when(jnp.logical_not(safe))
    def _():
        def visit(index, carry):
            shifted(own_ref, far_ref, out_ref, units[0, index], units[1, index], keypoints)
            return carry

        lax.fori_loop(0, found, visit, 0)


def far_pairs(members, own, far, totals):
    full = own.shape[1]
    vmem = pl.BlockSpec(memory_space=pltpu.VMEM)
    return pl.pallas_call(
        functools.partial(far_kernel, members),
        out_shape=jax.ShapeDtypeStruct(totals.shape, F32),
        in_specs=[vmem] * 3,
        out_specs=vmem,
        scratch_shapes=pair_scratch(2 * members, full),
        compiler_params=pltpu.CompilerParams(vmem_limit_bytes=VMEM_LIMIT),
        cost_estimate=LONG,
        name="far_pairs",
    )(own, far, totals)


def merge_kernel(totals_ref, partial_ref, *outs):
    for slot, out_ref in enumerate(outs):
        out_ref[...] = (totals_ref[slot] + partial_ref[slot]).astype(BF16)


def merge(members, totals, partial):
    vmem = pl.BlockSpec(memory_space=pltpu.VMEM)
    message = jax.ShapeDtypeStruct(totals.shape[1:], BF16)
    return pl.pallas_call(
        merge_kernel,
        out_shape=[message] * members,
        in_specs=[vmem, vmem],
        out_specs=[vmem] * members,
        compiler_params=pltpu.CompilerParams(vmem_limit_bytes=VMEM_LIMIT),
        name="merge",
    )(totals, partial)


def update_kernel(members, desc_ref, w_ref, *refs):
    pieces = refs[:members]
    out_hbm, held, sems = refs[members:]
    member = lax.axis_index("grp")
    weights = []
    for distance in range(members):
        head = lax.rem(member - distance + members, members)
        weights.append(w_ref[pl.ds(pl.multiple_of(head * HEAD_DIM, HEAD_DIM), HEAD_DIM), :])
    weights = jnp.concatenate(weights, 0)
    block = held.shape[0] // PARTS
    copies = []
    for part in range(PARTS):
        place = slice(part * block, (part + 1) * block)
        message = jnp.concatenate([piece[:, place] for piece in pieces], 0)
        update = lax.dot_general(message, weights, TN, preferred_element_type=F32)
        held[place, :] = (desc_ref[0, place, :].astype(F32) + update).astype(BF16)
        copies.append(
            pltpu.make_async_copy(held.at[place], out_hbm.at[0, place], sems.at[part])
        )
        copies[-1].start()
    for copy in copies:
        copy.wait()


def update(members, desc, w_out, pieces):
    vmem = pl.BlockSpec(memory_space=pltpu.VMEM)
    return pl.pallas_call(
        functools.partial(update_kernel, members),
        out_shape=jax.ShapeDtypeStruct(desc.shape, BF16),
        in_specs=[vmem] * (2 + members),
        out_specs=pl.BlockSpec(memory_space=pltpu.HBM),
        scratch_shapes=[
            pltpu.VMEM(desc.shape[1:], BF16),
            pltpu.SemaphoreType.DMA((PARTS,)),
        ],
        compiler_params=pltpu.CompilerParams(vmem_limit_bytes=VMEM_LIMIT),
        name="update",
    )(desc, w_out, *pieces)


def on_device(desc, w_proj, w_out, pair_list, pair_count):
    columns = lax.axis_size("img")
    members = lax.axis_size("grp")

    def from_ahead(block, distance):
        route = [((i + distance) % members, i) for i in range(members)]
        return lax.ppermute(block, "grp", route)

    def swap(block, offset):
        pairs = []
        for i in range(offset, columns + offset, 2):
            low, high = i % columns, (i + 1) % columns
            pairs += [(low, high), (high, low)]
        return lax.ppermute(block, "img", pairs)

    sent = project(members, pair_list, pair_count, desc, w_proj)
    own = [sent[0]] + [from_ahead(sent[k], k) for k in range(1, members)]
    near = [swap(block, 0) for block in own]
    gathered, *near = lax.optimization_barrier([jnp.stack(own)] + near)
    far = swap(gathered, 1)
    totals, other = shared(members, [gathered] + near)
    partial = swap(other, 0)
    totals = far_pairs(members, gathered, far, totals)
    messages = merge(members, totals, partial)
    back = [messages[0]]
    for distance in range(1, members):
        back.append(from_ahead(messages[distance], members - distance))
    return update(members, desc, w_out, back)


def solution(mesh):
    return jax.shard_map(
        on_device,
        mesh=mesh,
        in_specs=(
            P(("img", "grp"), None, None),
            P(),
            P(),
            P(("img", "grp"), None),
            P(("img", "grp")),
        ),
        out_specs=P(("img", "grp"), None, None),
        check_vma=False,
    )
```

```python
import functools
import math

import jax
import jax.numpy as jnp
from jax import lax
from jax.experimental import pallas as pl
from jax.experimental.pallas import tpu as pltpu
from jax.sharding import PartitionSpec as P

D = 256
HEADS = 4
HEAD_DIM = 64
LANES = 128
ONES = 16
INFO = 16
PARTS = 4
SCALE = HEAD_DIM ** -0.5
LOG2E = math.log2(math.e)
SAFE_SCORE = 64.0
NORM_CAP = 250.0
BF16 = jnp.bfloat16
F32 = jnp.float32
NT = (((1,), (1,)), ((), ()))
TN = (((0,), (0,)), ((), ()))
VMEM_LIMIT = 28 * 1024 * 1024
ROW = 16
SHORT = pl.CostEstimate(flops=10**4, bytes_accessed=10**4, transcendentals=0)
LONG = pl.CostEstimate(flops=10**10, bytes_accessed=10**7, transcendentals=0)


def project_kernel(members, count_ref, list_hbm, desc_hbm, w_hbm, *refs):
    outs = refs[:members]
    turned, list_ref, desc_ref, w_ref, sems = refs[members:]
    copies = [
        pltpu.make_async_copy(source, target, sems.at[k])
        for k, (source, target) in enumerate(
            ((w_hbm, w_ref), (desc_hbm, desc_ref), (list_hbm, list_ref))
        )
    ]
    for copy in copies:
        copy.start()
    keypoints = desc_ref.shape[1]
    cap = list_ref.shape[1]
    member = lax.axis_index("grp")
    copies[0].wait()
    turned[...] = w_ref[...].T
    copies[2].wait()
    lane = lax.broadcasted_iota(jnp.int32, (INFO, LANES), 1)
    common = jnp.where(lane == 0, count_ref[0], 0)
    for slot in range(cap):
        first = jnp.broadcast_to(list_ref[0:1, slot : slot + 1], lane.shape)
        second = jnp.broadcast_to(list_ref[1:2, slot : slot + 1], lane.shape)
        common = jnp.where(lane == 2 + 2 * slot, first, common)
        common = jnp.where(lane == 3 + 2 * slot, second, common)
    common = common.astype(F32)
    copies[1].wait()
    desc = desc_ref[0]
    for distance in range(members):
        head = lax.rem(member - distance + members, members)
        lower = pl.multiple_of(head * HEAD_DIM, HEAD_DIM)
        weights = jnp.concatenate(
            [turned[pl.ds(lower, HEAD_DIM), :], turned[pl.ds(D + lower, HEAD_DIM), :]], 0
        )
        both = lax.dot_general(weights, desc, NT, preferred_element_type=F32).astype(BF16)
        for block in range(keypoints // LANES):
            outs[distance][block * LANES : (block + 1) * LANES, :] = both[
                :, block * LANES : (block + 1) * LANES
            ]
        query = both[:HEAD_DIM].astype(F32)
        squares = jnp.sum(query * query, axis=0, keepdims=True)
        norm = jnp.sqrt(jnp.max(squares, axis=1, keepdims=True)) * 1.001
        norm = jnp.ceil(jnp.minimum(norm, NORM_CAP))
        info = jnp.where(lane == 1, jnp.broadcast_to(norm, lane.shape), common)
        outs[distance][keypoints:, :] = info.astype(BF16)


def project(members, pair_list, pair_count, desc, w_proj):
    keypoints = desc.shape[1]
    hbm = pl.BlockSpec(memory_space=pltpu.HBM)
    out = jax.ShapeDtypeStruct((keypoints + INFO, LANES), BF16)
    listed = pair_list.T
    return pl.pallas_call(
        functools.partial(project_kernel, members),
        out_shape=[out] * members,
        in_specs=[pl.BlockSpec(memory_space=pltpu.SMEM), hbm, hbm, hbm],
        out_specs=[pl.BlockSpec(memory_space=pltpu.VMEM)] * members,
        scratch_shapes=[
            pltpu.VMEM((2 * D, D), BF16),
            pltpu.VMEM(listed.shape, jnp.int32),
            pltpu.VMEM(desc.shape, BF16),
            pltpu.VMEM(w_proj.shape, BF16),
            pltpu.SemaphoreType.DMA((3,)),
        ],
        compiler_params=pltpu.CompilerParams(vmem_limit_bytes=VMEM_LIMIT),
        name="project",
    )(pair_count, *[pltpu.with_memory_space_constraint(x, pltpu.HBM) for x in (listed, desc, w_proj)])


def query_of(rows, image, lower, size):
    parts = [
        rows[image, block : block + HEAD_DIM, :] for block in range(lower, lower + size, LANES)
    ]
    return jnp.concatenate(parts, 1)


def value_of(rows, image, lower, size):
    parts = [
        rows[image, block + HEAD_DIM : block + LANES, :]
        for block in range(lower, lower + size, LANES)
    ]
    return jnp.concatenate([jnp.ones((ONES, size), BF16), jnp.concatenate(parts, 1)], 0)


def score_one(rows, others, target, source, weights, block):
    keypoints = weights.shape[0]
    query = query_of(rows, target, 0, keypoints)
    for lower in range(0, keypoints, block):
        keys = query_of(others, source, lower, block)
        scores = lax.dot_general(keys, query, TN, preferred_element_type=F32)
        weights[lower : lower + block, :] = jnp.exp2(scores * (SCALE * LOG2E)).astype(BF16)


def apply_one(rows, others, totals, target, source, weights):
    values = value_of(others, source, 0, weights.shape[0])
    total = jnp.dot(values, weights[...], preferred_element_type=F32)
    totals[target] += total[ONES:] / total[:1]


def score_two(rows, others, target, source, weights, block):
    score_one(others, rows, source, target, weights, block)


def apply_two(rows, others, totals, target, source, weights):
    values = value_of(others, source, 0, weights.shape[0])
    total = lax.dot_general(values, weights[...], NT, preferred_element_type=F32)
    totals[target] += total[ONES:] / total[:1]
    apply_one(others, rows, totals, source, target, weights)


def run_units(rows, others, totals, units, begin, count, even_weights, odd_weights, score, apply):
    block = even_weights.shape[0] // 2

    def scored(index, weights):
        score(rows, others, units[0, index], units[1, index], weights, block)

    def applied(index, weights):
        apply(rows, others, totals, units[0, index], units[1, index], weights)

    @pl.when(count > 0)
    def _():
        scored(begin, even_weights)

        def step(index, carry):
            now = begin + 2 * index
            scored(now + 1, odd_weights)
            applied(now, even_weights)
            scored(now + 2, even_weights)
            applied(now + 1, odd_weights)
            return carry

        lax.fori_loop(0, (count - 1) // 2, step, 0)
        last = begin + count - 1

        @pl.when(lax.rem(count, 2) == 0)
        def _():
            scored(last, odd_weights)
            applied(last - 1, even_weights)
            applied(last, odd_weights)

        @pl.when(lax.rem(count, 2) == 1)
        def _():
            applied(last, even_weights)


def shifted(rows, others, totals, target, source, keypoints):
    narrow = 2 * LANES
    keys = query_of(others, source, 0, keypoints)
    values = value_of(others, source, 0, keypoints)

    def step(index, carry):
        lower = pl.multiple_of(index * narrow, narrow)
        parts = [
            rows[target, pl.ds(pl.multiple_of(lower + offset, LANES), HEAD_DIM), :]
            for offset in range(0, narrow, LANES)
        ]
        query = jnp.concatenate(parts, 1)
        scores = lax.dot_general(keys, query, TN, preferred_element_type=F32) * SCALE
        weights = jnp.exp(scores - jnp.max(scores, axis=0, keepdims=True)).astype(BF16)
        total = jnp.dot(values, weights, preferred_element_type=F32)
        totals[target, :, pl.ds(lower, narrow)] += total[ONES:] / total[:1]
        return carry

    lax.fori_loop(0, keypoints // narrow, step, 0)


def start_copies(pieces, rows, info_v, sems):
    keypoints = rows.shape[1] - INFO
    copies = []
    position = 0
    for piece in pieces:
        if len(piece.shape) == 3:
            place = slice(position, position + piece.shape[0])
            position += piece.shape[0]
            listed = piece[:, keypoints : keypoints + 8]
        else:
            place = position
            position += 1
            listed = piece[keypoints : keypoints + 8]
        copies.append(pltpu.make_async_copy(piece, rows.at[place], sems.at[len(copies)]))
        copies[-1].start()
        info_v[place] = listed.astype(F32).astype(jnp.int32)
    return copies


def to_scalars(info_v, info, info_sem):
    copy = pltpu.make_async_copy(info_v, info, info_sem)
    copy.start()
    copy.wait()


def column_of(image, members):
    if members & (members - 1) == 0:
        return lax.shift_right_logical(image, members.bit_length() - 1)
    return lax.div(image, members)


def place_of(image, members, member):
    if members & (members - 1) == 0:
        return jnp.bitwise_and(image - member, members - 1)
    return lax.rem(lax.rem(image, members) - member + members, members)


def shared_kernel(members, pieces_count, *refs):
    count = 2 * members
    pieces, (own_ref, other_ref, *refs) = refs[:pieces_count], refs[pieces_count:]
    rows, totals, even_weights, odd_weights, *refs = refs
    info_v, info, units, info_sem, sems = refs
    keypoints = totals.shape[2]
    column = lax.axis_index("img")
    member = lax.axis_index("grp")

    copies = start_copies(pieces, rows, info_v, sems)
    to_scalars(info_v, info, info_sem)
    totals[...] = jnp.zeros_like(totals)
    side = lax.rem(column, 2)

    def slot(index, found):
        right = index >= members
        base = jnp.where(right == (side == 1), 0, members)
        owner = base + index - jnp.where(right, members, 0)
        listed = column - side + right.astype(jnp.int32)

        def position(step, found):
            first = info[owner, 0, 2 + 2 * step]
            second = info[owner, 0, 3 + 2 * step]
            inside = column_of(second, members) == listed
            shared = jnp.logical_or(jnp.logical_not(right), inside)

            @pl.when(shared)
            def _():
                units[0, found] = base + place_of(first, members, member)
                units[1, found] = jnp.where(inside, base, members - base) + place_of(
                    second, members, member
                )

            return found + shared.astype(jnp.int32)

        return lax.fori_loop(0, info[owner, 0, 0], position, found)

    found = lax.fori_loop(0, count, slot, jnp.int32(0))
    row = lax.rem(column - side, ROW)
    shift = (row == ROW - 2).astype(jnp.int32) - (row == 0).astype(jnp.int32)
    half = jnp.clip(found // 2 + 2 * shift, 0, found)
    begin = jnp.where(side == 0, 0, half)
    end = jnp.where(side == 0, half, found)
    largest = info[0, 0, 1]
    for position in range(1, count):
        largest = jnp.maximum(largest, info[position, 0, 1])
    safe = largest * largest <= int(SAFE_SCORE / SCALE)
    for copy in copies:
        copy.wait()

    @pl.when(safe)
    def _():
        run_units(
            rows, rows, totals, units, begin, end - begin, even_weights, odd_weights,
            score_two, apply_two,
        )

    @pl.when(jnp.logical_not(safe))
    def _():
        def visit(index, carry):
            target, source = units[0, index], units[1, index]
            shifted(rows, rows, totals, target, source, keypoints)
            shifted(rows, rows, totals, source, target, keypoints)
            return carry

        lax.fori_loop(begin, end, visit, 0)

    own_ref[...] = totals[:members]
    other_ref[...] = totals[members:]


def pair_scratch(count, full):
    keypoints = full - INFO
    return [
        pltpu.VMEM((keypoints, keypoints), BF16),
        pltpu.VMEM((keypoints, keypoints), BF16),
        pltpu.VMEM((count, 8, LANES), jnp.int32),
        pltpu.SMEM((count, 8, LANES), jnp.int32),
        pltpu.SMEM((2, 8 * LANES), jnp.int32),
        pltpu.SemaphoreType.DMA,
    ]


def shared(members, pieces):
    full = pieces[0].shape[1]
    keypoints = full - INFO
    count = 2 * members
    vmem = pl.BlockSpec(memory_space=pltpu.VMEM)
    whole = jax.ShapeDtypeStruct((members, HEAD_DIM, keypoints), F32)
    return pl.pallas_call(
        functools.partial(shared_kernel, members, len(pieces)),
        out_shape=[whole, whole],
        in_specs=[vmem] * len(pieces),
        out_specs=[vmem, vmem],
        scratch_shapes=[
            pltpu.VMEM((count, full, LANES), BF16),
            pltpu.VMEM((count, HEAD_DIM, keypoints), F32),
            *pair_scratch(count, full),
            pltpu.SemaphoreType.DMA((len(pieces),)),
        ],
        compiler_params=pltpu.CompilerParams(vmem_limit_bytes=VMEM_LIMIT),
        cost_estimate=SHORT,
        name="shared",
    )(*pieces)


def far_kernel(members, own_ref, far_ref, start_ref, out_ref, *refs):
    even_weights, odd_weights, info_v, info, units, info_sem = refs
    keypoints = out_ref.shape[2]
    column = lax.axis_index("img")
    member = lax.axis_index("grp")
    info_v[:members] = own_ref[:, keypoints : keypoints + 8].astype(F32).astype(jnp.int32)
    info_v[members:] = far_ref[:, keypoints : keypoints + 8].astype(F32).astype(jnp.int32)
    to_scalars(info_v, info, info_sem)
    out_ref[...] = start_ref[...]
    ahead = lax.rem(column, 2) == 1
    listed = jnp.where(ahead, 0, members)

    def slot(index, found):
        owner = listed + index

        def position(step, found):
            first = info[owner, 0, 2 + 2 * step]
            second = info[owner, 0, 3 + 2 * step]
            wanted = (column_of(second, members) == column) != ahead

            @pl.when(wanted)
            def _():
                left = place_of(first, members, member)
                right = place_of(second, members, member)
                units[0, found] = jnp.where(ahead, left, right)
                units[1, found] = jnp.where(ahead, right, left)

            return found + wanted.astype(jnp.int32)

        return lax.fori_loop(0, info[owner, 0, 0], position, found)

    found = lax.fori_loop(0, members, slot, jnp.int32(0))
    left, right = info[0, 0, 1], info[members, 0, 1]
    for position in range(1, members):
        left = jnp.maximum(left, info[position, 0, 1])
        right = jnp.maximum(right, info[members + position, 0, 1])
    safe = jnp.logical_and(
        jnp.maximum(left, right) < int(NORM_CAP), left * right <= int(SAFE_SCORE / SCALE)
    )

    @pl.when(safe)
    def _():
        run_units(
            own_ref, far_ref, out_ref, units, jnp.int32(0), found, even_weights, odd_weights,
            score_one, apply_one,
        )

    @pl.when(jnp.logical_not(safe))
    def _():
        def visit(index, carry):
            shifted(own_ref, far_ref, out_ref, units[0, index], units[1, index], keypoints)
            return carry

        lax.fori_loop(0, found, visit, 0)


def far_pairs(members, own, far, totals):
    full = own.shape[1]
    vmem = pl.BlockSpec(memory_space=pltpu.VMEM)
    return pl.pallas_call(
        functools.partial(far_kernel, members),
        out_shape=jax.ShapeDtypeStruct(totals.shape, F32),
        in_specs=[vmem] * 3,
        out_specs=vmem,
        scratch_shapes=pair_scratch(2 * members, full),
        compiler_params=pltpu.CompilerParams(vmem_limit_bytes=VMEM_LIMIT),
        cost_estimate=LONG,
        name="far_pairs",
    )(own, far, totals)


def merge_kernel(totals_ref, partial_ref, *outs):
    for slot, out_ref in enumerate(outs):
        out_ref[...] = (totals_ref[slot] + partial_ref[slot]).astype(BF16)


def merge(members, totals, partial):
    vmem = pl.BlockSpec(memory_space=pltpu.VMEM)
    message = jax.ShapeDtypeStruct(totals.shape[1:], BF16)
    return pl.pallas_call(
        merge_kernel,
        out_shape=[message] * members,
        in_specs=[vmem, vmem],
        out_specs=[vmem] * members,
        compiler_params=pltpu.CompilerParams(vmem_limit_bytes=VMEM_LIMIT),
        name="merge",
    )(totals, partial)


def update_kernel(members, desc_ref, w_ref, *refs):
    pieces = refs[:members]
    out_hbm, held, sems = refs[members:]
    member = lax.axis_index("grp")
    weights = []
    for distance in range(members):
        head = lax.rem(member - distance + members, members)
        weights.append(w_ref[pl.ds(pl.multiple_of(head * HEAD_DIM, HEAD_DIM), HEAD_DIM), :])
    weights = jnp.concatenate(weights, 0)
    block = held.shape[0] // PARTS
    copies = []
    for part in range(PARTS):
        place = slice(part * block, (part + 1) * block)
        message = jnp.concatenate([piece[:, place] for piece in pieces], 0)
        update = lax.dot_general(message, weights, TN, preferred_element_type=F32)
        held[place, :] = (desc_ref[0, place, :].astype(F32) + update).astype(BF16)
        copies.append(
            pltpu.make_async_copy(held.at[place], out_hbm.at[0, place], sems.at[part])
        )
        copies[-1].start()
    for copy in copies:
        copy.wait()


def update(members, desc, w_out, pieces):
    vmem = pl.BlockSpec(memory_space=pltpu.VMEM)
    return pl.pallas_call(
        functools.partial(update_kernel, members),
        out_shape=jax.ShapeDtypeStruct(desc.shape, BF16),
        in_specs=[vmem] * (2 + members),
        out_specs=pl.BlockSpec(memory_space=pltpu.HBM),
        scratch_shapes=[
            pltpu.VMEM(desc.shape[1:], BF16),
            pltpu.SemaphoreType.DMA((PARTS,)),
        ],
        compiler_params=pltpu.CompilerParams(vmem_limit_bytes=VMEM_LIMIT),
        name="update",
    )(desc, w_out, *pieces)


def on_device(desc, w_proj, w_out, pair_list, pair_count):
    columns = lax.axis_size("img")
    members = lax.axis_size("grp")

    def from_ahead(block, distance):
        route = [((i + distance) % members, i) for i in range(members)]
        return lax.ppermute(block, "grp", route)

    def swap(block, offset):
        pairs = []
        for i in range(offset, columns + offset, 2):
            low, high = i % columns, (i + 1) % columns
            pairs += [(low, high), (high, low)]
        return lax.ppermute(block, "img", pairs)

    sent = project(members, pair_list, pair_count, desc, w_proj)
    own = [sent[0]] + [from_ahead(sent[k], k) for k in range(1, members)]
    near = [swap(block, 0) for block in own]
    gathered, *near = lax.optimization_barrier([jnp.stack(own)] + near)
    far = swap(gathered, 1)
    totals, other = shared(members, [gathered] + near)
    partial = swap(other, 0)
    totals = far_pairs(members, gathered, far, totals)
    messages = merge(members, totals, partial)
    back = [messages[0]]
    for distance in range(1, members):
        back.append(from_ahead(messages[distance], members - distance))
    return update(members, desc, w_out, back)


def solution(mesh):
    return jax.shard_map(
        on_device,
        mesh=mesh,
        in_specs=(
            P(("img", "grp"), None, None),
            P(),
            P(),
            P(("img", "grp"), None),
            P(("img", "grp")),
        ),
        out_specs=P(("img", "grp"), None, None),
        check_vma=False,
    )
```

```python
import functools
import math

import jax
import jax.numpy as jnp
from jax import lax
from jax.experimental import pallas as pl
from jax.experimental.pallas import tpu as pltpu
from jax.sharding import PartitionSpec as P

D = 256
HEADS = 4
HEAD_DIM = 64
LANES = 128
ONES = 16
INFO = 16
PARTS = 4
SCALE = HEAD_DIM ** -0.5
LOG2E = math.log2(math.e)
SAFE_SCORE = 64.0
NORM_CAP = 250.0
BF16 = jnp.bfloat16
F32 = jnp.float32
NT = (((1,), (1,)), ((), ()))
TN = (((0,), (0,)), ((), ()))
VMEM_LIMIT = 28 * 1024 * 1024
ROW = 16
SHORT = pl.CostEstimate(flops=10**4, bytes_accessed=10**4, transcendentals=0)
LONG = pl.CostEstimate(flops=10**10, bytes_accessed=10**7, transcendentals=0)


def project_kernel(members, count_ref, list_hbm, desc_hbm, w_hbm, *refs):
    outs = refs[:members]
    turned, list_ref, desc_ref, w_ref, sems = refs[members:]
    copies = [
        pltpu.make_async_copy(source, target, sems.at[k])
        for k, (source, target) in enumerate(
            ((w_hbm, w_ref), (desc_hbm, desc_ref), (list_hbm, list_ref))
        )
    ]
    for copy in copies:
        copy.start()
    keypoints = desc_ref.shape[1]
    cap = list_ref.shape[1]
    member = lax.axis_index("grp")
    copies[0].wait()
    turned[...] = w_ref[...].T
    copies[2].wait()
    lane = lax.broadcasted_iota(jnp.int32, (INFO, LANES), 1)
    common = jnp.where(lane == 0, count_ref[0], 0)
    for slot in range(cap):
        first = jnp.broadcast_to(list_ref[0:1, slot : slot + 1], lane.shape)
        second = jnp.broadcast_to(list_ref[1:2, slot : slot + 1], lane.shape)
        common = jnp.where(lane == 2 + 2 * slot, first, common)
        common = jnp.where(lane == 3 + 2 * slot, second, common)
    common = common.astype(F32)
    copies[1].wait()
    desc = desc_ref[0]
    for distance in range(members):
        head = lax.rem(member - distance + members, members)
        lower = pl.multiple_of(head * HEAD_DIM, HEAD_DIM)
        weights = jnp.concatenate(
            [turned[pl.ds(lower, HEAD_DIM), :], turned[pl.ds(D + lower, HEAD_DIM), :]], 0
        )
        both = lax.dot_general(weights, desc, NT, preferred_element_type=F32).astype(BF16)
        for block in range(keypoints // LANES):
            outs[distance][block * LANES : (block + 1) * LANES, :] = both[
                :, block * LANES : (block + 1) * LANES
            ]
        query = both[:HEAD_DIM].astype(F32)
        squares = jnp.sum(query * query, axis=0, keepdims=True)
        norm = jnp.sqrt(jnp.max(squares, axis=1, keepdims=True)) * 1.001
        norm = jnp.ceil(jnp.minimum(norm, NORM_CAP))
        info = jnp.where(lane == 1, jnp.broadcast_to(norm, lane.shape), common)
        outs[distance][keypoints:, :] = info.astype(BF16)


def project(members, pair_list, pair_count, desc, w_proj):
    keypoints = desc.shape[1]
    hbm = pl.BlockSpec(memory_space=pltpu.HBM)
    out = jax.ShapeDtypeStruct((keypoints + INFO, LANES), BF16)
    listed = pair_list.T
    return pl.pallas_call(
        functools.partial(project_kernel, members),
        out_shape=[out] * members,
        in_specs=[pl.BlockSpec(memory_space=pltpu.SMEM), hbm, hbm, hbm],
        out_specs=[pl.BlockSpec(memory_space=pltpu.VMEM)] * members,
        scratch_shapes=[
            pltpu.VMEM((2 * D, D), BF16),
            pltpu.VMEM(listed.shape, jnp.int32),
            pltpu.VMEM(desc.shape, BF16),
            pltpu.VMEM(w_proj.shape, BF16),
            pltpu.SemaphoreType.DMA((3,)),
        ],
        compiler_params=pltpu.CompilerParams(vmem_limit_bytes=VMEM_LIMIT),
        name="project",
    )(pair_count, *[pltpu.with_memory_space_constraint(x, pltpu.HBM) for x in (listed, desc, w_proj)])


def query_of(rows, image, lower, size):
    parts = [
        rows[image, block : block + HEAD_DIM, :] for block in range(lower, lower + size, LANES)
    ]
    return jnp.concatenate(parts, 1)


def value_of(rows, image, lower, size):
    parts = [
        rows[image, block + HEAD_DIM : block + LANES, :]
        for block in range(lower, lower + size, LANES)
    ]
    return jnp.concatenate([jnp.ones((ONES, size), BF16), jnp.concatenate(parts, 1)], 0)


def score_one(rows, others, target, source, weights, block):
    keypoints = weights.shape[0]
    query = query_of(rows, target, 0, keypoints)
    for lower in range(0, keypoints, block):
        keys = query_of(others, source, lower, block)
        scores = lax.dot_general(keys, query, TN, preferred_element_type=F32)
        weights[lower : lower + block, :] = jnp.exp2(scores * (SCALE * LOG2E)).astype(BF16)


def apply_one(rows, others, totals, target, source, weights):
    values = value_of(others, source, 0, weights.shape[0])
    total = jnp.dot(values, weights[...], preferred_element_type=F32)
    totals[target] += total[ONES:] / total[:1]


def score_two(rows, others, target, source, weights, block):
    score_one(others, rows, source, target, weights, block)


def apply_two(rows, others, totals, target, source, weights):
    values = value_of(others, source, 0, weights.shape[0])
    total = lax.dot_general(values, weights[...], NT, preferred_element_type=F32)
    totals[target] += total[ONES:] / total[:1]
    apply_one(others, rows, totals, source, target, weights)


def run_units(rows, others, totals, units, begin, count, even_weights, odd_weights, score, apply):
    block = even_weights.shape[0] // 2

    def scored(index, weights):
        score(rows, others, units[0, index], units[1, index], weights, block)

    def applied(index, weights):
        apply(rows, others, totals, units[0, index], units[1, index], weights)

    @pl.when(count > 0)
    def _():
        scored(begin, even_weights)

        def step(index, carry):
            now = begin + 2 * index
            scored(now + 1, odd_weights)
            applied(now, even_weights)
            scored(now + 2, even_weights)
            applied(now + 1, odd_weights)
            return carry

        lax.fori_loop(0, (count - 1) // 2, step, 0)
        last = begin + count - 1

        @pl.when(lax.rem(count, 2) == 0)
        def _():
            scored(last, odd_weights)
            applied(last - 1, even_weights)
            applied(last, odd_weights)

        @pl.when(lax.rem(count, 2) == 1)
        def _():
            applied(last, even_weights)


def shifted(rows, others, totals, target, source, keypoints):
    narrow = 2 * LANES
    keys = query_of(others, source, 0, keypoints)
    values = value_of(others, source, 0, keypoints)

    def step(index, carry):
        lower = pl.multiple_of(index * narrow, narrow)
        parts = [
            rows[target, pl.ds(pl.multiple_of(lower + offset, LANES), HEAD_DIM), :]
            for offset in range(0, narrow, LANES)
        ]
        query = jnp.concatenate(parts, 1)
        scores = lax.dot_general(keys, query, TN, preferred_element_type=F32) * SCALE
        weights = jnp.exp(scores - jnp.max(scores, axis=0, keepdims=True)).astype(BF16)
        total = jnp.dot(values, weights, preferred_element_type=F32)
        totals[target, :, pl.ds(lower, narrow)] += total[ONES:] / total[:1]
        return carry

    lax.fori_loop(0, keypoints // narrow, step, 0)


def start_copies(pieces, rows, info_v, sems):
    keypoints = rows.shape[1] - INFO
    copies = []
    position = 0
    for piece in pieces:
        if len(piece.shape) == 3:
            place = slice(position, position + piece.shape[0])
            position += piece.shape[0]
            listed = piece[:, keypoints : keypoints + 8]
        else:
            place = position
            position += 1
            listed = piece[keypoints : keypoints + 8]
        copies.append(pltpu.make_async_copy(piece, rows.at[place], sems.at[len(copies)]))
        copies[-1].start()
        info_v[place] = listed.astype(F32).astype(jnp.int32)
    return copies


def to_scalars(info_v, info, info_sem):
    copy = pltpu.make_async_copy(info_v, info, info_sem)
    copy.start()
    copy.wait()


def column_of(image, members):
    if members & (members - 1) == 0:
        return lax.shift_right_logical(image, members.bit_length() - 1)
    return lax.div(image, members)


def place_of(image, members, member):
    if members & (members - 1) == 0:
        return jnp.bitwise_and(image - member, members - 1)
    return lax.rem(lax.rem(image, members) - member + members, members)


def shared_kernel(members, pieces_count, *refs):
    count = 2 * members
    pieces, (own_ref, other_ref, *refs) = refs[:pieces_count], refs[pieces_count:]
    rows, totals, even_weights, odd_weights, *refs = refs
    info_v, info, units, info_sem, sems = refs
    keypoints = totals.shape[2]
    column = lax.axis_index("img")
    member = lax.axis_index("grp")

    copies = start_copies(pieces, rows, info_v, sems)
    to_scalars(info_v, info, info_sem)
    totals[...] = jnp.zeros_like(totals)
    side = lax.rem(column, 2)

    def slot(index, found):
        right = index >= members
        base = jnp.where(right == (side == 1), 0, members)
        owner = base + index - jnp.where(right, members, 0)
        listed = column - side + right.astype(jnp.int32)

        def position(step, found):
            first = info[owner, 0, 2 + 2 * step]
            second = info[owner, 0, 3 + 2 * step]
            inside = column_of(second, members) == listed
            shared = jnp.logical_or(jnp.logical_not(right), inside)

            @pl.when(shared)
            def _():
                units[0, found] = base + place_of(first, members, member)
                units[1, found] = jnp.where(inside, base, members - base) + place_of(
                    second, members, member
                )

            return found + shared.astype(jnp.int32)

        return lax.fori_loop(0, info[owner, 0, 0], position, found)

    found = lax.fori_loop(0, count, slot, jnp.int32(0))
    row = lax.rem(column - side, ROW)
    extra = jnp.where(row == ROW - 2, 4, jnp.where(row == 0, -3, 0))
    half = jnp.clip(found + extra, 0, 2 * found) // 2
    begin = jnp.where(side == 0, 0, half)
    end = jnp.where(side == 0, half, found)
    largest = info[0, 0, 1]
    for position in range(1, count):
        largest = jnp.maximum(largest, info[position, 0, 1])
    safe = largest * largest <= int(SAFE_SCORE / SCALE)
    for copy in copies:
        copy.wait()

    @pl.when(safe)
    def _():
        run_units(
            rows, rows, totals, units, begin, end - begin, even_weights, odd_weights,
            score_two, apply_two,
        )

    @pl.when(jnp.logical_not(safe))
    def _():
        def visit(index, carry):
            target, source = units[0, index], units[1, index]
            shifted(rows, rows, totals, target, source, keypoints)
            shifted(rows, rows, totals, source, target, keypoints)
            return carry

        lax.fori_loop(begin, end, visit, 0)

    own_ref[...] = totals[:members]
    other_ref[...] = totals[members:]


def pair_scratch(count, full):
    keypoints = full - INFO
    return [
        pltpu.VMEM((keypoints, keypoints), BF16),
        pltpu.VMEM((keypoints, keypoints), BF16),
        pltpu.VMEM((count, 8, LANES), jnp.int32),
        pltpu.SMEM((count, 8, LANES), jnp.int32),
        pltpu.SMEM((2, 8 * LANES), jnp.int32),
        pltpu.SemaphoreType.DMA,
    ]


def shared(members, pieces):
    full = pieces[0].shape[1]
    keypoints = full - INFO
    count = 2 * members
    vmem = pl.BlockSpec(memory_space=pltpu.VMEM)
    whole = jax.ShapeDtypeStruct((members, HEAD_DIM, keypoints), F32)
    return pl.pallas_call(
        functools.partial(shared_kernel, members, len(pieces)),
        out_shape=[whole, whole],
        in_specs=[vmem] * len(pieces),
        out_specs=[vmem, vmem],
        scratch_shapes=[
            pltpu.VMEM((count, full, LANES), BF16),
            pltpu.VMEM((count, HEAD_DIM, keypoints), F32),
            *pair_scratch(count, full),
            pltpu.SemaphoreType.DMA((len(pieces),)),
        ],
        compiler_params=pltpu.CompilerParams(vmem_limit_bytes=VMEM_LIMIT),
        cost_estimate=SHORT,
        name="shared",
    )(*pieces)


def far_kernel(members, own_ref, far_ref, start_ref, out_ref, *refs):
    even_weights, odd_weights, info_v, info, units, info_sem = refs
    keypoints = out_ref.shape[2]
    column = lax.axis_index("img")
    member = lax.axis_index("grp")
    info_v[:members] = own_ref[:, keypoints : keypoints + 8].astype(F32).astype(jnp.int32)
    info_v[members:] = far_ref[:, keypoints : keypoints + 8].astype(F32).astype(jnp.int32)
    to_scalars(info_v, info, info_sem)
    out_ref[...] = start_ref[...]
    ahead = lax.rem(column, 2) == 1
    listed = jnp.where(ahead, 0, members)

    def slot(index, found):
        owner = listed + index

        def position(step, found):
            first = info[owner, 0, 2 + 2 * step]
            second = info[owner, 0, 3 + 2 * step]
            wanted = (column_of(second, members) == column) != ahead

            @pl.when(wanted)
            def _():
                left = place_of(first, members, member)
                right = place_of(second, members, member)
                units[0, found] = jnp.where(ahead, left, right)
                units[1, found] = jnp.where(ahead, right, left)

            return found + wanted.astype(jnp.int32)

        return lax.fori_loop(0, info[owner, 0, 0], position, found)

    found = lax.fori_loop(0, members, slot, jnp.int32(0))
    left, right = info[0, 0, 1], info[members, 0, 1]
    for position in range(1, members):
        left = jnp.maximum(left, info[position, 0, 1])
        right = jnp.maximum(right, info[members + position, 0, 1])
    safe = jnp.logical_and(
        jnp.maximum(left, right) < int(NORM_CAP), left * right <= int(SAFE_SCORE / SCALE)
    )

    @pl.when(safe)
    def _():
        run_units(
            own_ref, far_ref, out_ref, units, jnp.int32(0), found, even_weights, odd_weights,
            score_one, apply_one,
        )

    @pl.when(jnp.logical_not(safe))
    def _():
        def visit(index, carry):
            shifted(own_ref, far_ref, out_ref, units[0, index], units[1, index], keypoints)
            return carry

        lax.fori_loop(0, found, visit, 0)


def far_pairs(members, own, far, totals):
    full = own.shape[1]
    vmem = pl.BlockSpec(memory_space=pltpu.VMEM)
    return pl.pallas_call(
        functools.partial(far_kernel, members),
        out_shape=jax.ShapeDtypeStruct(totals.shape, F32),
        in_specs=[vmem] * 3,
        out_specs=vmem,
        scratch_shapes=pair_scratch(2 * members, full),
        compiler_params=pltpu.CompilerParams(vmem_limit_bytes=VMEM_LIMIT),
        cost_estimate=LONG,
        name="far_pairs",
    )(own, far, totals)


def merge_kernel(totals_ref, partial_ref, *outs):
    for slot, out_ref in enumerate(outs):
        out_ref[...] = (totals_ref[slot] + partial_ref[slot]).astype(BF16)


def merge(members, totals, partial):
    vmem = pl.BlockSpec(memory_space=pltpu.VMEM)
    message = jax.ShapeDtypeStruct(totals.shape[1:], BF16)
    return pl.pallas_call(
        merge_kernel,
        out_shape=[message] * members,
        in_specs=[vmem, vmem],
        out_specs=[vmem] * members,
        compiler_params=pltpu.CompilerParams(vmem_limit_bytes=VMEM_LIMIT),
        name="merge",
    )(totals, partial)


def update_kernel(members, desc_ref, w_ref, *refs):
    pieces = refs[:members]
    out_hbm, held, sems = refs[members:]
    member = lax.axis_index("grp")
    weights = []
    for distance in range(members):
        head = lax.rem(member - distance + members, members)
        weights.append(w_ref[pl.ds(pl.multiple_of(head * HEAD_DIM, HEAD_DIM), HEAD_DIM), :])
    weights = jnp.concatenate(weights, 0)
    block = held.shape[0] // PARTS
    copies = []
    for part in range(PARTS):
        place = slice(part * block, (part + 1) * block)
        message = jnp.concatenate([piece[:, place] for piece in pieces], 0)
        update = lax.dot_general(message, weights, TN, preferred_element_type=F32)
        held[place, :] = (desc_ref[0, place, :].astype(F32) + update).astype(BF16)
        copies.append(
            pltpu.make_async_copy(held.at[place], out_hbm.at[0, place], sems.at[part])
        )
        copies[-1].start()
    for copy in copies:
        copy.wait()


def update(members, desc, w_out, pieces):
    vmem = pl.BlockSpec(memory_space=pltpu.VMEM)
    return pl.pallas_call(
        functools.partial(update_kernel, members),
        out_shape=jax.ShapeDtypeStruct(desc.shape, BF16),
        in_specs=[vmem] * (2 + members),
        out_specs=pl.BlockSpec(memory_space=pltpu.HBM),
        scratch_shapes=[
            pltpu.VMEM(desc.shape[1:], BF16),
            pltpu.SemaphoreType.DMA((PARTS,)),
        ],
        compiler_params=pltpu.CompilerParams(vmem_limit_bytes=VMEM_LIMIT),
        name="update",
    )(desc, w_out, *pieces)


def on_device(desc, w_proj, w_out, pair_list, pair_count):
    columns = lax.axis_size("img")
    members = lax.axis_size("grp")

    def from_ahead(block, distance):
        route = [((i + distance) % members, i) for i in range(members)]
        return lax.ppermute(block, "grp", route)

    def swap(block, offset):
        pairs = []
        for i in range(offset, columns + offset, 2):
            low, high = i % columns, (i + 1) % columns
            pairs += [(low, high), (high, low)]
        return lax.ppermute(block, "img", pairs)

    sent = project(members, pair_list, pair_count, desc, w_proj)
    own = [sent[0]] + [from_ahead(sent[k], k) for k in range(1, members)]
    near = [swap(block, 0) for block in own]
    gathered, *near = lax.optimization_barrier([jnp.stack(own)] + near)
    far = swap(gathered, 1)
    totals, other = shared(members, [gathered] + near)
    partial = swap(other, 0)
    totals = far_pairs(members, gathered, far, totals)
    messages = merge(members, totals, partial)
    back = [messages[0]]
    for distance in range(1, members):
        back.append(from_ahead(messages[distance], members - distance))
    return update(members, desc, w_out, back)


def solution(mesh):
    return jax.shard_map(
        on_device,
        mesh=mesh,
        in_specs=(
            P(("img", "grp"), None, None),
            P(),
            P(),
            P(("img", "grp"), None),
            P(("img", "grp")),
        ),
        out_specs=P(("img", "grp"), None, None),
        check_vma=False,
    )
```
